32 devices in a mesh: space: 8 (over z, y), ens: 4 (over x, core).
Axes of the slice: x: 2, y: 2, z: 4, core: 2. Of those that a mesh axis runs over, the one named last changes fastest.
Arguments:
- latent: bfloat16 [4, 6144, 1024], P('ens', 'space'), may hold values from -6 to 6
- head_weight: bfloat16 [1024, 100], replicated, may hold values from -0.1875 to 0.1875
- head_bias: float32 [100], replicated, may hold values from -3 to 3
- targets: bfloat16 [100, 6144], P(None, 'space'), may hold values from -6 to 6
- var_weight: float32 [100], replicated, may hold values from 0.25 to 2.5
- tile_fill: int32 [48], P('space'), may hold values from 1 to 128, 4608 in all
Outputs:
- grad_latent: bfloat16 [4, 6144, 1024], P('ens', 'space')
- grad_weight: float32 [1024, 100], replicated
- grad_bias: float32 [100], replicated
The draws below stay inside these ranges and needn't reach their ends.
Inputs may be any that keep to these rules, and one draw needn't show every extreme that they name: tile_fill counts the live points of each tile.
All inputs are finite; a program needn't handle non-finite values. No bound on the sum of `tile_fill` on one device may be relied on, other than what follows from the above.
Results may differ from the reference program's by a relative error of at most 0.0099.
Values may be sent and summed in bfloat16 or wider, within the bound.
No kernel may reach another device: no remote copies, remote signals or barrier semaphores. Data moves between devices by JAX's collectives and lax.ppermute only.
A program may use at most 64 MiB of HBM per device.

```python
import math
import jax
import jax.numpy as jnp
import numpy as np
from jax import lax

D = 1024
V = 100
TILE_PTS = 128
MEMBERS = 4
NTILES = 48
POINTS = 6144


def level_of(key, shape, cuts, low, top_value):
    def one(axis_at, blocks):
        steps = jax.random.uniform(jax.random.fold_in(jax.random.fold_in(key, 6), axis_at), (blocks,), jnp.float32, low / len(cuts), top_value / len(cuts))
        return jnp.repeat(jnp.exp(steps), shape[axis_at] // blocks).reshape((-1,) + (1,) * (len(shape) - axis_at - 1))

    factor_of = one(*cuts[0])
    for cut in cuts[1:]:
        factor_of = factor_of * one(*cut)
    return factor_of


def length_profile(number_of, total, limit, lean):
    loads = [(1 << 20) // math.isqrt(grade ** lean) + 1 for grade in range(2, number_of + 1)]
    rest, given = total - limit - (number_of - 1), [1] * (number_of - 1)
    while rest > 0:
        movable = [i for i in range(number_of - 1) if given[i] < limit]
        mass, remaining = sum([loads[i] for i in movable]), rest
        for i in movable:
            more = min(limit - given[i], max(1, remaining * loads[i] // mass), rest)
            given[i] = given[i] + more
            rest = rest - more
    return np.array([limit] + given)


def ragged(key, number_of, total, reach, skew):
    if number_of == 2:
        one = jax.random.randint(key, (), max(1, total - reach), min(reach, total - 1) + 1)
        return jnp.stack([one, total - one])
    tallies = jnp.asarray(length_profile(number_of, total, reach, skew), jnp.int32)
    couples = (number_of - 1) // 2
    donor, receiver = tallies[1:1 + 2 * couples:2], tallies[2:2 + 2 * couples:2]
    slack = jnp.minimum(donor - 1, reach - receiver)
    moved = jax.random.randint(jax.random.fold_in(key, 1), (couples,), 0, 1 << 20) % (slack + 1)
    tallies = tallies.at[1:1 + 2 * couples:2].set(donor - moved).at[2:2 + 2 * couples:2].set(receiver + moved)
    return tallies[jax.random.permutation(jax.random.fold_in(key, 2), number_of)]


def scatter_about(own_key, shape, spread, bound, cuts=(), kind=jnp.bfloat16):
    drawn = spread * jax.random.normal(own_key, shape, jnp.float32)
    if cuts:
        drawn = drawn * level_of(own_key, shape, cuts, -0.22, 0.18)
    return jnp.clip(drawn, -bound, bound).astype(kind)


def setup_inputs(seed: int = 0) -> dict:
    keys = jax.random.split(jax.random.key(seed), 7)
    return {
        "latent": scatter_about(keys[0], (MEMBERS, POINTS, D), 1.0, 6.0, ((0, 4), (1, 8))),
        "head_weight": scatter_about(keys[1], (D, V), D ** -0.5, 0.1875),
        "head_bias": scatter_about(keys[2], (V,), 0.5, 3.0, (), jnp.float32),
        "targets": scatter_about(keys[3], (V, POINTS), 1.0, 6.0, ((1, 8),)),
        "var_weight": jnp.clip(jnp.exp(jax.random.uniform(keys[4], (V,), jnp.float32, math.log(0.25), math.log(2.5))), 0.25, 2.5),
        "tile_fill": ragged(keys[5], NTILES, NTILES * TILE_PTS * 3 // 4, TILE_PTS, 2).astype(jnp.int32),
    }


SMOOTH = 0.05

def smooth_sign(value):
    return value / jnp.sqrt(value * value + SMOOTH * SMOOTH)

def reference(latent, head_weight, head_bias, targets, var_weight, tile_fill):
    members = latent.shape[0]
    points = latent.shape[1]

    def project(rows):
        return (jnp.dot(rows, head_weight, preferred_element_type=jnp.float32) + head_bias[None, :]).T.astype(jnp.bfloat16)
    preds = lax.map(project, latent)
    values = preds.astype(jnp.float32)

    def add_pair(carry, other):
        return (carry + smooth_sign(values - other[None]), None)
    pair, _ = lax.scan(add_pair, jnp.zeros(values.shape, jnp.float32), values)
    index = jnp.arange(points, dtype=jnp.int32)
    fill = jnp.repeat(tile_fill, TILE_PTS)
    live = index % TILE_PTS < fill
    latitude = jnp.pi * ((index.astype(jnp.float32) + 0.5) / points - 0.5)
    area = jnp.where(live, jnp.cos(latitude), 0.0).astype(jnp.float32)
    observed = targets.astype(jnp.float32)
    grad_pred = area[None, None, :] * var_weight[None, :, None] * (smooth_sign(values - observed[None]) - pair / (members - 1))
    grad_pred = grad_pred.astype(jnp.bfloat16)

    def back(rows):
        return jnp.dot(rows.T, head_weight.T, preferred_element_type=jnp.float32).astype(jnp.bfloat16)
    grad_latent = lax.map(back, grad_pred)

    def accumulate(carry, pieces):
        rows, grads = pieces
        return (carry + jnp.dot(rows.T, grads.T, preferred_element_type=jnp.float32), None)
    weight_sum, _ = lax.scan(accumulate, jnp.zeros(head_weight.shape, jnp.float32), (latent, grad_pred))
    scale = 1.0 / jnp.sqrt(jnp.float32(members) * jnp.float32(points))
    bias_sum = lax.optimization_barrier(jnp.sum(grad_pred.astype(jnp.float32), axis=(0, 2)))
    return (grad_latent, weight_sum * scale, bias_sum * scale)
```

```python
import jax
import jax.numpy as jnp
from jax import lax
from jax.sharding import PartitionSpec as P

TILE_PTS = 128
SMOOTH = 0.05
ALL = ("space", "ens")


def smooth_sign(value):
    return value / jnp.sqrt(value * value + SMOOTH * SMOOTH)


def is_pow2(n):
    return n > 0 and n & (n - 1) == 0


def swap(value, bits_of):
    count = lax.axis_size("space") * lax.axis_size("ens")
    return lax.ppermute(value, ALL, [(i, i ^ bits_of(i)) for i in range(count)])


def round_bf16(value):
    return lax.reduce_precision(value, exponent_bits=8, mantissa_bits=7)


def butterfly(block):
    ens = lax.axis_size("ens")
    count = lax.axis_size("space") * ens
    steps = []
    bit = 2
    while bit < count:
        steps.append(bit)
        bit *= 2
    for up, down in zip(steps, reversed(steps)):
        sent = round_bf16(block)
        got = swap(sent.astype(jnp.bfloat16), lambda i: down if i % 2 else up)
        block = sent + got.astype(jnp.float32)
    return block


def reduce_all(weight_sum, bias_sum):
    variables, channels = weight_sum.shape
    ens = lax.axis_size("ens")
    if not (is_pow2(ens) and is_pow2(lax.axis_size("space")) and ens > 1 and variables <= channels // 2):
        return lax.psum((weight_sum, bias_sum), ALL)
    half = channels // 2
    core = lax.axis_index("ens") % 2
    row = jnp.pad(bias_sum[None, :], ((0, 0), (0, half - variables)))
    mine = lax.dynamic_slice_in_dim(weight_sum, core * half, half, 1)
    other = lax.dynamic_slice_in_dim(weight_sum, (1 - core) * half, half, 1)
    mine = jnp.concatenate([mine, row], 0)
    other = jnp.concatenate([other, row], 0).astype(jnp.bfloat16)
    block = mine + swap(other, lambda i: 1).astype(jnp.float32)
    block = butterfly(block)
    there = swap(block, lambda i: 1)
    first = jnp.where(core == 0, block, there)
    second = jnp.where(core == 0, there, block)
    total = jnp.concatenate([first[:variables], second[:variables]], 1)
    return total, first[variables, :variables]


def other_members(preds):
    ens = lax.axis_size("ens")
    if preds.shape[0] == 1 and ens == 4:
        across = swap(preds, lambda i: 2)
        beside = swap(preds, lambda i: 1)
        return [beside, across, swap(across, lambda i: 1)]
    everyone = lax.all_gather(preds, "ens", axis=0, tiled=True)
    return [everyone[k : k + 1] for k in range(everyone.shape[0])]


def local(latent, head_weight, head_bias, targets, var_weight, tile_fill):
    mem_local = latent.shape[0]
    local_points = latent.shape[1]
    members = mem_local * lax.axis_size("ens")
    points = local_points * lax.axis_size("space")
    preds = jnp.einsum("mpd,dv->mvp", latent, head_weight, preferred_element_type=jnp.float32)
    preds = (preds + head_bias[None, :, None]).astype(jnp.bfloat16)
    values = preds.astype(jnp.float32)
    local_index = jnp.arange(local_points, dtype=jnp.int32)
    global_index = lax.axis_index("space") * local_points + local_index
    fill = jnp.repeat(tile_fill, TILE_PTS)
    live = local_index % TILE_PTS < fill
    latitude = jnp.pi * ((global_index.astype(jnp.float32) + 0.5) / points - 0.5)
    area = jnp.where(live, jnp.cos(latitude), 0.0)
    observed = targets.astype(jnp.float32)
    pair = jnp.zeros(values.shape, jnp.float32)
    for other in other_members(preds):
        pair = pair + smooth_sign(values - other.astype(jnp.float32))
    grad_pred = (
        area[None, None, :]
        * var_weight[None, :, None]
        * (smooth_sign(values - observed[None]) - pair / (members - 1))
    ).astype(jnp.bfloat16)
    grad_latent = jnp.einsum(
        "mvp,dv->mpd", grad_pred, head_weight, preferred_element_type=jnp.float32
    ).astype(jnp.bfloat16)
    scale = 1.0 / jnp.sqrt(jnp.float32(members) * jnp.float32(points))
    weight_sum = jnp.einsum("mpd,mvp->vd", latent, grad_pred, preferred_element_type=jnp.float32)
    bias_sum = jnp.sum(grad_pred.astype(jnp.float32), axis=(0, 2))
    weight_total, bias_total = reduce_all(weight_sum * scale, bias_sum * scale)
    return (grad_latent, weight_total.T, bias_total)


def solution(mesh):
    placed = (P("ens", "space", None), P(), P(), P(None, "space"), P(), P("space"))
    return jax.shard_map(
        local,
        mesh=mesh,
        in_specs=placed,
        out_specs=(P("ens", "space", None), P(), P()),
        check_vma=False,
    )
```

```python
import jax
import jax.numpy as jnp
from jax import lax
from jax.sharding import PartitionSpec as P

TILE_PTS = 128
SMOOTH = 0.05
ALL = ("space", "ens")


def smooth_sign(value):
    return value * lax.rsqrt(value * value + SMOOTH * SMOOTH)


def is_pow2(n):
    return n > 0 and n & (n - 1) == 0


def swap(value, bits_of):
    count = lax.axis_size("space") * lax.axis_size("ens")
    return lax.ppermute(value, ALL, [(i, i ^ bits_of(i)) for i in range(count)])


def round_bf16(value):
    return lax.reduce_precision(value, exponent_bits=8, mantissa_bits=7)


def butterfly(block, beside):
    ens = lax.axis_size("ens")
    count = lax.axis_size("space") * ens
    steps = []
    bit = 2
    while bit < count:
        steps.append(bit)
        bit *= 2
    for up, down in zip(steps, reversed(steps)):
        sent = round_bf16(block)
        got = swap(sent.astype(jnp.bfloat16), lambda i: down if i % 2 else up)
        if up == 4:
            got, beside = lax.optimization_barrier((got, beside))
        block = sent + got.astype(jnp.float32)
    return block, beside


def area_of(local_points, tile_fill):
    points = local_points * lax.axis_size("space")
    local_index = jnp.arange(local_points, dtype=jnp.int32)
    global_index = lax.axis_index("space") * local_points + local_index
    live = local_index % TILE_PTS < jnp.repeat(tile_fill, TILE_PTS)
    latitude = jnp.pi * ((global_index.astype(jnp.float32) + 0.5) / points - 0.5)
    return jnp.where(live, jnp.cos(latitude), 0.0)


def project(latent, head_weight, head_bias):
    preds = jnp.einsum("mpd,dv->mvp", latent, head_weight, preferred_element_type=jnp.float32)
    return (preds + head_bias[None, :, None]).astype(jnp.bfloat16)


def back(grad_pred, head_weight):
    return jnp.einsum(
        "mvp,dv->mpd", grad_pred, head_weight, preferred_element_type=jnp.float32
    ).astype(jnp.bfloat16)


def general(latent, head_weight, head_bias, targets, var_weight, tile_fill):
    members = latent.shape[0] * lax.axis_size("ens")
    points = latent.shape[1] * lax.axis_size("space")
    preds = project(latent, head_weight, head_bias)
    values = preds.astype(jnp.float32)
    everyone = lax.all_gather(preds, "ens", axis=0, tiled=True)

    def one_member(slot, total):
        other = lax.dynamic_index_in_dim(everyone, slot, 0, keepdims=True).astype(jnp.float32)
        return total + smooth_sign(values - other)

    pair = lax.fori_loop(0, members, one_member, jnp.zeros(values.shape, jnp.float32))
    weight = area_of(latent.shape[1], tile_fill)[None, :] * var_weight[:, None]
    sign = smooth_sign(values - targets.astype(jnp.float32)[None])
    grad_pred = (weight[None] * (sign - pair / (members - 1))).astype(jnp.bfloat16)
    grad_latent = back(grad_pred, head_weight)
    scale = 1.0 / jnp.sqrt(jnp.float32(members) * jnp.float32(points))
    weight_sum = jnp.einsum("mpd,mvp->dv", latent, grad_pred, preferred_element_type=jnp.float32)
    bias_sum = jnp.sum(grad_pred.astype(jnp.float32), axis=(0, 2))
    weight_total, bias_total = lax.psum((weight_sum * scale, bias_sum * scale), ALL)
    return grad_latent, weight_total, bias_total


def four_members(latent, head_weight, head_bias, targets, var_weight, tile_fill):
    points = latent.shape[1] * lax.axis_size("space")
    half = latent.shape[2] // 2
    core = lax.axis_index("ens") % 2
    kept = lax.dynamic_slice_in_dim(latent[0], core * half, half, 1)
    given = lax.dynamic_slice_in_dim(latent[0], (1 - core) * half, half, 1)
    taken = swap(given, lambda i: 1)
    preds = project(latent, head_weight, head_bias)
    across = swap(preds, lambda i: 2)
    beside = swap(preds, lambda i: 1)
    corner = swap(across, lambda i: 1)
    own, mate, far, corner, seen = (
        v.reshape(v.shape[-2:]).astype(jnp.float32) for v in (preds, beside, across, corner, targets)
    )
    weight = area_of(latent.shape[1], tile_fill)[None, :] * var_weight[:, None]
    inside = smooth_sign(own - mate)
    pair = inside + smooth_sign(own - far) + smooth_sign(own - corner)
    grad_own = (weight * (smooth_sign(own - seen) - pair / 3)).astype(jnp.bfloat16)
    pair = smooth_sign(mate - far) + smooth_sign(mate - corner) - inside
    grad_mate = (weight * (smooth_sign(mate - seen) - pair / 3)).astype(jnp.bfloat16)
    scale = 1.0 / jnp.sqrt(4 * jnp.float32(points))
    block = jnp.dot(grad_own, kept, preferred_element_type=jnp.float32)
    block += jnp.dot(grad_mate, taken, preferred_element_type=jnp.float32)
    bias = jnp.sum(grad_own.astype(jnp.float32) + grad_mate.astype(jnp.float32), axis=1)
    variables = bias.shape[0]
    row = jnp.pad(bias[None, :], ((0, 0), (0, half - variables)))
    block = jnp.concatenate([block, row], 0) * scale

    grad_latent = back(grad_own[None], head_weight)
    block, grad_latent = butterfly(block, grad_latent)
    there = swap(block, lambda i: 1)
    first = jnp.where(core == 0, block, there)
    second = jnp.where(core == 0, there, block)
    total = jnp.concatenate([first[:variables], second[:variables]], 1)
    return grad_latent, total.T, first[variables, :variables]


def local(latent, head_weight, head_bias, targets, var_weight, tile_fill):
    space, ens = lax.axis_size("space"), lax.axis_size("ens")
    members, _, channels = latent.shape
    fits = members == 1 and ens == 4 and is_pow2(space)
    fits = fits and channels % 256 == 0 and targets.shape[0] <= channels // 2
    plan = four_members if fits else general
    return plan(latent, head_weight, head_bias, targets, var_weight, tile_fill)


def solution(mesh):
    placed = (P("ens", "space", None), P(), P(), P(None, "space"), P(), P("space"))
    return jax.shard_map(
        local,
        mesh=mesh,
        in_specs=placed,
        out_specs=(P("ens", "space", None), P(), P()),
        check_vma=False,
    )
```

```python
import jax
import jax.numpy as jnp
from jax import lax
from jax.sharding import PartitionSpec as P

TILE_PTS = 128
SMOOTH = 0.05
ALL = ("space", "ens")


def smooth_sign(value):
    return value * lax.rsqrt(value * value + SMOOTH * SMOOTH)


def is_pow2(n):
    return n > 0 and n & (n - 1) == 0


def swap(value, bits_of):
    count = lax.axis_size("space") * lax.axis_size("ens")
    return lax.ppermute(value, ALL, [(i, i ^ bits_of(i)) for i in range(count)])


def round_bf16(value):
    return lax.reduce_precision(value, exponent_bits=8, mantissa_bits=7)


def hops():
    count = lax.axis_size("space") * lax.axis_size("ens")
    bits = [1 << k for k in range(1, count.bit_length() - 1)]
    groups = [bits[k : k + 2] for k in range(0, len(bits), 2)]
    other = groups[::-1] if len(groups[-1]) == 2 else groups
    return list(zip(groups, other))


def butterfly(block, beside):
    for hop, (even, odd) in enumerate(hops()):
        sent = round_bf16(block)
        wire = sent.astype(jnp.bfloat16)
        got = [swap(wire, lambda i: odd[0] if i % 2 else even[0])]
        if len(even) == 2:
            got.append(swap(wire, lambda i: odd[1] if i % 2 else even[1]))
            got.append(swap(wire, lambda i: sum(odd) if i % 2 else sum(even)))
        if hop == 0:
            got[-1], beside = lax.optimization_barrier((got[-1], beside))
        got = [value.astype(jnp.float32) for value in got]
        block = sent + got[0]
        if len(got) == 3:
            block = block + (got[1] + got[2])
    return block, beside


def area_of(local_points, tile_fill):
    points = local_points * lax.axis_size("space")
    local_index = jnp.arange(local_points, dtype=jnp.int32)
    global_index = lax.axis_index("space") * local_points + local_index
    live = local_index % TILE_PTS < jnp.repeat(tile_fill, TILE_PTS)
    latitude = jnp.pi * ((global_index.astype(jnp.float32) + 0.5) / points - 0.5)
    return jnp.where(live, jnp.cos(latitude), 0.0)


def project(latent, head_weight, head_bias):
    preds = jnp.einsum("mpd,dv->mvp", latent, head_weight, preferred_element_type=jnp.float32)
    return (preds + head_bias[None, :, None]).astype(jnp.bfloat16)


def back(grad_pred, head_weight):
    return jnp.einsum(
        "mvp,dv->mpd", grad_pred, head_weight, preferred_element_type=jnp.float32
    ).astype(jnp.bfloat16)


def general(latent, head_weight, head_bias, targets, var_weight, tile_fill):
    members = latent.shape[0] * lax.axis_size("ens")
    points = latent.shape[1] * lax.axis_size("space")
    preds = project(latent, head_weight, head_bias)
    values = preds.astype(jnp.float32)
    everyone = lax.all_gather(preds, "ens", axis=0, tiled=True)

    def one_member(slot, total):
        other = lax.dynamic_index_in_dim(everyone, slot, 0, keepdims=True).astype(jnp.float32)
        return total + smooth_sign(values - other)

    pair = lax.fori_loop(0, members, one_member, jnp.zeros(values.shape, jnp.float32))
    weight = area_of(latent.shape[1], tile_fill)[None, :] * var_weight[:, None]
    sign = smooth_sign(values - targets.astype(jnp.float32)[None])
    grad_pred = (weight[None] * (sign - pair / (members - 1))).astype(jnp.bfloat16)
    grad_latent = back(grad_pred, head_weight)
    scale = 1.0 / jnp.sqrt(jnp.float32(members) * jnp.float32(points))
    weight_sum = jnp.einsum("mpd,mvp->dv", latent, grad_pred, preferred_element_type=jnp.float32)
    bias_sum = jnp.sum(grad_pred.astype(jnp.float32), axis=(0, 2))
    weight_total, bias_total = lax.psum((weight_sum * scale, bias_sum * scale), ALL)
    return grad_latent, weight_total, bias_total


def four_members(latent, head_weight, head_bias, targets, var_weight, tile_fill):
    points = latent.shape[1] * lax.axis_size("space")
    half = latent.shape[2] // 2
    core = lax.axis_index("ens") % 2
    kept = lax.dynamic_slice_in_dim(latent[0], core * half, half, 1)
    given = lax.dynamic_slice_in_dim(latent[0], (1 - core) * half, half, 1)
    taken = swap(given, lambda i: 1)
    preds = project(latent, head_weight, head_bias)
    across = swap(preds, lambda i: 2)
    beside = swap(preds, lambda i: 1)
    corner = swap(across, lambda i: 1)
    own, mate, far, corner, seen = (
        v.reshape(v.shape[-2:]).astype(jnp.float32) for v in (preds, beside, across, corner, targets)
    )
    weight = area_of(latent.shape[1], tile_fill)[None, :] * var_weight[:, None]
    inside = smooth_sign(own - mate)
    pair = inside + smooth_sign(own - far) + smooth_sign(own - corner)
    grad_own = (weight * (smooth_sign(own - seen) - pair / 3)).astype(jnp.bfloat16)
    pair = smooth_sign(mate - far) + smooth_sign(mate - corner) - inside
    grad_mate = (weight * (smooth_sign(mate - seen) - pair / 3)).astype(jnp.bfloat16)
    scale = 1.0 / jnp.sqrt(4 * jnp.float32(points))
    block = jnp.dot(grad_own, kept, preferred_element_type=jnp.float32)
    block += jnp.dot(grad_mate, taken, preferred_element_type=jnp.float32)
    bias = jnp.sum(grad_own.astype(jnp.float32) + grad_mate.astype(jnp.float32), axis=1)
    variables = bias.shape[0]
    row = jnp.pad(bias[None, :], ((0, 0), (0, half - variables)))
    block = jnp.concatenate([block, row], 0) * scale

    grad_latent = back(grad_own[None], head_weight)
    block, grad_latent = butterfly(block, grad_latent)
    there = swap(block, lambda i: 1)
    first = jnp.where(core == 0, block, there)
    second = jnp.where(core == 0, there, block)
    total = jnp.concatenate([first[:variables], second[:variables]], 1)
    return grad_latent, total.T, first[variables, :variables]


def local(latent, head_weight, head_bias, targets, var_weight, tile_fill):
    space, ens = lax.axis_size("space"), lax.axis_size("ens")
    members, _, channels = latent.shape
    fits = members == 1 and ens == 4 and is_pow2(space)
    fits = fits and channels % 256 == 0 and targets.shape[0] <= channels // 2
    plan = four_members if fits else general
    return plan(latent, head_weight, head_bias, targets, var_weight, tile_fill)


def solution(mesh):
    placed = (P("ens", "space", None), P(), P(), P(None, "space"), P(), P("space"))
    return jax.shard_map(
        local,
        mesh=mesh,
        in_specs=placed,
        out_specs=(P("ens", "space", None), P(), P()),
        check_vma=False,
    )
```

```python
import functools
import math

import jax
import jax.numpy as jnp
from jax import lax
from jax.experimental import pallas as pl
from jax.experimental.pallas import tpu as pltpu
from jax.sharding import PartitionSpec as P

TILE_PTS = 128
SMOOTH = 0.05
ALL = ("space", "ens")


def smooth_sign(value):
    return value * lax.rsqrt(value * value + SMOOTH * SMOOTH)


def is_pow2(n):
    return n > 0 and n & (n - 1) == 0


def swap(value, bits_of):
    count = lax.axis_size("space") * lax.axis_size("ens")
    return lax.ppermute(value, ALL, [(i, i ^ bits_of(i)) for i in range(count)])


def round_bf16(value):
    return lax.reduce_precision(value, exponent_bits=8, mantissa_bits=7)


def hops():
    count = lax.axis_size("space") * lax.axis_size("ens")
    bits = [1 << k for k in range(1, count.bit_length() - 1)]
    groups = [bits[k : k + 2] for k in range(0, len(bits), 2)]
    other = groups[::-1] if len(groups[-1]) == 2 else groups
    return list(zip(groups, other))


def butterfly(wire, beside):
    for hop, (even, odd) in enumerate(hops()):
        got = [swap(wire, lambda i: odd[0] if i % 2 else even[0])]
        if len(even) == 2:
            got.append(swap(wire, lambda i: odd[1] if i % 2 else even[1]))
            got.append(swap(wire, lambda i: sum(odd) if i % 2 else sum(even)))
        if hop == 0:
            got[-1], beside = lax.optimization_barrier((got[-1], beside))
        got = [value.astype(jnp.float32) for value in got]
        block = wire.astype(jnp.float32) + got[0]
        if len(got) == 3:
            block = block + (got[1] + got[2])
        wire = round_bf16(block).astype(jnp.bfloat16)
    return wire, beside


def area_of(local_points, tile_fill):
    points = local_points * lax.axis_size("space")
    local_index = jnp.arange(local_points, dtype=jnp.int32)
    global_index = lax.axis_index("space") * local_points + local_index
    live = local_index % TILE_PTS < jnp.repeat(tile_fill, TILE_PTS)
    latitude = jnp.pi * ((global_index.astype(jnp.float32) + 0.5) / points - 0.5)
    return jnp.where(live, jnp.cos(latitude), 0.0)


def project(latent, head_weight, head_bias):
    preds = jnp.einsum("mpd,dv->mvp", latent, head_weight, preferred_element_type=jnp.float32)
    return (preds + head_bias[None, :, None]).astype(jnp.bfloat16)


def back(grad_pred, head_weight):
    return jnp.einsum(
        "mvp,dv->mpd", grad_pred, head_weight, preferred_element_type=jnp.float32
    ).astype(jnp.bfloat16)


def general(latent, head_weight, head_bias, targets, var_weight, tile_fill):
    members = latent.shape[0] * lax.axis_size("ens")
    points = latent.shape[1] * lax.axis_size("space")
    preds = project(latent, head_weight, head_bias)
    values = preds.astype(jnp.float32)
    everyone = lax.all_gather(preds, "ens", axis=0, tiled=True)

    def one_member(slot, total):
        other = lax.dynamic_index_in_dim(everyone, slot, 0, keepdims=True).astype(jnp.float32)
        return total + smooth_sign(values - other)

    pair = lax.fori_loop(0, members, one_member, jnp.zeros(values.shape, jnp.float32))
    weight = area_of(latent.shape[1], tile_fill)[None, :] * var_weight[:, None]
    sign = smooth_sign(values - targets.astype(jnp.float32)[None])
    grad_pred = (weight[None] * (sign - pair / (members - 1))).astype(jnp.bfloat16)
    grad_latent = back(grad_pred, head_weight)
    scale = 1.0 / jnp.sqrt(jnp.float32(members) * jnp.float32(points))
    weight_sum = jnp.einsum("mpd,mvp->dv", latent, grad_pred, preferred_element_type=jnp.float32)
    bias_sum = jnp.sum(grad_pred.astype(jnp.float32), axis=(0, 2))
    weight_total, bias_total = lax.psum((weight_sum * scale, bias_sum * scale), ALL)
    return grad_latent, weight_total, bias_total


VMEM = pl.BlockSpec(memory_space=pltpu.VMEM)
SMEM = pl.BlockSpec(memory_space=pltpu.SMEM)
HBM = pl.BlockSpec(memory_space=pltpu.HBM)
LAST = (((1,), (1,)), ((), ()))
in_hbm = functools.partial(pltpu.with_memory_space_constraint, memory_space=pltpu.HBM)
PIECES = 3


def project_kernel(start, latent_hbm, weight_hbm, bias_hbm, out_ref, rows, weight, bias, row_sems, weight_sem, bias_sem):
    step = rows.shape[0] // PIECES
    weight_copy = pltpu.make_async_copy(weight_hbm, weight, weight_sem)
    weight_copy.start()
    bias_copy = pltpu.make_async_copy(bias_hbm, bias, bias_sem)
    bias_copy.start()
    copies = [
        pltpu.make_async_copy(
            latent_hbm.at[pl.ds(start + k * step, step)], rows.at[pl.ds(k * step, step)], row_sems.at[k]
        )
        for k in range(PIECES)
    ]
    for copy in copies:
        copy.start()
    weight_copy.wait()
    bias_copy.wait()
    for k, copy in enumerate(copies):
        copy.wait()
        part = lax.dot_general(
            rows[k * step : (k + 1) * step], weight[...], LAST, preferred_element_type=jnp.float32
        )
        out_ref[:, k * step : (k + 1) * step] = (part + bias[...]).T.astype(out_ref.dtype)


def project_rows(latent, weight, bias, start, count):
    variables, channels = weight.shape
    return pl.pallas_call(
        functools.partial(project_kernel, start),
        out_shape=jax.ShapeDtypeStruct((variables, count), jnp.bfloat16),
        in_specs=[HBM, HBM, HBM],
        out_specs=VMEM,
        scratch_shapes=[
            pltpu.VMEM((count, channels), jnp.bfloat16),
            pltpu.VMEM((variables, channels), jnp.bfloat16),
            pltpu.VMEM((1, variables), jnp.float32),
            pltpu.SemaphoreType.DMA((PIECES,)),
            pltpu.SemaphoreType.DMA,
            pltpu.SemaphoreType.DMA,
        ],
        compiler_params=pltpu.CompilerParams(vmem_limit_bytes=4 << 20),
        cost_estimate=pl.CostEstimate(
            flops=2 * count * channels * variables,
            bytes_accessed=2 * channels * (count + variables),
            transcendentals=0,
        ),
        name="project_rows",
    )(latent, weight, bias)


def gradient_kernel(start, final, scale, core_ref, var_ref, area_ref, own_ref, mate_ref, far_ref, corner_ref, seen_ref,
                    kept_hbm, taken_any, *rest):
    before_ref, grad_ref, block_ref, mate_grad, kept, taken, sems = rest if final else (None, *rest)
    variables, count = own_ref.shape
    half = block_ref.shape[1]
    lanes = pl.ds(pl.multiple_of(core_ref[0] * half, 128), half)
    copies = [
        pltpu.make_async_copy(source.at[pl.ds(start, count), lanes], target, sems.at[k])
        for k, (source, target) in enumerate(((kept_hbm, kept), (taken_any, taken)))
    ]
    for copy in copies:
        copy.start()
    var_weight = jnp.broadcast_to(var_ref[...], (128, variables)).T
    for k in range(count // 128):
        at = slice(k * 128, (k + 1) * 128)
        seen_at = slice(start + k * 128, start + (k + 1) * 128)
        own, mate, far, corner = (r[:, at].astype(jnp.float32) for r in (own_ref, mate_ref, far_ref, corner_ref))
        seen = seen_ref[:, seen_at].astype(jnp.float32)
        weight = area_ref[:, seen_at] * var_weight
        inside = smooth_sign(own - mate)
        pair = smooth_sign(own - far) + smooth_sign(own - corner) + inside
        grad_ref[:, at] = (weight * (smooth_sign(own - seen) - pair / 3)).astype(jnp.bfloat16)
        pair = smooth_sign(mate - far) + smooth_sign(mate - corner) - inside
        mate_grad[:, at] = (weight * (smooth_sign(mate - seen) - pair / 3)).astype(jnp.bfloat16)
    ones = jnp.ones((8, count), jnp.bfloat16)
    bias = lax.dot_general(ones, grad_ref[...], LAST, preferred_element_type=jnp.float32)
    bias += lax.dot_general(ones, mate_grad[...], LAST, preferred_element_type=jnp.float32)
    bias = jnp.pad(bias[: block_ref.shape[0] - variables], ((0, 0), (0, half - variables)))
    copies[0].wait()
    block = jnp.dot(grad_ref[...], kept[...], preferred_element_type=jnp.float32)
    copies[1].wait()
    block += jnp.dot(mate_grad[...], taken[...], preferred_element_type=jnp.float32)
    if final:
        block_ref[:variables] = ((block + before_ref[:variables]) * scale).astype(block_ref.dtype)
        block_ref[variables:] = ((bias + before_ref[variables:]) * scale).astype(block_ref.dtype)
    else:
        block_ref[:variables] = block
        block_ref[variables:] = bias


def gradient_rows(start, scale, core, var_weight, area, members, seen, kept, taken, before=None):
    variables, count = members[0].shape
    half = kept.shape[1] // 2
    final = before is not None
    rows = -(-(variables + 1) // 8) * 8
    more = (before,) if final else ()
    return pl.pallas_call(
        functools.partial(gradient_kernel, start, final, scale),
        out_shape=(
            jax.ShapeDtypeStruct((variables, count), jnp.bfloat16),
            jax.ShapeDtypeStruct((rows, half), jnp.bfloat16 if final else jnp.float32),
        ),
        in_specs=[SMEM] + [VMEM] * 7 + [HBM, pl.BlockSpec(memory_space=pl.ANY)] + [VMEM] * len(more),
        out_specs=(VMEM, VMEM),
        scratch_shapes=[
            pltpu.VMEM((variables, count), jnp.bfloat16),
            pltpu.VMEM((count, half), jnp.bfloat16),
            pltpu.VMEM((count, half), jnp.bfloat16),
            pltpu.SemaphoreType.DMA((2,)),
        ],
        compiler_params=pltpu.CompilerParams(vmem_limit_bytes=8 << 20),
        cost_estimate=pl.CostEstimate(
            flops=4 * count * half * rows, bytes_accessed=4 * count * half, transcendentals=7 * variables * count
        ),
        name="gradient_rows",
    )(core, var_weight[None], area[None], *members, seen, kept, taken, *more)


def tail_kernel(core_ref, here_ref, there_ref, out_ref, bias_ref):
    variables, channels = out_ref.shape
    half = channels // 2
    core = core_ref[0]
    out_ref[:, pl.ds(pl.multiple_of(core * half, 128), half)] = here_ref[:variables].astype(jnp.float32)
    out_ref[:, pl.ds(pl.multiple_of((1 - core) * half, 128), half)] = there_ref[:variables].astype(jnp.float32)
    row = slice(variables, variables + 1)
    bias = jnp.where(core == 0, here_ref[row].astype(jnp.float32), there_ref[row].astype(jnp.float32))
    bias_ref[...] = bias[:, :variables]


def tail(core, here, there, variables):
    return pl.pallas_call(
        tail_kernel,
        out_shape=(
            jax.ShapeDtypeStruct((variables, 2 * here.shape[1]), jnp.float32),
            jax.ShapeDtypeStruct((1, variables), jnp.float32),
        ),
        in_specs=[SMEM, VMEM, VMEM],
        out_specs=(VMEM, VMEM),
        compiler_params=pltpu.CompilerParams(vmem_limit_bytes=4 << 20),
        name="tail",
    )(core, here, there)


def four_members(latent, head_weight, head_bias, targets, var_weight, tile_fill):
    _, local_points, _ = latent.shape
    variables = targets.shape[0]
    core = (lax.axis_index("ens") % 2).astype(jnp.int32)[None]
    kept = in_hbm(latent[0])
    taken = swap(latent[0], lambda i: 1)
    weight = in_hbm(head_weight.T)
    offset = in_hbm(head_bias[None])
    area = area_of(local_points, tile_fill)
    scale = 1.0 / math.sqrt(4 * local_points * lax.axis_size("space"))
    count = local_points // 2
    first = project_rows(kept, weight, offset, 0, count)
    second = project_rows(kept, weight, offset, count, count)
    crossed = [swap(first, lambda i: 2), swap(second, lambda i: 2)]
    beside = [swap(first, lambda i: 1), swap(second, lambda i: 1)]
    corner = [swap(value, lambda i: 1) for value in crossed]
    members = list(zip((first, second), beside, crossed, corner))
    gradient = functools.partial(gradient_rows, scale=scale, core=core, var_weight=var_weight, area=area, seen=targets,
                                 kept=kept, taken=taken)
    first_grad, block = gradient(0, members=members[0])
    second_grad, block = gradient(count, members=members[1], before=block)
    grad_latent = back(jnp.concatenate([first_grad, second_grad], 1)[None], head_weight)
    block, grad_latent = butterfly(block, grad_latent)
    there = swap(block, lambda i: 1)
    total, bias = tail(core, block, there, variables)
    return grad_latent, total.T, bias[0]


def local(latent, head_weight, head_bias, targets, var_weight, tile_fill):
    space, ens = lax.axis_size("space"), lax.axis_size("ens")
    members, _, channels = latent.shape
    fits = members == 1 and ens == 4 and is_pow2(space)
    fits = fits and channels % 256 == 0 and targets.shape[0] <= 128 and latent.shape[1] % (256 * PIECES) == 0
    plan = four_members if fits else general
    return plan(latent, head_weight, head_bias, targets, var_weight, tile_fill)


def solution(mesh):
    placed = (P("ens", "space", None), P(), P(), P(None, "space"), P(), P("space"))
    return jax.shard_map(
        local,
        mesh=mesh,
        in_specs=placed,
        out_specs=(P("ens", "space", None), P(), P()),
        check_vma=False,
    )
```

```python
import functools
import math

import jax
import jax.numpy as jnp
from jax import lax
from jax.experimental import pallas as pl
from jax.experimental.pallas import tpu as pltpu
from jax.sharding import PartitionSpec as P

TILE_PTS = 128
SMOOTH = 0.05
ALL = ("space", "ens")


def smooth_sign(value):
    return value * lax.rsqrt(value * value + SMOOTH * SMOOTH)


def is_pow2(n):
    return n > 0 and n & (n - 1) == 0


def swap(value, bits_of):
    count = lax.axis_size("space") * lax.axis_size("ens")
    return lax.ppermute(value, ALL, [(i, i ^ bits_of(i)) for i in range(count)])


def round_bf16(value):
    return lax.reduce_precision(value, exponent_bits=8, mantissa_bits=7)


def hops():
    count = lax.axis_size("space") * lax.axis_size("ens")
    bits = [1 << k for k in range(1, count.bit_length() - 1)]
    groups = [bits[k : k + 2] for k in range(0, len(bits), 2)]
    other = groups[::-1] if len(groups[-1]) == 2 else groups
    return list(zip(groups, other))


def butterfly(wire, beside):
    for hop, (even, odd) in enumerate(hops()):
        got = [swap(wire, lambda i: odd[0] if i % 2 else even[0])]
        if len(even) == 2:
            got.append(swap(wire, lambda i: odd[1] if i % 2 else even[1]))
            got.append(swap(wire, lambda i: sum(odd) if i % 2 else sum(even)))
        if hop == 0:
            got[-1], beside = lax.optimization_barrier((got[-1], beside))
        got = [value.astype(jnp.float32) for value in got]
        block = wire.astype(jnp.float32) + got[0]
        if len(got) == 3:
            block = block + (got[1] + got[2])
        wire = round_bf16(block).astype(jnp.bfloat16)
    return wire, beside


def area_of(local_points, tile_fill):
    points = local_points * lax.axis_size("space")
    local_index = jnp.arange(local_points, dtype=jnp.int32)
    global_index = lax.axis_index("space") * local_points + local_index
    live = local_index % TILE_PTS < jnp.repeat(tile_fill, TILE_PTS)
    latitude = jnp.pi * ((global_index.astype(jnp.float32) + 0.5) / points - 0.5)
    return jnp.where(live, jnp.cos(latitude), 0.0)


def project(latent, head_weight, head_bias):
    preds = jnp.einsum("mpd,dv->mvp", latent, head_weight, preferred_element_type=jnp.float32)
    return (preds + head_bias[None, :, None]).astype(jnp.bfloat16)


def back(grad_pred, head_weight):
    return jnp.einsum(
        "mvp,dv->mpd", grad_pred, head_weight, preferred_element_type=jnp.float32
    ).astype(jnp.bfloat16)


def general(latent, head_weight, head_bias, targets, var_weight, tile_fill):
    members = latent.shape[0] * lax.axis_size("ens")
    points = latent.shape[1] * lax.axis_size("space")
    preds = project(latent, head_weight, head_bias)
    values = preds.astype(jnp.float32)
    everyone = lax.all_gather(preds, "ens", axis=0, tiled=True)

    def one_member(slot, total):
        other = lax.dynamic_index_in_dim(everyone, slot, 0, keepdims=True).astype(jnp.float32)
        return total + smooth_sign(values - other)

    pair = lax.fori_loop(0, members, one_member, jnp.zeros(values.shape, jnp.float32))
    weight = area_of(latent.shape[1], tile_fill)[None, :] * var_weight[:, None]
    sign = smooth_sign(values - targets.astype(jnp.float32)[None])
    grad_pred = (weight[None] * (sign - pair / (members - 1))).astype(jnp.bfloat16)
    grad_latent = back(grad_pred, head_weight)
    scale = 1.0 / jnp.sqrt(jnp.float32(members) * jnp.float32(points))
    weight_sum = jnp.einsum("mpd,mvp->dv", latent, grad_pred, preferred_element_type=jnp.float32)
    bias_sum = jnp.sum(grad_pred.astype(jnp.float32), axis=(0, 2))
    weight_total, bias_total = lax.psum((weight_sum * scale, bias_sum * scale), ALL)
    return grad_latent, weight_total, bias_total


VMEM = pl.BlockSpec(memory_space=pltpu.VMEM)
SMEM = pl.BlockSpec(memory_space=pltpu.SMEM)
HBM = pl.BlockSpec(memory_space=pltpu.HBM)
LAST = (((1,), (1,)), ((), ()))
in_hbm = functools.partial(pltpu.with_memory_space_constraint, memory_space=pltpu.HBM)
in_hbm = functools.partial(pltpu.with_memory_space_constraint, memory_space=pltpu.HBM)


def halves_of(core, half):
    return [pl.ds(pl.multiple_of(c * half, 128), half) for c in (core, 1 - core)]


def project_kernel(core_ref, latent_hbm, weight_hbm, bias_hbm, preds_ref, kept_ref, given_ref, weight, bias, sems):
    sides = list(zip(halves_of(core_ref[0], kept_ref.shape[1]), (kept_ref, given_ref)))
    pairs = [(weight_hbm, weight), (bias_hbm, bias)]
    pairs += [(latent_hbm.at[:, lanes], target) for lanes, target in sides]
    copies = [pltpu.make_async_copy(source, target, sems.at[k]) for k, (source, target) in enumerate(pairs)]
    for copy in copies:
        copy.start()
    for copy in copies:
        copy.wait()
    total = bias[...]
    for lanes, rows in sides:
        total = total + lax.dot_general(rows[...], weight[:, lanes], LAST, preferred_element_type=jnp.float32)
    preds_ref[...] = total.T.astype(preds_ref.dtype)


def project_rows(core, latent, weight, bias):
    variables, channels = weight.shape
    count = latent.shape[0]
    part = jax.ShapeDtypeStruct((count, channels // 2), jnp.bfloat16)
    return pl.pallas_call(
        project_kernel,
        out_shape=(jax.ShapeDtypeStruct((variables, count), jnp.bfloat16), part, part),
        in_specs=[SMEM, HBM, HBM, HBM],
        out_specs=(VMEM, VMEM, VMEM),
        scratch_shapes=[
            pltpu.VMEM((variables, channels), jnp.bfloat16),
            pltpu.VMEM((1, variables), jnp.float32),
            pltpu.SemaphoreType.DMA((4,)),
        ],
        compiler_params=pltpu.CompilerParams(vmem_limit_bytes=8 << 20),
        cost_estimate=pl.CostEstimate(
            flops=2 * count * channels * variables,
            bytes_accessed=2 * channels * (count + variables),
            transcendentals=0,
        ),
        name="project_rows",
    )(core, latent, weight, bias)


def gradient_kernel(scale, var_ref, area_ref, own_ref, mate_ref, far_ref, corner_ref, seen_ref, kept_ref, taken_ref,
                    grad_ref, block_ref, mate_grad):
    variables, count = own_ref.shape
    half = block_ref.shape[1]
    var_weight = jnp.broadcast_to(var_ref[...], (128, variables)).T
    for k in range(count // 128):
        at = slice(k * 128, (k + 1) * 128)
        own, mate, far, corner, seen = (
            r[:, at].astype(jnp.float32) for r in (own_ref, mate_ref, far_ref, corner_ref, seen_ref)
        )
        weight = area_ref[:, at] * var_weight
        inside = smooth_sign(own - mate)
        pair = smooth_sign(own - far) + smooth_sign(own - corner) + inside
        grad_ref[:, at] = (weight * (smooth_sign(own - seen) - pair * (1 / 3))).astype(jnp.bfloat16)
        pair = smooth_sign(mate - far) + smooth_sign(mate - corner) - inside
        mate_grad[:, at] = (weight * (smooth_sign(mate - seen) - pair * (1 / 3))).astype(jnp.bfloat16)
    block = jnp.dot(grad_ref[...], kept_ref[...], preferred_element_type=jnp.float32)
    block += jnp.dot(mate_grad[...], taken_ref[...], preferred_element_type=jnp.float32)
    ones = jnp.ones((8, count), jnp.bfloat16)
    bias = lax.dot_general(ones, grad_ref[...], LAST, preferred_element_type=jnp.float32)
    bias += lax.dot_general(ones, mate_grad[...], LAST, preferred_element_type=jnp.float32)
    bias = jnp.pad(bias[: block_ref.shape[0] - variables], ((0, 0), (0, half - variables)))
    block_ref[:variables] = (block * scale).astype(block_ref.dtype)
    block_ref[variables:] = (bias * scale).astype(block_ref.dtype)


def gradient_rows(scale, var_weight, area, own, mate, far, corner, seen, kept, taken):
    variables, count = own.shape
    half = kept.shape[1]
    rows = -(-(variables + 1) // 8) * 8
    return pl.pallas_call(
        functools.partial(gradient_kernel, scale),
        out_shape=(
            jax.ShapeDtypeStruct((variables, count), jnp.bfloat16),
            jax.ShapeDtypeStruct((rows, half), jnp.bfloat16),
        ),
        in_specs=[VMEM] * 9,
        out_specs=(VMEM, VMEM),
        scratch_shapes=[pltpu.VMEM((variables, count), jnp.bfloat16)],
        compiler_params=pltpu.CompilerParams(vmem_limit_bytes=8 << 20),
        cost_estimate=pl.CostEstimate(
            flops=4 * count * half * rows, bytes_accessed=4 * count * half, transcendentals=7 * variables * count
        ),
        name="gradient_rows",
    )(var_weight[None], area[None], own, mate, far, corner, seen, kept, taken)


def tail_kernel(core_ref, here_ref, there_ref, out_ref, bias_ref):
    variables, channels = out_ref.shape
    half = channels // 2
    core = core_ref[0]
    out_ref[:, pl.ds(pl.multiple_of(core * half, 128), half)] = here_ref[:variables].astype(jnp.float32)
    out_ref[:, pl.ds(pl.multiple_of((1 - core) * half, 128), half)] = there_ref[:variables].astype(jnp.float32)
    row = slice(variables, variables + 1)
    bias = jnp.where(core == 0, here_ref[row].astype(jnp.float32), there_ref[row].astype(jnp.float32))
    bias_ref[...] = bias[:, :variables]


def tail(core, here, there, variables):
    return pl.pallas_call(
        tail_kernel,
        out_shape=(
            jax.ShapeDtypeStruct((variables, 2 * here.shape[1]), jnp.float32),
            jax.ShapeDtypeStruct((1, variables), jnp.float32),
        ),
        in_specs=[SMEM, VMEM, VMEM],
        out_specs=(VMEM, VMEM),
        compiler_params=pltpu.CompilerParams(vmem_limit_bytes=4 << 20),
        name="tail",
    )(core, here, there)


def four_members(latent, head_weight, head_bias, targets, var_weight, tile_fill):
    _, local_points, _ = latent.shape
    core = (lax.axis_index("ens") % 2).astype(jnp.int32)[None]
    area = area_of(local_points, tile_fill)
    scale = 1.0 / math.sqrt(4 * local_points * lax.axis_size("space"))
    own, kept, given = project_rows(core, in_hbm(latent[0]), in_hbm(head_weight.T), in_hbm(head_bias[None]))
    far = swap(own, lambda i: 2)
    mate = swap(own, lambda i: 1)
    mate, given = lax.optimization_barrier((mate, given))
    taken = swap(given, lambda i: 1)
    corner = swap(far, lambda i: 1)
    grad, block = gradient_rows(scale, var_weight, area, own, mate, far, corner, targets, kept, taken)
    grad_latent = back(grad[None], head_weight)
    block, grad_latent = butterfly(block, grad_latent)
    there = swap(block, lambda i: 1)
    total, bias = tail(core, block, there, targets.shape[0])
    return grad_latent, total.T, bias[0]


def local(latent, head_weight, head_bias, targets, var_weight, tile_fill):
    space, ens = lax.axis_size("space"), lax.axis_size("ens")
    members, _, channels = latent.shape
    fits = members == 1 and ens == 4 and is_pow2(space)
    fits = fits and channels % 256 == 0 and targets.shape[0] <= 128 and latent.shape[1] % 128 == 0
    plan = four_members if fits else general
    return plan(latent, head_weight, head_bias, targets, var_weight, tile_fill)


def solution(mesh):
    placed = (P("ens", "space", None), P(), P(), P(None, "space"), P(), P("space"))
    return jax.shard_map(
        local,
        mesh=mesh,
        in_specs=placed,
        out_specs=(P("ens", "space", None), P(), P()),
        check_vma=False,
    )
```

```python
import functools
import math

import jax
import jax.numpy as jnp
from jax import lax
from jax.experimental import pallas as pl
from jax.experimental.pallas import tpu as pltpu
from jax.sharding import PartitionSpec as P

TILE_PTS = 128
SMOOTH = 0.05
ALL = ("space", "ens")


def smooth_sign(value):
    return value * lax.rsqrt(value * value + SMOOTH * SMOOTH)


def is_pow2(n):
    return n > 0 and n & (n - 1) == 0


def swap(value, bits_of):
    count = lax.axis_size("space") * lax.axis_size("ens")
    return lax.ppermute(value, ALL, [(i, i ^ bits_of(i)) for i in range(count)])


def round_bf16(value):
    return lax.reduce_precision(value, exponent_bits=8, mantissa_bits=7)


def hops():
    count = lax.axis_size("space") * lax.axis_size("ens")
    bits = [1 << k for k in range(1, count.bit_length() - 1)]
    groups = [bits[k : k + 2] for k in range(0, len(bits), 2)]
    other = groups[::-1] if len(groups[-1]) == 2 else groups
    return list(zip(groups, other))


def butterfly(wire, beside):
    for hop, (even, odd) in enumerate(hops()):
        got = [swap(wire, lambda i: odd[0] if i % 2 else even[0])]
        if len(even) == 2:
            got.append(swap(wire, lambda i: odd[1] if i % 2 else even[1]))
            got.append(swap(wire, lambda i: sum(odd) if i % 2 else sum(even)))
        if hop == 0:
            got[-1], beside = lax.optimization_barrier((got[-1], beside))
        got = [value.astype(jnp.float32) for value in got]
        block = wire.astype(jnp.float32) + got[0]
        if len(got) == 3:
            block = block + (got[1] + got[2])
        wire = round_bf16(block).astype(jnp.bfloat16)
    return wire, beside


def area_of(local_points, tile_fill):
    points = local_points * lax.axis_size("space")
    local_index = jnp.arange(local_points, dtype=jnp.int32)
    global_index = lax.axis_index("space") * local_points + local_index
    live = local_index % TILE_PTS < jnp.repeat(tile_fill, TILE_PTS)
    latitude = jnp.pi * ((global_index.astype(jnp.float32) + 0.5) / points - 0.5)
    return jnp.where(live, jnp.cos(latitude), 0.0)


def project(latent, head_weight, head_bias):
    preds = jnp.einsum("mpd,dv->mvp", latent, head_weight, preferred_element_type=jnp.float32)
    return (preds + head_bias[None, :, None]).astype(jnp.bfloat16)


def back(grad_pred, head_weight):
    return jnp.einsum(
        "mvp,dv->mpd", grad_pred, head_weight, preferred_element_type=jnp.float32
    ).astype(jnp.bfloat16)


def general(latent, head_weight, head_bias, targets, var_weight, tile_fill):
    members = latent.shape[0] * lax.axis_size("ens")
    points = latent.shape[1] * lax.axis_size("space")
    preds = project(latent, head_weight, head_bias)
    values = preds.astype(jnp.float32)
    everyone = lax.all_gather(preds, "ens", axis=0, tiled=True)

    def one_member(slot, total):
        other = lax.dynamic_index_in_dim(everyone, slot, 0, keepdims=True).astype(jnp.float32)
        return total + smooth_sign(values - other)

    pair = lax.fori_loop(0, members, one_member, jnp.zeros(values.shape, jnp.float32))
    weight = area_of(latent.shape[1], tile_fill)[None, :] * var_weight[:, None]
    sign = smooth_sign(values - targets.astype(jnp.float32)[None])
    grad_pred = (weight[None] * (sign - pair / (members - 1))).astype(jnp.bfloat16)
    grad_latent = back(grad_pred, head_weight)
    scale = 1.0 / jnp.sqrt(jnp.float32(members) * jnp.float32(points))
    weight_sum = jnp.einsum("mpd,mvp->dv", latent, grad_pred, preferred_element_type=jnp.float32)
    bias_sum = jnp.sum(grad_pred.astype(jnp.float32), axis=(0, 2))
    weight_total, bias_total = lax.psum((weight_sum * scale, bias_sum * scale), ALL)
    return grad_latent, weight_total, bias_total


VMEM = pl.BlockSpec(memory_space=pltpu.VMEM)
SMEM = pl.BlockSpec(memory_space=pltpu.SMEM)
HBM = pl.BlockSpec(memory_space=pltpu.HBM)
LAST = (((1,), (1,)), ((), ()))
PIECES = 3
in_hbm = functools.partial(pltpu.with_memory_space_constraint, memory_space=pltpu.HBM)
in_hbm = functools.partial(pltpu.with_memory_space_constraint, memory_space=pltpu.HBM)


def halves_of(core, half):
    return [pl.ds(pl.multiple_of(c * half, 128), half) for c in (core, 1 - core)]


def project_kernel(core_ref, latent_hbm, weight_hbm, bias_hbm, preds_ref, kept_ref, *rest):
    *given_refs, weight, bias, sems = rest
    mine, other = halves_of(core_ref[0], kept_ref.shape[1])
    step = given_refs[0].shape[0]
    pairs = [(weight_hbm, weight), (bias_hbm, bias), (latent_hbm.at[:, mine], kept_ref)]
    pairs += [(latent_hbm.at[pl.ds(k * step, step), other], ref) for k, ref in enumerate(given_refs)]
    copies = [pltpu.make_async_copy(source, target, sems.at[k]) for k, (source, target) in enumerate(pairs)]
    for copy in copies:
        copy.start()
    for copy in copies:
        copy.wait()
    given = jnp.concatenate([ref[...] for ref in given_refs], 0)
    total = bias[...] + lax.dot_general(kept_ref[...], weight[:, mine], LAST, preferred_element_type=jnp.float32)
    total = total + lax.dot_general(given, weight[:, other], LAST, preferred_element_type=jnp.float32)
    preds_ref[...] = total.T.astype(preds_ref.dtype)


def project_rows(core, latent, weight, bias):
    variables, channels = weight.shape
    count = latent.shape[0]
    part = jax.ShapeDtypeStruct((count, channels // 2), jnp.bfloat16)
    piece = jax.ShapeDtypeStruct((count // PIECES, channels // 2), jnp.bfloat16)
    return pl.pallas_call(
        project_kernel,
        out_shape=[jax.ShapeDtypeStruct((variables, count), jnp.bfloat16), part] + [piece] * PIECES,
        in_specs=[SMEM, HBM, HBM, HBM],
        out_specs=[VMEM] * (2 + PIECES),
        scratch_shapes=[
            pltpu.VMEM((variables, channels), jnp.bfloat16),
            pltpu.VMEM((1, variables), jnp.float32),
            pltpu.SemaphoreType.DMA((3 + PIECES,)),
        ],
        compiler_params=pltpu.CompilerParams(vmem_limit_bytes=8 << 20),
        cost_estimate=pl.CostEstimate(
            flops=2 * count * channels * variables,
            bytes_accessed=2 * channels * (count + variables),
            transcendentals=0,
        ),
        name="project_rows",
    )(core, latent, weight, bias)


def gradient_kernel(scale, var_ref, area_ref, own_ref, mate_ref, far_ref, corner_ref, seen_ref, kept_ref, *rest):
    *taken_refs, grad_ref, block_ref, mate_grad = rest
    variables, count = own_ref.shape
    half = block_ref.shape[1]
    var_weight = jnp.broadcast_to(var_ref[...], (128, variables)).T
    for k in range(count // 128):
        at = slice(k * 128, (k + 1) * 128)
        own, mate, far, corner, seen = (
            r[:, at].astype(jnp.float32) for r in (own_ref, mate_ref, far_ref, corner_ref, seen_ref)
        )
        weight = area_ref[:, at] * var_weight
        inside = smooth_sign(own - mate)
        pair = smooth_sign(own - far) + smooth_sign(own - corner) + inside
        grad_ref[:, at] = (weight * (smooth_sign(own - seen) - pair * (1 / 3))).astype(jnp.bfloat16)
        pair = smooth_sign(mate - far) + smooth_sign(mate - corner) - inside
        mate_grad[:, at] = (weight * (smooth_sign(mate - seen) - pair * (1 / 3))).astype(jnp.bfloat16)
    block = jnp.dot(grad_ref[...], kept_ref[...], preferred_element_type=jnp.float32)
    taken = jnp.concatenate([ref[...] for ref in taken_refs], 0)
    block += jnp.dot(mate_grad[...], taken, preferred_element_type=jnp.float32)
    ones = jnp.ones((8, count), jnp.bfloat16)
    bias = lax.dot_general(ones, grad_ref[...], LAST, preferred_element_type=jnp.float32)
    bias += lax.dot_general(ones, mate_grad[...], LAST, preferred_element_type=jnp.float32)
    bias = jnp.pad(bias[: block_ref.shape[0] - variables], ((0, 0), (0, half - variables)))
    block_ref[:variables] = (block * scale).astype(block_ref.dtype)
    block_ref[variables:] = (bias * scale).astype(block_ref.dtype)


def gradient_rows(scale, var_weight, area, own, mate, far, corner, seen, kept, taken):
    variables, count = own.shape
    half = kept.shape[1]
    rows = -(-(variables + 1) // 8) * 8
    return pl.pallas_call(
        functools.partial(gradient_kernel, scale),
        out_shape=(
            jax.ShapeDtypeStruct((variables, count), jnp.bfloat16),
            jax.ShapeDtypeStruct((rows, half), jnp.bfloat16),
        ),
        in_specs=[VMEM] * (8 + PIECES),
        out_specs=(VMEM, VMEM),
        scratch_shapes=[pltpu.VMEM((variables, count), jnp.bfloat16)],
        compiler_params=pltpu.CompilerParams(vmem_limit_bytes=8 << 20),
        cost_estimate=pl.CostEstimate(
            flops=4 * count * half * rows, bytes_accessed=4 * count * half, transcendentals=7 * variables * count
        ),
        name="gradient_rows",
    )(var_weight[None], area[None], own, mate, far, corner, seen, kept, *taken)


def tail_kernel(core_ref, here_ref, there_ref, out_ref, bias_ref):
    variables, channels = out_ref.shape
    half = channels // 2
    core = core_ref[0]
    out_ref[:, pl.ds(pl.multiple_of(core * half, 128), half)] = here_ref[:variables].astype(jnp.float32)
    out_ref[:, pl.ds(pl.multiple_of((1 - core) * half, 128), half)] = there_ref[:variables].astype(jnp.float32)
    row = slice(variables, variables + 1)
    bias = jnp.where(core == 0, here_ref[row].astype(jnp.float32), there_ref[row].astype(jnp.float32))
    bias_ref[...] = bias[:, :variables]


def tail(core, here, there, variables):
    return pl.pallas_call(
        tail_kernel,
        out_shape=(
            jax.ShapeDtypeStruct((variables, 2 * here.shape[1]), jnp.float32),
            jax.ShapeDtypeStruct((1, variables), jnp.float32),
        ),
        in_specs=[SMEM, VMEM, VMEM],
        out_specs=(VMEM, VMEM),
        compiler_params=pltpu.CompilerParams(vmem_limit_bytes=4 << 20),
        name="tail",
    )(core, here, there)


def four_members(latent, head_weight, head_bias, targets, var_weight, tile_fill):
    _, local_points, _ = latent.shape
    core = (lax.axis_index("ens") % 2).astype(jnp.int32)[None]
    scale = 1.0 / math.sqrt(4 * local_points * lax.axis_size("space"))
    area = area_of(local_points, tile_fill)
    own, kept, *given = project_rows(core, in_hbm(latent[0]), in_hbm(head_weight.T), in_hbm(head_bias[None]))
    far = swap(own, lambda i: 2)
    mate = swap(own, lambda i: 1)
    taken = [swap(piece, lambda i: 1) for piece in given]
    corner = swap(far, lambda i: 1)
    grad, block = gradient_rows(scale, var_weight, area, own, mate, far, corner, targets, kept, taken)
    grad_latent = back(grad[None], head_weight)
    block, grad_latent = butterfly(block, grad_latent)
    there = swap(block, lambda i: 1)
    total, bias = tail(core, block, there, targets.shape[0])
    return grad_latent, total.T, bias[0]


def local(latent, head_weight, head_bias, targets, var_weight, tile_fill):
    space, ens = lax.axis_size("space"), lax.axis_size("ens")
    members, _, channels = latent.shape
    fits = members == 1 and ens == 4 and is_pow2(space)
    fits = fits and channels % 256 == 0 and targets.shape[0] <= 128 and latent.shape[1] % (128 * PIECES) == 0
    plan = four_members if fits else general
    return plan(latent, head_weight, head_bias, targets, var_weight, tile_fill)


def solution(mesh):
    placed = (P("ens", "space", None), P(), P(), P(None, "space"), P(), P("space"))
    return jax.shard_map(
        local,
        mesh=mesh,
        in_specs=placed,
        out_specs=(P("ens", "space", None), P(), P()),
        check_vma=False,
    )
```

```python
import functools
import math

import jax
import jax.numpy as jnp
from jax import lax
from jax.experimental import pallas as pl
from jax.experimental.pallas import tpu as pltpu
from jax.sharding import PartitionSpec as P

TILE_PTS = 128
SMOOTH = 0.05
ALL = ("space", "ens")


def smooth_sign(value):
    return value * lax.rsqrt(value * value + SMOOTH * SMOOTH)


def is_pow2(n):
    return n > 0 and n & (n - 1) == 0


def swap(value, bits_of):
    count = lax.axis_size("space") * lax.axis_size("ens")
    return lax.ppermute(value, ALL, [(i, i ^ bits_of(i)) for i in range(count)])


def round_bf16(value):
    return lax.reduce_precision(value, exponent_bits=8, mantissa_bits=7)


def hops():
    count = lax.axis_size("space") * lax.axis_size("ens")
    bits = [1 << k for k in range(1, count.bit_length() - 1)]
    groups = [bits[k : k + 2] for k in range(0, len(bits), 2)]
    other = groups[::-1] if len(groups[-1]) == 2 else groups
    return list(zip(groups, other))


def butterfly(wire, beside):
    for hop, (even, odd) in enumerate(hops()):
        got = [swap(wire, lambda i: odd[0] if i % 2 else even[0])]
        if len(even) == 2:
            got.append(swap(wire, lambda i: odd[1] if i % 2 else even[1]))
            got.append(swap(wire, lambda i: sum(odd) if i % 2 else sum(even)))
        if hop == 0:
            *got, beside = lax.optimization_barrier((*got, beside))
        got = [value.astype(jnp.float32) for value in got]
        block = wire.astype(jnp.float32) + got[0]
        if len(got) == 3:
            block = block + (got[1] + got[2])
        wire = round_bf16(block).astype(jnp.bfloat16)
    return wire, beside


def area_of(local_points, tile_fill):
    points = local_points * lax.axis_size("space")
    local_index = jnp.arange(local_points, dtype=jnp.int32)
    global_index = lax.axis_index("space") * local_points + local_index
    live = local_index % TILE_PTS < jnp.repeat(tile_fill, TILE_PTS)
    latitude = jnp.pi * ((global_index.astype(jnp.float32) + 0.5) / points - 0.5)
    return jnp.where(live, jnp.cos(latitude), 0.0)


def project(latent, head_weight, head_bias):
    preds = jnp.einsum("mpd,dv->mvp", latent, head_weight, preferred_element_type=jnp.float32)
    return (preds + head_bias[None, :, None]).astype(jnp.bfloat16)


def back(grad_pred, head_weight):
    return jnp.einsum(
        "mvp,dv->mpd", grad_pred, head_weight, preferred_element_type=jnp.float32
    ).astype(jnp.bfloat16)


def general(latent, head_weight, head_bias, targets, var_weight, tile_fill):
    members = latent.shape[0] * lax.axis_size("ens")
    points = latent.shape[1] * lax.axis_size("space")
    preds = project(latent, head_weight, head_bias)
    values = preds.astype(jnp.float32)
    everyone = lax.all_gather(preds, "ens", axis=0, tiled=True)

    def one_member(slot, total):
        other = lax.dynamic_index_in_dim(everyone, slot, 0, keepdims=True).astype(jnp.float32)
        return total + smooth_sign(values - other)

    pair = lax.fori_loop(0, members, one_member, jnp.zeros(values.shape, jnp.float32))
    weight = area_of(latent.shape[1], tile_fill)[None, :] * var_weight[:, None]
    sign = smooth_sign(values - targets.astype(jnp.float32)[None])
    grad_pred = (weight[None] * (sign - pair / (members - 1))).astype(jnp.bfloat16)
    grad_latent = back(grad_pred, head_weight)
    scale = 1.0 / jnp.sqrt(jnp.float32(members) * jnp.float32(points))
    weight_sum = jnp.einsum("mpd,mvp->dv", latent, grad_pred, preferred_element_type=jnp.float32)
    bias_sum = jnp.sum(grad_pred.astype(jnp.float32), axis=(0, 2))
    weight_total, bias_total = lax.psum((weight_sum * scale, bias_sum * scale), ALL)
    return grad_latent, weight_total, bias_total


VMEM = pl.BlockSpec(memory_space=pltpu.VMEM)
SMEM = pl.BlockSpec(memory_space=pltpu.SMEM)
HBM = pl.BlockSpec(memory_space=pltpu.HBM)
LAST = (((1,), (1,)), ((), ()))
PIECES = 3
in_hbm = functools.partial(pltpu.with_memory_space_constraint, memory_space=pltpu.HBM)
in_hbm = functools.partial(pltpu.with_memory_space_constraint, memory_space=pltpu.HBM)


def halves_of(core, half):
    return [pl.ds(pl.multiple_of(c * half, 128), half) for c in (core, 1 - core)]


def project_kernel(core_ref, latent_hbm, weight_hbm, bias_hbm, preds_ref, kept_ref, *rest):
    *given_refs, weight, bias, sems = rest
    mine, other = halves_of(core_ref[0], kept_ref.shape[1])
    step = given_refs[0].shape[0]
    pairs = [(weight_hbm, weight), (bias_hbm, bias), (latent_hbm.at[:, mine], kept_ref)]
    pairs += [(latent_hbm.at[pl.ds(k * step, step), other], ref) for k, ref in enumerate(given_refs)]
    copies = [pltpu.make_async_copy(source, target, sems.at[k]) for k, (source, target) in enumerate(pairs)]
    for copy in copies:
        copy.start()
    for copy in copies:
        copy.wait()
    given = jnp.concatenate([ref[...] for ref in given_refs], 0)
    total = bias[...] + lax.dot_general(kept_ref[...], weight[:, mine], LAST, preferred_element_type=jnp.float32)
    total = total + lax.dot_general(given, weight[:, other], LAST, preferred_element_type=jnp.float32)
    preds_ref[...] = total.T.astype(preds_ref.dtype)


def project_rows(core, latent, weight, bias):
    variables, channels = weight.shape
    count = latent.shape[0]
    part = jax.ShapeDtypeStruct((count, channels // 2), jnp.bfloat16)
    piece = jax.ShapeDtypeStruct((count // PIECES, channels // 2), jnp.bfloat16)
    return pl.pallas_call(
        project_kernel,
        out_shape=[jax.ShapeDtypeStruct((variables, count), jnp.bfloat16), part] + [piece] * PIECES,
        in_specs=[SMEM, HBM, HBM, HBM],
        out_specs=[VMEM] * (2 + PIECES),
        scratch_shapes=[
            pltpu.VMEM((variables, channels), jnp.bfloat16),
            pltpu.VMEM((1, variables), jnp.float32),
            pltpu.SemaphoreType.DMA((3 + PIECES,)),
        ],
        compiler_params=pltpu.CompilerParams(vmem_limit_bytes=8 << 20),
        cost_estimate=pl.CostEstimate(
            flops=2 * count * channels * variables,
            bytes_accessed=2 * channels * (count + variables),
            transcendentals=0,
        ),
        name="project_rows",
    )(core, latent, weight, bias)


def chunks(count):
    return [slice(k, k + 128) for k in range(0, count, 128)]


def column(row):
    return jnp.broadcast_to(row, (128, row.shape[1])).T


def terms_kernel(var_ref, area_ref, own_ref, mate_ref, far_ref, seen_ref, own_terms, mate_terms):
    var_weight = column(var_ref[...])
    for at in chunks(own_ref.shape[1]):
        own, mate, far, seen = (r[:, at].astype(jnp.float32) for r in (own_ref, mate_ref, far_ref, seen_ref))
        weight = area_ref[:, at] * var_weight
        inside = smooth_sign(own - mate)
        own_terms[:, at] = weight * (smooth_sign(own - seen) - (smooth_sign(own - far) + inside) * (1 / 3))
        mate_terms[:, at] = weight * (smooth_sign(mate - seen) - (smooth_sign(mate - far) - inside) * (1 / 3))


def terms_rows(var_weight, area, own, mate, far, seen):
    part = jax.ShapeDtypeStruct(own.shape, jnp.float32)
    return pl.pallas_call(
        terms_kernel,
        out_shape=(part, part),
        in_specs=[VMEM] * 6,
        out_specs=(VMEM, VMEM),
        compiler_params=pltpu.CompilerParams(vmem_limit_bytes=8 << 20),
        cost_estimate=pl.CostEstimate(flops=40 * own.size, bytes_accessed=16 * own.size, transcendentals=5 * own.size),
        name="terms_rows",
    )(var_weight, area, own, mate, far, seen)


def gradient_kernel(scale, var_ref, area_ref, own_ref, mate_ref, corner_ref, own_terms, mate_terms, kept_ref, *rest):
    *taken_refs, grad_ref, block_ref, mate_grad = rest
    variables, count = own_ref.shape
    half = block_ref.shape[1]
    third = column(var_ref[...]) * (1 / 3)
    total = jnp.zeros((variables, 128), jnp.float32)
    for at in chunks(count):
        own, mate, corner = (r[:, at].astype(jnp.float32) for r in (own_ref, mate_ref, corner_ref))
        weight = area_ref[:, at] * third
        own = (own_terms[:, at] - weight * smooth_sign(own - corner)).astype(jnp.bfloat16)
        mate = (mate_terms[:, at] - weight * smooth_sign(mate - corner)).astype(jnp.bfloat16)
        grad_ref[:, at] = own
        mate_grad[:, at] = mate
        total = total + (own.astype(jnp.float32) + mate.astype(jnp.float32))
    block = jnp.dot(grad_ref[...], kept_ref[...], preferred_element_type=jnp.float32)
    taken = jnp.concatenate([ref[...] for ref in taken_refs], 0)
    block += jnp.dot(mate_grad[...], taken, preferred_element_type=jnp.float32)
    bias = jnp.sum(total.T, axis=0, keepdims=True)
    bias = jnp.pad(bias, ((0, 0), (0, half - variables)))
    block_ref[:variables] = (block * scale).astype(block_ref.dtype)
    spare = block_ref.shape[0] - variables
    block_ref[variables:] = jnp.broadcast_to(bias * scale, (spare, half)).astype(block_ref.dtype)


def gradient_rows(scale, var_weight, area, own, mate, corner, terms, kept, taken):
    variables, count = own.shape
    half = kept.shape[1]
    rows = -(-(variables + 1) // 8) * 8
    return pl.pallas_call(
        functools.partial(gradient_kernel, scale),
        out_shape=(
            jax.ShapeDtypeStruct((variables, count), jnp.bfloat16),
            jax.ShapeDtypeStruct((rows, half), jnp.bfloat16),
        ),
        in_specs=[VMEM] * (8 + PIECES),
        out_specs=(VMEM, VMEM),
        scratch_shapes=[pltpu.VMEM((variables, count), jnp.bfloat16)],
        compiler_params=pltpu.CompilerParams(vmem_limit_bytes=8 << 20),
        cost_estimate=pl.CostEstimate(
            flops=4 * count * half * rows, bytes_accessed=4 * count * half, transcendentals=2 * variables * count
        ),
        name="gradient_rows",
    )(var_weight, area, own, mate, corner, *terms, kept, *taken)


def tail_kernel(core_ref, here_ref, there_ref, out_ref, bias_ref):
    variables, channels = out_ref.shape
    half = channels // 2
    core = core_ref[0]
    out_ref[:, pl.ds(pl.multiple_of(core * half, 128), half)] = here_ref[:variables].astype(jnp.float32)
    out_ref[:, pl.ds(pl.multiple_of((1 - core) * half, 128), half)] = there_ref[:variables].astype(jnp.float32)
    row = slice(variables, variables + 1)
    bias = jnp.where(core == 0, here_ref[row].astype(jnp.float32), there_ref[row].astype(jnp.float32))
    bias_ref[...] = bias[:, :variables]


def tail(core, here, there, variables):
    return pl.pallas_call(
        tail_kernel,
        out_shape=(
            jax.ShapeDtypeStruct((variables, 2 * here.shape[1]), jnp.float32),
            jax.ShapeDtypeStruct((1, variables), jnp.float32),
        ),
        in_specs=[SMEM, VMEM, VMEM],
        out_specs=(VMEM, VMEM),
        compiler_params=pltpu.CompilerParams(vmem_limit_bytes=4 << 20),
        name="tail",
    )(core, here, there)


def four_members(latent, head_weight, head_bias, targets, var_weight, tile_fill):
    _, local_points, _ = latent.shape
    core = (lax.axis_index("ens") % 2).astype(jnp.int32)[None]
    scale = 1.0 / math.sqrt(4 * local_points * lax.axis_size("space"))
    area = area_of(local_points, tile_fill)
    own, kept, *given = project_rows(core, in_hbm(latent[0]), in_hbm(head_weight.T), in_hbm(head_bias[None]))
    far = swap(own, lambda i: 2)
    mate = swap(own, lambda i: 1)
    taken = [swap(piece, lambda i: 1) for piece in given]
    corner = swap(far, lambda i: 1)
    rows = (var_weight[None], area[None])
    terms = terms_rows(*rows, own, mate, far, targets)
    grad, block = gradient_rows(scale, *rows, own, mate, corner, terms, kept, taken)
    grad_latent = back(grad[None], head_weight)
    block, grad_latent = butterfly(block, grad_latent)
    there = swap(block, lambda i: 1)
    total, bias = tail(core, block, there, targets.shape[0])
    return grad_latent, total.T, bias[0]


def local(latent, head_weight, head_bias, targets, var_weight, tile_fill):
    space, ens = lax.axis_size("space"), lax.axis_size("ens")
    members, _, channels = latent.shape
    fits = members == 1 and ens == 4 and is_pow2(space)
    fits = fits and channels % 256 == 0 and targets.shape[0] <= 128 and latent.shape[1] % (128 * PIECES) == 0
    plan = four_members if fits else general
    return plan(latent, head_weight, head_bias, targets, var_weight, tile_fill)


def solution(mesh):
    placed = (P("ens", "space", None), P(), P(), P(None, "space"), P(), P("space"))
    return jax.shard_map(
        local,
        mesh=mesh,
        in_specs=placed,
        out_specs=(P("ens", "space", None), P(), P()),
        check_vma=False,
    )
```

```python
import functools
import math

import jax
import jax.numpy as jnp
from jax import lax
from jax.experimental import pallas as pl
from jax.experimental.pallas import tpu as pltpu
from jax.sharding import PartitionSpec as P

TILE_PTS = 128
SMOOTH = 0.05
ALL = ("space", "ens")


def smooth_sign(value):
    return value * lax.rsqrt(value * value + SMOOTH * SMOOTH)


def is_pow2(n):
    return n > 0 and n & (n - 1) == 0


def swap(value, bits_of):
    count = lax.axis_size("space") * lax.axis_size("ens")
    return lax.ppermute(value, ALL, [(i, i ^ bits_of(i)) for i in range(count)])


def round_bf16(value):
    return lax.reduce_precision(value, exponent_bits=8, mantissa_bits=7)


def groups_of(count):
    bits = [1 << k for k in range(1, count.bit_length() - 1)]
    groups = [bits[k : k + 2] for k in range(0, len(bits), 2)]
    return groups, sum(group[-1] for group in groups)


def parity(value):
    return value.bit_count() % 2


def role_of(index, crossed):
    role = index % 2
    bit = 2
    while bit <= crossed:
        if bit & crossed:
            role = (role + index // bit) % 2
        bit *= 2
    return role


def hop_swap(wire, crossed, first, second):
    def bits_of(index):
        bits = second if role_of(index, crossed) else first
        return bits ^ parity(bits & crossed)

    return swap(wire, bits_of)


def butterfly(wire, beside):
    groups, crossed = groups_of(lax.axis_size("space") * lax.axis_size("ens"))
    other = groups[::-1] if len(groups[-1]) == 2 else groups
    for hop, (first, second) in enumerate(zip(groups, other)):
        got = [hop_swap(wire, crossed, first[0], second[0])]
        if len(first) == 2:
            got.append(hop_swap(wire, crossed, first[1], second[1]))
            got.append(hop_swap(wire, crossed, sum(first), sum(second)))
        if hop == 0:
            *got, beside = lax.optimization_barrier((*got, beside))
        got = [value.astype(jnp.float32) for value in got]
        block = wire.astype(jnp.float32) + got[0]
        if len(got) == 3:
            block = block + (got[1] + got[2])
        wire = round_bf16(block).astype(jnp.bfloat16)
    return wire, beside


def area_of(local_points, tile_fill):
    points = local_points * lax.axis_size("space")
    local_index = jnp.arange(local_points, dtype=jnp.int32)
    global_index = lax.axis_index("space") * local_points + local_index
    live = local_index % TILE_PTS < jnp.repeat(tile_fill, TILE_PTS)
    latitude = jnp.pi * ((global_index.astype(jnp.float32) + 0.5) / points - 0.5)
    return jnp.where(live, jnp.cos(latitude), 0.0)


def project(latent, head_weight, head_bias):
    preds = jnp.einsum("mpd,dv->mvp", latent, head_weight, preferred_element_type=jnp.float32)
    return (preds + head_bias[None, :, None]).astype(jnp.bfloat16)


def back(grad_pred, head_weight):
    return jnp.einsum(
        "mvp,dv->mpd", grad_pred, head_weight, preferred_element_type=jnp.float32
    ).astype(jnp.bfloat16)


def general(latent, head_weight, head_bias, targets, var_weight, tile_fill):
    members = latent.shape[0] * lax.axis_size("ens")
    points = latent.shape[1] * lax.axis_size("space")
    preds = project(latent, head_weight, head_bias)
    values = preds.astype(jnp.float32)
    everyone = lax.all_gather(preds, "ens", axis=0, tiled=True)

    def one_member(slot, total):
        other = lax.dynamic_index_in_dim(everyone, slot, 0, keepdims=True).astype(jnp.float32)
        return total + smooth_sign(values - other)

    pair = lax.fori_loop(0, members, one_member, jnp.zeros(values.shape, jnp.float32))
    weight = area_of(latent.shape[1], tile_fill)[None, :] * var_weight[:, None]
    sign = smooth_sign(values - targets.astype(jnp.float32)[None])
    grad_pred = (weight[None] * (sign - pair / (members - 1))).astype(jnp.bfloat16)
    grad_latent = back(grad_pred, head_weight)
    scale = 1.0 / jnp.sqrt(jnp.float32(members) * jnp.float32(points))
    weight_sum = jnp.einsum("mpd,mvp->dv", latent, grad_pred, preferred_element_type=jnp.float32)
    bias_sum = jnp.sum(grad_pred.astype(jnp.float32), axis=(0, 2))
    weight_total, bias_total = lax.psum((weight_sum * scale, bias_sum * scale), ALL)
    return grad_latent, weight_total, bias_total


VMEM = pl.BlockSpec(memory_space=pltpu.VMEM)
SMEM = pl.BlockSpec(memory_space=pltpu.SMEM)
HBM = pl.BlockSpec(memory_space=pltpu.HBM)
LAST = (((1,), (1,)), ((), ()))
PIECES = 3
in_hbm = functools.partial(pltpu.with_memory_space_constraint, memory_space=pltpu.HBM)
in_hbm = functools.partial(pltpu.with_memory_space_constraint, memory_space=pltpu.HBM)


def halves_of(role, half):
    return [pl.ds(pl.multiple_of(r * half, 128), half) for r in (role, 1 - role)]


def project_kernel(role_ref, latent_hbm, weight_hbm, bias_hbm, preds_ref, kept_ref, *rest):
    *given_refs, weight, bias, sems = rest
    mine, other = halves_of(role_ref[0], kept_ref.shape[1])
    step = given_refs[0].shape[0]
    pairs = [(weight_hbm, weight), (bias_hbm, bias), (latent_hbm.at[:, mine], kept_ref)]
    pairs += [(latent_hbm.at[pl.ds(k * step, step), other], ref) for k, ref in enumerate(given_refs)]
    copies = [pltpu.make_async_copy(source, target, sems.at[k]) for k, (source, target) in enumerate(pairs)]
    for copy in copies:
        copy.start()
    for copy in copies:
        copy.wait()
    given = jnp.concatenate([ref[...] for ref in given_refs], 0)
    total = bias[...] + lax.dot_general(kept_ref[...], weight[:, mine], LAST, preferred_element_type=jnp.float32)
    total = total + lax.dot_general(given, weight[:, other], LAST, preferred_element_type=jnp.float32)
    preds_ref[...] = total.T.astype(preds_ref.dtype)


def project_rows(role, latent, weight, bias):
    variables, channels = weight.shape
    count = latent.shape[0]
    part = jax.ShapeDtypeStruct((count, channels // 2), jnp.bfloat16)
    piece = jax.ShapeDtypeStruct((count // PIECES, channels // 2), jnp.bfloat16)
    return pl.pallas_call(
        project_kernel,
        out_shape=[jax.ShapeDtypeStruct((variables, count), jnp.bfloat16), part] + [piece] * PIECES,
        in_specs=[SMEM, HBM, HBM, HBM],
        out_specs=[VMEM] * (2 + PIECES),
        scratch_shapes=[
            pltpu.VMEM((variables, channels), jnp.bfloat16),
            pltpu.VMEM((1, variables), jnp.float32),
            pltpu.SemaphoreType.DMA((3 + PIECES,)),
        ],
        compiler_params=pltpu.CompilerParams(vmem_limit_bytes=8 << 20),
        cost_estimate=pl.CostEstimate(
            flops=2 * count * channels * variables,
            bytes_accessed=2 * channels * (count + variables),
            transcendentals=0,
        ),
        name="project_rows",
    )(role, latent, weight, bias)


def chunks(count):
    return [slice(k, k + 128) for k in range(0, count, 128)]


def column(row):
    return jnp.broadcast_to(row, (128, row.shape[1])).T


def terms_kernel(var_ref, area_ref, own_ref, mate_ref, far_ref, seen_ref, own_terms, mate_terms):
    var_weight = column(var_ref[...])
    for at in chunks(own_ref.shape[1]):
        own, mate, far, seen = (r[:, at].astype(jnp.float32) for r in (own_ref, mate_ref, far_ref, seen_ref))
        weight = area_ref[:, at] * var_weight
        inside = smooth_sign(own - mate)
        own_terms[:, at] = weight * (smooth_sign(own - seen) - (smooth_sign(own - far) + inside) * (1 / 3))
        mate_terms[:, at] = weight * (smooth_sign(mate - seen) - (smooth_sign(mate - far) - inside) * (1 / 3))


def terms_rows(var_weight, area, own, mate, far, seen):
    part = jax.ShapeDtypeStruct(own.shape, jnp.float32)
    return pl.pallas_call(
        terms_kernel,
        out_shape=(part, part),
        in_specs=[VMEM] * 6,
        out_specs=(VMEM, VMEM),
        compiler_params=pltpu.CompilerParams(vmem_limit_bytes=8 << 20),
        cost_estimate=pl.CostEstimate(flops=40 * own.size, bytes_accessed=16 * own.size, transcendentals=5 * own.size),
        name="terms_rows",
    )(var_weight, area, own, mate, far, seen)


def gradient_kernel(scale, var_ref, area_ref, own_ref, mate_ref, corner_ref, own_terms, mate_terms, kept_ref, *rest):
    *taken_refs, grad_ref, block_ref, mate_grad = rest
    variables, count = own_ref.shape
    half = block_ref.shape[1]
    third = column(var_ref[...]) * (1 / 3)
    total = jnp.zeros((variables, 128), jnp.float32)
    for at in chunks(count):
        own, mate, corner = (r[:, at].astype(jnp.float32) for r in (own_ref, mate_ref, corner_ref))
        weight = area_ref[:, at] * third
        own = (own_terms[:, at] - weight * smooth_sign(own - corner)).astype(jnp.bfloat16)
        mate = (mate_terms[:, at] - weight * smooth_sign(mate - corner)).astype(jnp.bfloat16)
        grad_ref[:, at] = own
        mate_grad[:, at] = mate
        total = total + (own.astype(jnp.float32) + mate.astype(jnp.float32))
    block = jnp.dot(grad_ref[...], kept_ref[...], preferred_element_type=jnp.float32)
    taken = jnp.concatenate([ref[...] for ref in taken_refs], 0)
    block += jnp.dot(mate_grad[...], taken, preferred_element_type=jnp.float32)
    bias = jnp.sum(total.T, axis=0, keepdims=True)
    bias = jnp.pad(bias, ((0, 0), (0, half - variables)))
    block_ref[:variables] = (block * scale).astype(block_ref.dtype)
    spare = block_ref.shape[0] - variables
    block_ref[variables:] = jnp.broadcast_to(bias * scale, (spare, half)).astype(block_ref.dtype)


def gradient_rows(scale, var_weight, area, own, mate, corner, terms, kept, taken):
    variables, count = own.shape
    half = kept.shape[1]
    rows = -(-(variables + 1) // 8) * 8
    return pl.pallas_call(
        functools.partial(gradient_kernel, scale),
        out_shape=(
            jax.ShapeDtypeStruct((variables, count), jnp.bfloat16),
            jax.ShapeDtypeStruct((rows, half), jnp.bfloat16),
        ),
        in_specs=[VMEM] * (8 + PIECES),
        out_specs=(VMEM, VMEM),
        scratch_shapes=[pltpu.VMEM((variables, count), jnp.bfloat16)],
        compiler_params=pltpu.CompilerParams(vmem_limit_bytes=8 << 20),
        cost_estimate=pl.CostEstimate(
            flops=4 * count * half * rows, bytes_accessed=4 * count * half, transcendentals=2 * variables * count
        ),
        name="gradient_rows",
    )(var_weight, area, own, mate, corner, *terms, kept, *taken)


def tail_kernel(role_ref, here_ref, there_ref, out_ref, bias_ref):
    variables, channels = out_ref.shape
    half = channels // 2
    role = role_ref[0]
    mine, other = halves_of(role, half)
    out_ref[:, mine] = here_ref[:variables].astype(jnp.float32)
    out_ref[:, other] = there_ref[:variables].astype(jnp.float32)
    row = slice(variables, variables + 1)
    bias = jnp.where(role == 0, here_ref[row].astype(jnp.float32), there_ref[row].astype(jnp.float32))
    bias_ref[...] = bias[:, :variables]


def tail(role, here, there, variables):
    return pl.pallas_call(
        tail_kernel,
        out_shape=(
            jax.ShapeDtypeStruct((variables, 2 * here.shape[1]), jnp.float32),
            jax.ShapeDtypeStruct((1, variables), jnp.float32),
        ),
        in_specs=[SMEM, VMEM, VMEM],
        out_specs=(VMEM, VMEM),
        compiler_params=pltpu.CompilerParams(vmem_limit_bytes=4 << 20),
        name="tail",
    )(role, here, there)


def four_members(latent, head_weight, head_bias, targets, var_weight, tile_fill):
    _, local_points, _ = latent.shape
    ens = lax.axis_size("ens")
    index = lax.axis_index("space") * ens + lax.axis_index("ens")
    role = role_of(index, groups_of(lax.axis_size("space") * ens)[1]).astype(jnp.int32)[None]
    scale = 1.0 / math.sqrt(4 * local_points * lax.axis_size("space"))
    area = area_of(local_points, tile_fill)
    own, kept, *given = project_rows(role, in_hbm(latent[0]), in_hbm(head_weight.T), in_hbm(head_bias[None]))
    far = swap(own, lambda i: 3)
    mate = swap(own, lambda i: 1)
    taken = [swap(piece, lambda i: 1) for piece in given]
    corner = swap(far, lambda i: 1)
    rows = (var_weight[None], area[None])
    terms = terms_rows(*rows, own, mate, far, targets)
    grad, block = gradient_rows(scale, *rows, own, mate, corner, terms, kept, taken)
    grad_latent = back(grad[None], head_weight)
    block, grad_latent = butterfly(block, grad_latent)
    there = swap(block, lambda i: 1)
    total, bias = tail(role, block, there, targets.shape[0])
    return grad_latent, total.T, bias[0]


def local(latent, head_weight, head_bias, targets, var_weight, tile_fill):
    space, ens = lax.axis_size("space"), lax.axis_size("ens")
    members, _, channels = latent.shape
    fits = members == 1 and ens == 4 and is_pow2(space)
    fits = fits and channels % 256 == 0 and targets.shape[0] <= 128 and latent.shape[1] % (128 * PIECES) == 0
    plan = four_members if fits else general
    return plan(latent, head_weight, head_bias, targets, var_weight, tile_fill)


def solution(mesh):
    placed = (P("ens", "space", None), P(), P(), P(None, "space"), P(), P("space"))
    return jax.shard_map(
        local,
        mesh=mesh,
        in_specs=placed,
        out_specs=(P("ens", "space", None), P(), P()),
        check_vma=False,
    )
```

```python
import functools
import math

import jax
import jax.numpy as jnp
from jax import lax
from jax.experimental import pallas as pl
from jax.experimental.pallas import tpu as pltpu
from jax.sharding import PartitionSpec as P

TILE_PTS = 128
SMOOTH = 0.05
ALL = ("space", "ens")


def smooth_sign(value):
    return value * lax.rsqrt(value * value + SMOOTH * SMOOTH)


def is_pow2(n):
    return n > 0 and n & (n - 1) == 0


def swap(value, bits_of):
    count = lax.axis_size("space") * lax.axis_size("ens")
    return lax.ppermute(value, ALL, [(i, i ^ bits_of(i)) for i in range(count)])


def round_bf16(value):
    return lax.reduce_precision(value, exponent_bits=8, mantissa_bits=7)


def groups_of(count):
    bits = [1 << k for k in range(1, count.bit_length() - 1)]
    groups = [bits[k : k + 2] for k in range(0, len(bits), 2)]
    return groups, sum(group[-1] for group in groups)


def parity(value):
    return value.bit_count() % 2


def role_of(index, crossed):
    role = index % 2
    bit = 2
    while bit <= crossed:
        if bit & crossed:
            role = (role + index // bit) % 2
        bit *= 2
    return role


def hop_swap(wire, crossed, first, second):
    def bits_of(index):
        bits = second if role_of(index, crossed) else first
        return bits ^ parity(bits & crossed)

    return swap(wire, bits_of)


def butterfly(wire, beside):
    groups, crossed = groups_of(lax.axis_size("space") * lax.axis_size("ens"))
    other = groups[::-1] if len(groups[-1]) == 2 else groups
    for hop, (first, second) in enumerate(zip(groups, other)):
        got = [hop_swap(wire, crossed, first[0], second[0])]
        if len(first) == 2:
            got.append(hop_swap(wire, crossed, first[1], second[1]))
            got.append(hop_swap(wire, crossed, sum(first), sum(second)))
        if hop == 0:
            *got, beside = lax.optimization_barrier((*got, beside))
        got = [value.astype(jnp.float32) for value in got]
        block = wire.astype(jnp.float32) + got[0]
        if len(got) == 3:
            block = block + (got[1] + got[2])
        wire = round_bf16(block).astype(jnp.bfloat16)
    return wire, beside


def area_of(local_points, tile_fill):
    points = local_points * lax.axis_size("space")
    local_index = jnp.arange(local_points, dtype=jnp.int32)
    global_index = lax.axis_index("space") * local_points + local_index
    live = local_index % TILE_PTS < jnp.repeat(tile_fill, TILE_PTS)
    latitude = jnp.pi * ((global_index.astype(jnp.float32) + 0.5) / points - 0.5)
    return jnp.where(live, jnp.cos(latitude), 0.0)


def project(latent, head_weight, head_bias):
    preds = jnp.einsum("mpd,dv->mvp", latent, head_weight, preferred_element_type=jnp.float32)
    return (preds + head_bias[None, :, None]).astype(jnp.bfloat16)


def back(grad_pred, head_weight):
    return jnp.einsum(
        "mvp,dv->mpd", grad_pred, head_weight, preferred_element_type=jnp.float32
    ).astype(jnp.bfloat16)


def general(latent, head_weight, head_bias, targets, var_weight, tile_fill):
    members = latent.shape[0] * lax.axis_size("ens")
    points = latent.shape[1] * lax.axis_size("space")
    preds = project(latent, head_weight, head_bias)
    values = preds.astype(jnp.float32)
    everyone = lax.all_gather(preds, "ens", axis=0, tiled=True)

    def one_member(slot, total):
        other = lax.dynamic_index_in_dim(everyone, slot, 0, keepdims=True).astype(jnp.float32)
        return total + smooth_sign(values - other)

    pair = lax.fori_loop(0, members, one_member, jnp.zeros(values.shape, jnp.float32))
    weight = area_of(latent.shape[1], tile_fill)[None, :] * var_weight[:, None]
    sign = smooth_sign(values - targets.astype(jnp.float32)[None])
    grad_pred = (weight[None] * (sign - pair / (members - 1))).astype(jnp.bfloat16)
    grad_latent = back(grad_pred, head_weight)
    scale = 1.0 / jnp.sqrt(jnp.float32(members) * jnp.float32(points))
    weight_sum = jnp.einsum("mpd,mvp->dv", latent, grad_pred, preferred_element_type=jnp.float32)
    bias_sum = jnp.sum(grad_pred.astype(jnp.float32), axis=(0, 2))
    weight_total, bias_total = lax.psum((weight_sum * scale, bias_sum * scale), ALL)
    return grad_latent, weight_total, bias_total


VMEM = pl.BlockSpec(memory_space=pltpu.VMEM)
SMEM = pl.BlockSpec(memory_space=pltpu.SMEM)
HBM = pl.BlockSpec(memory_space=pltpu.HBM)
LAST = (((1,), (1,)), ((), ()))
PIECES = 3
in_hbm = functools.partial(pltpu.with_memory_space_constraint, memory_space=pltpu.HBM)
in_hbm = functools.partial(pltpu.with_memory_space_constraint, memory_space=pltpu.HBM)


def halves_of(role, half):
    return [pl.ds(pl.multiple_of(r * half, 128), half) for r in (role, 1 - role)]


def project_kernel(role_ref, latent_hbm, weight_hbm, bias_hbm, preds_ref, kept_ref, *rest):
    *given_refs, weight, bias, sems = rest
    mine, other = halves_of(role_ref[0], kept_ref.shape[1])
    step = given_refs[0].shape[0]
    pairs = [(weight_hbm, weight), (bias_hbm, bias), (latent_hbm.at[:, mine], kept_ref)]
    pairs += [(latent_hbm.at[pl.ds(k * step, step), other], ref) for k, ref in enumerate(given_refs)]
    copies = [pltpu.make_async_copy(source, target, sems.at[k]) for k, (source, target) in enumerate(pairs)]
    for copy in copies:
        copy.start()
    for copy in copies:
        copy.wait()
    given = jnp.concatenate([ref[...] for ref in given_refs], 0)
    total = bias[...] + lax.dot_general(kept_ref[...], weight[:, mine], LAST, preferred_element_type=jnp.float32)
    total = total + lax.dot_general(given, weight[:, other], LAST, preferred_element_type=jnp.float32)
    preds_ref[...] = total.T.astype(preds_ref.dtype)


def project_rows(role, latent, weight, bias):
    variables, channels = weight.shape
    count = latent.shape[0]
    part = jax.ShapeDtypeStruct((count, channels // 2), jnp.bfloat16)
    piece = jax.ShapeDtypeStruct((count // PIECES, channels // 2), jnp.bfloat16)
    return pl.pallas_call(
        project_kernel,
        out_shape=[jax.ShapeDtypeStruct((variables, count), jnp.bfloat16), part] + [piece] * PIECES,
        in_specs=[SMEM, HBM, HBM, HBM],
        out_specs=[VMEM] * (2 + PIECES),
        scratch_shapes=[
            pltpu.VMEM((variables, channels), jnp.bfloat16),
            pltpu.VMEM((1, variables), jnp.float32),
            pltpu.SemaphoreType.DMA((3 + PIECES,)),
        ],
        compiler_params=pltpu.CompilerParams(vmem_limit_bytes=8 << 20),
        cost_estimate=pl.CostEstimate(
            flops=2 * count * channels * variables,
            bytes_accessed=2 * channels * (count + variables),
            transcendentals=0,
        ),
        name="project_rows",
    )(role, latent, weight, bias)


def chunks(count):
    return [slice(k, k + 128) for k in range(0, count, 128)]


def column(row):
    return jnp.broadcast_to(row, (128, row.shape[1])).T


def terms_kernel(var_ref, area_ref, own_ref, mate_ref, far_ref, seen_ref, own_terms, mate_terms):
    var_weight = column(var_ref[...])
    for at in chunks(own_ref.shape[1]):
        own, mate, far, seen = (r[:, at].astype(jnp.float32) for r in (own_ref, mate_ref, far_ref, seen_ref))
        weight = area_ref[:, at] * var_weight
        inside = smooth_sign(own - mate)
        own_terms[:, at] = weight * (smooth_sign(own - seen) - (smooth_sign(own - far) + inside) * (1 / 3))
        mate_terms[:, at] = weight * (smooth_sign(mate - seen) - (smooth_sign(mate - far) - inside) * (1 / 3))


def terms_rows(var_weight, area, own, mate, far, seen):
    part = jax.ShapeDtypeStruct(own.shape, jnp.float32)
    return pl.pallas_call(
        terms_kernel,
        out_shape=(part, part),
        in_specs=[VMEM] * 6,
        out_specs=(VMEM, VMEM),
        compiler_params=pltpu.CompilerParams(vmem_limit_bytes=8 << 20),
        cost_estimate=pl.CostEstimate(flops=40 * own.size, bytes_accessed=16 * own.size, transcendentals=5 * own.size),
        name="terms_rows",
    )(var_weight, area, own, mate, far, seen)


def gradient_kernel(scale, var_ref, area_ref, own_ref, mate_ref, corner_ref, own_terms, mate_terms, kept_ref, *rest):
    *taken_refs, grad_ref, block_ref, mate_grad = rest
    variables, count = own_ref.shape
    half = block_ref.shape[1]
    third = column(var_ref[...]) * (1 / 3)
    total = jnp.zeros((variables, 128), jnp.float32)
    for at in chunks(count):
        own, mate, corner = (r[:, at].astype(jnp.float32) for r in (own_ref, mate_ref, corner_ref))
        weight = area_ref[:, at] * third
        own = (own_terms[:, at] - weight * smooth_sign(own - corner)).astype(jnp.bfloat16)
        mate = (mate_terms[:, at] - weight * smooth_sign(mate - corner)).astype(jnp.bfloat16)
        grad_ref[:, at] = own
        mate_grad[:, at] = mate
        total = total + (own.astype(jnp.float32) + mate.astype(jnp.float32))
    block = jnp.dot(grad_ref[...], kept_ref[...], preferred_element_type=jnp.float32)
    taken = jnp.concatenate([ref[...] for ref in taken_refs], 0)
    block += jnp.dot(mate_grad[...], taken, preferred_element_type=jnp.float32)
    bias = jnp.sum(total.T, axis=0, keepdims=True)
    bias = jnp.pad(bias, ((0, 0), (0, half - variables)))
    block_ref[:variables] = (block * scale).astype(block_ref.dtype)
    spare = block_ref.shape[0] - variables
    block_ref[variables:] = jnp.broadcast_to(bias * scale, (spare, half)).astype(block_ref.dtype)


def gradient_rows(scale, var_weight, area, own, mate, corner, terms, kept, taken):
    variables, count = own.shape
    half = kept.shape[1]
    rows = -(-(variables + 1) // 8) * 8
    return pl.pallas_call(
        functools.partial(gradient_kernel, scale),
        out_shape=(
            jax.ShapeDtypeStruct((variables, count), jnp.bfloat16),
            jax.ShapeDtypeStruct((rows, half), jnp.bfloat16),
        ),
        in_specs=[VMEM] * (8 + PIECES),
        out_specs=(VMEM, VMEM),
        scratch_shapes=[pltpu.VMEM((variables, count), jnp.bfloat16)],
        compiler_params=pltpu.CompilerParams(vmem_limit_bytes=8 << 20),
        cost_estimate=pl.CostEstimate(
            flops=4 * count * half * rows, bytes_accessed=4 * count * half, transcendentals=2 * variables * count
        ),
        name="gradient_rows",
    )(var_weight, area, own, mate, corner, *terms, kept, *taken)


def tail_kernel(role_ref, here_ref, there_ref, out_ref, bias_ref):
    variables, channels = out_ref.shape
    half = channels // 2
    role = role_ref[0]
    mine, other = halves_of(role, half)
    out_ref[:, mine] = here_ref[:variables].astype(jnp.float32)
    out_ref[:, other] = there_ref[:variables].astype(jnp.float32)
    row = slice(variables, variables + 1)
    bias = jnp.where(role == 0, here_ref[row].astype(jnp.float32), there_ref[row].astype(jnp.float32))
    bias_ref[...] = bias[:, :variables]


def tail(role, here, there, variables):
    return pl.pallas_call(
        tail_kernel,
        out_shape=(
            jax.ShapeDtypeStruct((variables, 2 * here.shape[1]), jnp.float32),
            jax.ShapeDtypeStruct((1, variables), jnp.float32),
        ),
        in_specs=[SMEM, VMEM, VMEM],
        out_specs=(VMEM, VMEM),
        compiler_params=pltpu.CompilerParams(vmem_limit_bytes=4 << 20),
        name="tail",
    )(role, here, there)


def four_members(latent, head_weight, head_bias, targets, var_weight, tile_fill):
    _, local_points, _ = latent.shape
    ens = lax.axis_size("ens")
    index = lax.axis_index("space") * ens + lax.axis_index("ens")
    role = role_of(index, groups_of(lax.axis_size("space") * ens)[1]).astype(jnp.int32)[None]
    scale = 1.0 / math.sqrt(4 * local_points * lax.axis_size("space"))
    area = area_of(local_points, tile_fill)
    own, kept, *given = project_rows(role, in_hbm(latent[0]), in_hbm(head_weight.T), in_hbm(head_bias[None]))
    far = swap(own, lambda i: 2)
    mate = swap(own, lambda i: 1)
    taken = [swap(piece, lambda i: 1) for piece in given]
    corner = swap(far, lambda i: 1)
    rows = (var_weight[None], area[None])
    terms = terms_rows(*rows, own, mate, far, targets)
    grad, block = gradient_rows(scale, *rows, own, mate, corner, terms, kept, taken)
    grad_latent = back(grad[None], head_weight)
    block, grad_latent = butterfly(block, grad_latent)
    there = swap(block, lambda i: 1)
    total, bias = tail(role, block, there, targets.shape[0])
    return grad_latent, total.T, bias[0]


def local(latent, head_weight, head_bias, targets, var_weight, tile_fill):
    space, ens = lax.axis_size("space"), lax.axis_size("ens")
    members, _, channels = latent.shape
    fits = members == 1 and ens == 4 and is_pow2(space)
    fits = fits and channels % 256 == 0 and targets.shape[0] <= 128 and latent.shape[1] % (128 * PIECES) == 0
    plan = four_members if fits else general
    return plan(latent, head_weight, head_bias, targets, var_weight, tile_fill)


def solution(mesh):
    placed = (P("ens", "space", None), P(), P(), P(None, "space"), P(), P("space"))
    return jax.shard_map(
        local,
        mesh=mesh,
        in_specs=placed,
        out_specs=(P("ens", "space", None), P(), P()),
        check_vma=False,
    )
```

```python
import functools
import math

import jax
import jax.numpy as jnp
from jax import lax
from jax.experimental import pallas as pl
from jax.experimental.pallas import tpu as pltpu
from jax.sharding import PartitionSpec as P

TILE_PTS = 128
SMOOTH = 0.05
ALL = ("space", "ens")


def smooth_sign(value):
    return value * lax.rsqrt(value * value + SMOOTH * SMOOTH)


def is_pow2(n):
    return n > 0 and n & (n - 1) == 0


def swap(value, bits_of):
    count = lax.axis_size("space") * lax.axis_size("ens")
    return lax.ppermute(value, ALL, [(i, i ^ bits_of(i)) for i in range(count)])


def round_bf16(value):
    return lax.reduce_precision(value, exponent_bits=8, mantissa_bits=7)


def groups_of(count):
    bits = [1 << k for k in range(1, count.bit_length() - 1)]
    groups = [bits[k : k + 2] for k in range(0, len(bits), 2)]
    return groups, sum(group[-1] for group in groups)


def parity(value):
    return value.bit_count() % 2


def role_of(index, crossed):
    role = index % 2
    bit = 2
    while bit <= crossed:
        if bit & crossed:
            role = (role + index // bit) % 2
        bit *= 2
    return role


def hop_swap(wire, crossed, first, second):
    def bits_of(index):
        bits = second if role_of(index, crossed) else first
        return bits ^ parity(bits & crossed)

    return swap(wire, bits_of)


def butterfly(wire, beside):
    groups, crossed = groups_of(lax.axis_size("space") * lax.axis_size("ens"))
    other = groups[::-1] if len(groups[-1]) == 2 else groups
    for hop, (first, second) in enumerate(zip(groups, other)):
        got = [hop_swap(wire, crossed, first[0], second[0])]
        if len(first) == 2:
            got.append(hop_swap(wire, crossed, first[1], second[1]))
            got.append(hop_swap(wire, crossed, sum(first), sum(second)))
        if hop == 0:
            *got, beside = lax.optimization_barrier((*got, beside))
        got = [value.astype(jnp.float32) for value in got]
        block = wire.astype(jnp.float32) + got[0]
        if len(got) == 3:
            block = block + (got[1] + got[2])
        wire = round_bf16(block).astype(jnp.bfloat16)
    return wire, beside


def area_of(local_points, tile_fill):
    points = local_points * lax.axis_size("space")
    local_index = jnp.arange(local_points, dtype=jnp.int32)
    global_index = lax.axis_index("space") * local_points + local_index
    live = local_index % TILE_PTS < jnp.repeat(tile_fill, TILE_PTS)
    latitude = jnp.pi * ((global_index.astype(jnp.float32) + 0.5) / points - 0.5)
    return jnp.where(live, jnp.cos(latitude), 0.0)


def project(latent, head_weight, head_bias):
    preds = jnp.einsum("mpd,dv->mvp", latent, head_weight, preferred_element_type=jnp.float32)
    return (preds + head_bias[None, :, None]).astype(jnp.bfloat16)


def back(grad_pred, head_weight):
    return jnp.einsum(
        "mvp,dv->mpd", grad_pred, head_weight, preferred_element_type=jnp.float32
    ).astype(jnp.bfloat16)


def general(latent, head_weight, head_bias, targets, var_weight, tile_fill):
    members = latent.shape[0] * lax.axis_size("ens")
    points = latent.shape[1] * lax.axis_size("space")
    preds = project(latent, head_weight, head_bias)
    values = preds.astype(jnp.float32)
    everyone = lax.all_gather(preds, "ens", axis=0, tiled=True)

    def one_member(slot, total):
        other = lax.dynamic_index_in_dim(everyone, slot, 0, keepdims=True).astype(jnp.float32)
        return total + smooth_sign(values - other)

    pair = lax.fori_loop(0, members, one_member, jnp.zeros(values.shape, jnp.float32))
    weight = area_of(latent.shape[1], tile_fill)[None, :] * var_weight[:, None]
    sign = smooth_sign(values - targets.astype(jnp.float32)[None])
    grad_pred = (weight[None] * (sign - pair / (members - 1))).astype(jnp.bfloat16)
    grad_latent = back(grad_pred, head_weight)
    scale = 1.0 / jnp.sqrt(jnp.float32(members) * jnp.float32(points))
    weight_sum = jnp.einsum("mpd,mvp->dv", latent, grad_pred, preferred_element_type=jnp.float32)
    bias_sum = jnp.sum(grad_pred.astype(jnp.float32), axis=(0, 2))
    weight_total, bias_total = lax.psum((weight_sum * scale, bias_sum * scale), ALL)
    return grad_latent, weight_total, bias_total


VMEM = pl.BlockSpec(memory_space=pltpu.VMEM)
SMEM = pl.BlockSpec(memory_space=pltpu.SMEM)
HBM = pl.BlockSpec(memory_space=pltpu.HBM)
LAST = (((1,), (1,)), ((), ()))
HALVES = 2
PIECES = 1
in_hbm = functools.partial(pltpu.with_memory_space_constraint, memory_space=pltpu.HBM)
in_hbm = functools.partial(pltpu.with_memory_space_constraint, memory_space=pltpu.HBM)


def halves_of(role, half):
    return [pl.ds(pl.multiple_of(r * half, 128), half) for r in (role, 1 - role)]


def project_kernel(start, role_ref, latent_hbm, weight_hbm, bias_hbm, preds_ref, kept_ref, *rest):
    *given_refs, weight, bias, sems = rest
    mine, other = halves_of(role_ref[0], kept_ref.shape[1])
    count = kept_ref.shape[0]
    step = given_refs[0].shape[0]
    pairs = [(weight_hbm, weight), (bias_hbm, bias), (latent_hbm.at[pl.ds(start, count), mine], kept_ref)]
    pairs += [(latent_hbm.at[pl.ds(start + k * step, step), other], ref) for k, ref in enumerate(given_refs)]
    copies = [pltpu.make_async_copy(source, target, sems.at[k]) for k, (source, target) in enumerate(pairs)]
    for copy in copies:
        copy.start()
    for copy in copies[:3]:
        copy.wait()
    total = column(bias[...])[:, :1]
    total = total + lax.dot_general(weight[:, mine], kept_ref[...], LAST, preferred_element_type=jnp.float32)
    for copy in copies[3:]:
        copy.wait()
    given = jnp.concatenate([ref[...] for ref in given_refs], 0)
    total = total + lax.dot_general(weight[:, other], given, LAST, preferred_element_type=jnp.float32)
    preds_ref[...] = total.astype(preds_ref.dtype)


def project_rows(role, latent, weight, bias, start, count):
    variables, channels = weight.shape
    part = jax.ShapeDtypeStruct((count, channels // 2), jnp.bfloat16)
    piece = jax.ShapeDtypeStruct((count // PIECES, channels // 2), jnp.bfloat16)
    return pl.pallas_call(
        functools.partial(project_kernel, start),
        out_shape=[jax.ShapeDtypeStruct((variables, count), jnp.bfloat16), part] + [piece] * PIECES,
        in_specs=[SMEM, HBM, HBM, HBM],
        out_specs=[VMEM] * (2 + PIECES),
        scratch_shapes=[
            pltpu.VMEM((variables, channels), jnp.bfloat16),
            pltpu.VMEM((1, variables), jnp.float32),
            pltpu.SemaphoreType.DMA((3 + PIECES,)),
        ],
        compiler_params=pltpu.CompilerParams(vmem_limit_bytes=8 << 20),
        cost_estimate=pl.CostEstimate(
            flops=2 * count * channels * variables,
            bytes_accessed=2 * channels * (count + variables),
            transcendentals=0,
        ),
        name="project_rows",
    )(role, latent, weight, bias)


def chunks(count):
    return [slice(k, k + 128) for k in range(0, count, 128)]


def column(row):
    return jnp.broadcast_to(row, (128, row.shape[1])).T


def terms_kernel(start, var_ref, area_ref, own_ref, mate_ref, far_ref, seen_ref, own_terms, mate_terms):
    var_weight = column(var_ref[...])
    for at in chunks(own_ref.shape[1]):
        own, mate, far = (r[:, at].astype(jnp.float32) for r in (own_ref, mate_ref, far_ref))
        there = slice(start + at.start, start + at.stop)
        seen = seen_ref[:, there].astype(jnp.float32)
        weight = area_ref[:, there] * var_weight
        inside = smooth_sign(own - mate)
        own_terms[:, at] = weight * (smooth_sign(own - seen) - (smooth_sign(own - far) + inside) * (1 / 3))
        mate_terms[:, at] = weight * (smooth_sign(mate - seen) - (smooth_sign(mate - far) - inside) * (1 / 3))


def terms_rows(start, var_weight, area, own, mate, far, seen):
    part = jax.ShapeDtypeStruct(own.shape, jnp.float32)
    return pl.pallas_call(
        functools.partial(terms_kernel, start),
        out_shape=(part, part),
        in_specs=[VMEM] * 6,
        out_specs=(VMEM, VMEM),
        compiler_params=pltpu.CompilerParams(vmem_limit_bytes=8 << 20),
        cost_estimate=pl.CostEstimate(flops=40 * own.size, bytes_accessed=16 * own.size, transcendentals=5 * own.size),
        name="terms_rows",
    )(var_weight, area, own, mate, far, seen)


def gradient_kernel(scale, parts, var_ref, area_ref, *rest):
    *refs, grad_ref, block_ref, mate_grad = rest
    variables = grad_ref.shape[0]
    half = block_ref.shape[1]
    third = column(var_ref[...]) * (1 / 3)
    total = jnp.zeros((variables, 128), jnp.float32)
    start = 0
    kept, taken = [], []
    size = len(refs) // parts
    for k in range(parts):
        own_ref, mate_ref, corner_ref, own_terms, mate_terms, kept_ref, *taken_refs = refs[k * size : (k + 1) * size]
        for at in chunks(own_ref.shape[1]):
            own, mate, corner = (r[:, at].astype(jnp.float32) for r in (own_ref, mate_ref, corner_ref))
            there = slice(start + at.start, start + at.stop)
            weight = area_ref[:, there] * third
            own = (own_terms[:, at] - weight * smooth_sign(own - corner)).astype(jnp.bfloat16)
            mate = (mate_terms[:, at] - weight * smooth_sign(mate - corner)).astype(jnp.bfloat16)
            grad_ref[:, there] = own
            mate_grad[:, there] = mate
            total = total + (own.astype(jnp.float32) + mate.astype(jnp.float32))
        start += own_ref.shape[1]
        kept.append(kept_ref[...])
        taken += [ref[...] for ref in taken_refs]
    block = jnp.dot(grad_ref[...], jnp.concatenate(kept, 0), preferred_element_type=jnp.float32)
    block += jnp.dot(mate_grad[...], jnp.concatenate(taken, 0), preferred_element_type=jnp.float32)
    bias = jnp.sum(total.T, axis=0, keepdims=True)
    bias = jnp.pad(bias, ((0, 0), (0, half - variables)))
    block_ref[:variables] = (block * scale).astype(block_ref.dtype)
    spare = block_ref.shape[0] - variables
    block_ref[variables:] = jnp.broadcast_to(bias * scale, (spare, half)).astype(block_ref.dtype)


def gradient_rows(scale, var_weight, area, parts):
    variables = parts[0][0].shape[0]
    count = area.shape[1]
    half = parts[0][5].shape[1]
    rows = -(-(variables + 1) // 8) * 8
    operands = [value for part in parts for value in part]
    return pl.pallas_call(
        functools.partial(gradient_kernel, scale, len(parts)),
        out_shape=(
            jax.ShapeDtypeStruct((variables, count), jnp.bfloat16),
            jax.ShapeDtypeStruct((rows, half), jnp.bfloat16),
        ),
        in_specs=[VMEM] * (2 + len(operands)),
        out_specs=(VMEM, VMEM),
        scratch_shapes=[pltpu.VMEM((variables, count), jnp.bfloat16)],
        compiler_params=pltpu.CompilerParams(vmem_limit_bytes=8 << 20),
        cost_estimate=pl.CostEstimate(
            flops=4 * count * half * rows, bytes_accessed=4 * count * half, transcendentals=2 * variables * count
        ),
        name="gradient_rows",
    )(var_weight, area, *operands)


def tail_kernel(role_ref, here_ref, there_ref, out_ref, bias_ref):
    variables, channels = out_ref.shape
    half = channels // 2
    role = role_ref[0]
    mine, other = halves_of(role, half)
    out_ref[:, mine] = here_ref[:variables].astype(jnp.float32)
    out_ref[:, other] = there_ref[:variables].astype(jnp.float32)
    row = slice(variables, variables + 1)
    bias = jnp.where(role == 0, here_ref[row].astype(jnp.float32), there_ref[row].astype(jnp.float32))
    bias_ref[...] = bias[:, :variables]


def tail(role, here, there, variables):
    return pl.pallas_call(
        tail_kernel,
        out_shape=(
            jax.ShapeDtypeStruct((variables, 2 * here.shape[1]), jnp.float32),
            jax.ShapeDtypeStruct((1, variables), jnp.float32),
        ),
        in_specs=[SMEM, VMEM, VMEM],
        out_specs=(VMEM, VMEM),
        compiler_params=pltpu.CompilerParams(vmem_limit_bytes=4 << 20),
        name="tail",
    )(role, here, there)


def four_members(latent, head_weight, head_bias, targets, var_weight, tile_fill):
    _, local_points, _ = latent.shape
    ens = lax.axis_size("ens")
    index = lax.axis_index("space") * ens + lax.axis_index("ens")
    role = role_of(index, groups_of(lax.axis_size("space") * ens)[1]).astype(jnp.int32)[None]
    scale = 1.0 / math.sqrt(4 * local_points * lax.axis_size("space"))
    area = area_of(local_points, tile_fill)
    source = (in_hbm(latent[0]), in_hbm(head_weight.T), in_hbm(head_bias[None]))
    starts = [k * local_points // HALVES for k in range(HALVES)]
    projected = [project_rows(role, *source, start, local_points // HALVES) for start in starts]
    far = [swap(part[0], lambda i: 2) for part in projected]
    projected = lax.optimization_barrier(projected)
    rows = (var_weight[None], area[None])
    parts = []
    for start, (own, kept, *given), across in zip(starts, projected, far):
        mate = swap(own, lambda i: 1)
        taken = [swap(piece, lambda i: 1) for piece in given]
        corner = swap(across, lambda i: 1)
        terms = terms_rows(start, *rows, own, mate, across, targets)
        parts.append((own, mate, corner, *terms, kept, *taken))
    grad, block = gradient_rows(scale, *rows, parts)
    grad_latent = back(grad[None], head_weight)
    block, grad_latent = butterfly(block, grad_latent)
    there = swap(block, lambda i: 1)
    total, bias = tail(role, block, there, targets.shape[0])
    return grad_latent, total.T, bias[0]


def local(latent, head_weight, head_bias, targets, var_weight, tile_fill):
    space, ens = lax.axis_size("space"), lax.axis_size("ens")
    members, _, channels = latent.shape
    fits = members == 1 and ens == 4 and is_pow2(space)
    fits = fits and channels % 256 == 0 and targets.shape[0] <= 128 and latent.shape[1] % (128 * HALVES * PIECES) == 0
    plan = four_members if fits else general
    return plan(latent, head_weight, head_bias, targets, var_weight, tile_fill)


def solution(mesh):
    placed = (P("ens", "space", None), P(), P(), P(None, "space"), P(), P("space"))
    return jax.shard_map(
        local,
        mesh=mesh,
        in_specs=placed,
        out_specs=(P("ens", "space", None), P(), P()),
        check_vma=False,
    )
```

```python
import functools
import math

import jax
import jax.numpy as jnp
from jax import lax
from jax.experimental import pallas as pl
from jax.experimental.pallas import tpu as pltpu
from jax.sharding import PartitionSpec as P

TILE_PTS = 128
SMOOTH = 0.05
ALL = ("space", "ens")


def smooth_sign(value):
    return value * lax.rsqrt(value * value + SMOOTH * SMOOTH)


def is_pow2(n):
    return n > 0 and n & (n - 1) == 0


def swap(value, bits_of):
    count = lax.axis_size("space") * lax.axis_size("ens")
    return lax.ppermute(value, ALL, [(i, i ^ bits_of(i)) for i in range(count)])


def round_bf16(value):
    return lax.reduce_precision(value, exponent_bits=8, mantissa_bits=7)


def groups_of(count):
    bits = [1 << k for k in range(1, count.bit_length() - 1)]
    groups = [bits[k : k + 2] for k in range(0, len(bits), 2)]
    return groups, sum(group[-1] for group in groups)


def parity(value):
    return value.bit_count() % 2


def role_of(index, crossed):
    role = index % 2
    bit = 2
    while bit <= crossed:
        if bit & crossed:
            role = (role + index // bit) % 2
        bit *= 2
    return role


def hop_swap(wire, crossed, first, second):
    def bits_of(index):
        bits = second if role_of(index, crossed) else first
        return bits ^ parity(bits & crossed)

    return swap(wire, bits_of)


def butterfly(wire, beside):
    groups, crossed = groups_of(lax.axis_size("space") * lax.axis_size("ens"))
    other = groups[::-1] if len(groups[-1]) == 2 else groups
    for hop, (first, second) in enumerate(zip(groups, other)):
        got = [hop_swap(wire, crossed, first[0], second[0])]
        if len(first) == 2:
            got.append(hop_swap(wire, crossed, first[1], second[1]))
            got.append(hop_swap(wire, crossed, sum(first), sum(second)))
        if hop == 0:
            *got, beside = lax.optimization_barrier((*got, beside))
        got = [value.astype(jnp.float32) for value in got]
        block = wire.astype(jnp.float32) + got[0]
        if len(got) == 3:
            block = block + (got[1] + got[2])
        wire = round_bf16(block).astype(jnp.bfloat16)
    return wire, beside


def area_of(local_points, tile_fill):
    points = local_points * lax.axis_size("space")
    local_index = jnp.arange(local_points, dtype=jnp.int32)
    global_index = lax.axis_index("space") * local_points + local_index
    live = local_index % TILE_PTS < jnp.repeat(tile_fill, TILE_PTS)
    latitude = jnp.pi * ((global_index.astype(jnp.float32) + 0.5) / points - 0.5)
    return jnp.where(live, jnp.cos(latitude), 0.0)


def project(latent, head_weight, head_bias):
    preds = jnp.einsum("mpd,dv->mvp", latent, head_weight, preferred_element_type=jnp.float32)
    return (preds + head_bias[None, :, None]).astype(jnp.bfloat16)


def back(grad_pred, head_weight):
    return jnp.einsum(
        "mvp,dv->mpd", grad_pred, head_weight, preferred_element_type=jnp.float32
    ).astype(jnp.bfloat16)


def general(latent, head_weight, head_bias, targets, var_weight, tile_fill):
    members = latent.shape[0] * lax.axis_size("ens")
    points = latent.shape[1] * lax.axis_size("space")
    preds = project(latent, head_weight, head_bias)
    values = preds.astype(jnp.float32)
    everyone = lax.all_gather(preds, "ens", axis=0, tiled=True)

    def one_member(slot, total):
        other = lax.dynamic_index_in_dim(everyone, slot, 0, keepdims=True).astype(jnp.float32)
        return total + smooth_sign(values - other)

    pair = lax.fori_loop(0, members, one_member, jnp.zeros(values.shape, jnp.float32))
    weight = area_of(latent.shape[1], tile_fill)[None, :] * var_weight[:, None]
    sign = smooth_sign(values - targets.astype(jnp.float32)[None])
    grad_pred = (weight[None] * (sign - pair / (members - 1))).astype(jnp.bfloat16)
    grad_latent = back(grad_pred, head_weight)
    scale = 1.0 / jnp.sqrt(jnp.float32(members) * jnp.float32(points))
    weight_sum = jnp.einsum("mpd,mvp->dv", latent, grad_pred, preferred_element_type=jnp.float32)
    bias_sum = jnp.sum(grad_pred.astype(jnp.float32), axis=(0, 2))
    weight_total, bias_total = lax.psum((weight_sum * scale, bias_sum * scale), ALL)
    return grad_latent, weight_total, bias_total


VMEM = pl.BlockSpec(memory_space=pltpu.VMEM)
SMEM = pl.BlockSpec(memory_space=pltpu.SMEM)
HBM = pl.BlockSpec(memory_space=pltpu.HBM)
LAST = (((1,), (1,)), ((), ()))
HALVES = 1
PIECES = 3
in_hbm = functools.partial(pltpu.with_memory_space_constraint, memory_space=pltpu.HBM)
in_hbm = functools.partial(pltpu.with_memory_space_constraint, memory_space=pltpu.HBM)


def halves_of(role, half):
    return [pl.ds(pl.multiple_of(r * half, 128), half) for r in (role, 1 - role)]


def project_kernel(start, role_ref, latent_hbm, weight_hbm, bias_hbm, preds_ref, kept_ref, *rest):
    *given_refs, weight, bias, sems = rest
    mine, other = halves_of(role_ref[0], kept_ref.shape[1])
    count = kept_ref.shape[0]
    step = given_refs[0].shape[0]
    pairs = [(weight_hbm, weight), (bias_hbm, bias), (latent_hbm.at[pl.ds(start, count), mine], kept_ref)]
    pairs += [(latent_hbm.at[pl.ds(start + k * step, step), other], ref) for k, ref in enumerate(given_refs)]
    copies = [pltpu.make_async_copy(source, target, sems.at[k]) for k, (source, target) in enumerate(pairs)]
    for copy in copies:
        copy.start()
    for copy in copies[:3]:
        copy.wait()
    total = column(bias[...])[:, :1]
    total = total + lax.dot_general(weight[:, mine], kept_ref[...], LAST, preferred_element_type=jnp.float32)
    for copy in copies[3:]:
        copy.wait()
    given = jnp.concatenate([ref[...] for ref in given_refs], 0)
    total = total + lax.dot_general(weight[:, other], given, LAST, preferred_element_type=jnp.float32)
    preds_ref[...] = total.astype(preds_ref.dtype)


def project_rows(role, latent, weight, bias, start, count):
    variables, channels = weight.shape
    part = jax.ShapeDtypeStruct((count, channels // 2), jnp.bfloat16)
    piece = jax.ShapeDtypeStruct((count // PIECES, channels // 2), jnp.bfloat16)
    return pl.pallas_call(
        functools.partial(project_kernel, start),
        out_shape=[jax.ShapeDtypeStruct((variables, count), jnp.bfloat16), part] + [piece] * PIECES,
        in_specs=[SMEM, HBM, HBM, HBM],
        out_specs=[VMEM] * (2 + PIECES),
        scratch_shapes=[
            pltpu.VMEM((variables, channels), jnp.bfloat16),
            pltpu.VMEM((1, variables), jnp.float32),
            pltpu.SemaphoreType.DMA((3 + PIECES,)),
        ],
        compiler_params=pltpu.CompilerParams(vmem_limit_bytes=8 << 20),
        cost_estimate=pl.CostEstimate(
            flops=2 * count * channels * variables,
            bytes_accessed=2 * channels * (count + variables),
            transcendentals=0,
        ),
        name="project_rows",
    )(role, latent, weight, bias)


def chunks(count):
    return [slice(k, k + 128) for k in range(0, count, 128)]


def column(row):
    return jnp.broadcast_to(row, (128, row.shape[1])).T


def terms_kernel(start, var_ref, area_ref, own_ref, mate_ref, far_ref, seen_ref, own_terms, mate_terms):
    var_weight = column(var_ref[...])
    for at in chunks(own_ref.shape[1]):
        own, mate, far = (r[:, at].astype(jnp.float32) for r in (own_ref, mate_ref, far_ref))
        there = slice(start + at.start, start + at.stop)
        seen = seen_ref[:, there].astype(jnp.float32)
        weight = area_ref[:, there] * var_weight
        inside = smooth_sign(own - mate)
        own_terms[:, at] = weight * (smooth_sign(own - seen) - (smooth_sign(own - far) + inside) * (1 / 3))
        mate_terms[:, at] = weight * (smooth_sign(mate - seen) - (smooth_sign(mate - far) - inside) * (1 / 3))


def terms_rows(start, var_weight, area, own, mate, far, seen):
    part = jax.ShapeDtypeStruct(own.shape, jnp.float32)
    return pl.pallas_call(
        functools.partial(terms_kernel, start),
        out_shape=(part, part),
        in_specs=[VMEM] * 6,
        out_specs=(VMEM, VMEM),
        compiler_params=pltpu.CompilerParams(vmem_limit_bytes=8 << 20),
        cost_estimate=pl.CostEstimate(flops=40 * own.size, bytes_accessed=16 * own.size, transcendentals=5 * own.size),
        name="terms_rows",
    )(var_weight, area, own, mate, far, seen)


def gradient_kernel(scale, parts, var_ref, area_ref, *rest):
    *refs, grad_ref, block_ref, mate_grad = rest
    variables = grad_ref.shape[0]
    half = block_ref.shape[1]
    third = column(var_ref[...]) * (1 / 3)
    total = jnp.zeros((variables, 128), jnp.float32)
    start = 0
    kept, taken = [], []
    size = len(refs) // parts
    for k in range(parts):
        own_ref, mate_ref, corner_ref, own_terms, mate_terms, kept_ref, *taken_refs = refs[k * size : (k + 1) * size]
        for at in chunks(own_ref.shape[1]):
            own, mate, corner = (r[:, at].astype(jnp.float32) for r in (own_ref, mate_ref, corner_ref))
            there = slice(start + at.start, start + at.stop)
            weight = area_ref[:, there] * third
            own = (own_terms[:, at] - weight * smooth_sign(own - corner)).astype(jnp.bfloat16)
            mate = (mate_terms[:, at] - weight * smooth_sign(mate - corner)).astype(jnp.bfloat16)
            grad_ref[:, there] = own
            mate_grad[:, there] = mate
            total = total + (own.astype(jnp.float32) + mate.astype(jnp.float32))
        start += own_ref.shape[1]
        kept.append(kept_ref[...])
        taken += [ref[...] for ref in taken_refs]
    block = jnp.dot(grad_ref[...], jnp.concatenate(kept, 0), preferred_element_type=jnp.float32)
    block += jnp.dot(mate_grad[...], jnp.concatenate(taken, 0), preferred_element_type=jnp.float32)
    bias = jnp.sum(total.T, axis=0, keepdims=True)
    bias = jnp.pad(bias, ((0, 0), (0, half - variables)))
    block_ref[:variables] = (block * scale).astype(block_ref.dtype)
    spare = block_ref.shape[0] - variables
    block_ref[variables:] = jnp.broadcast_to(bias * scale, (spare, half)).astype(block_ref.dtype)


def gradient_rows(scale, var_weight, area, parts):
    variables = parts[0][0].shape[0]
    count = area.shape[1]
    half = parts[0][5].shape[1]
    rows = -(-(variables + 1) // 8) * 8
    operands = [value for part in parts for value in part]
    return pl.pallas_call(
        functools.partial(gradient_kernel, scale, len(parts)),
        out_shape=(
            jax.ShapeDtypeStruct((variables, count), jnp.bfloat16),
            jax.ShapeDtypeStruct((rows, half), jnp.bfloat16),
        ),
        in_specs=[VMEM] * (2 + len(operands)),
        out_specs=(VMEM, VMEM),
        scratch_shapes=[pltpu.VMEM((variables, count), jnp.bfloat16)],
        compiler_params=pltpu.CompilerParams(vmem_limit_bytes=8 << 20),
        cost_estimate=pl.CostEstimate(
            flops=4 * count * half * rows, bytes_accessed=4 * count * half, transcendentals=2 * variables * count
        ),
        name="gradient_rows",
    )(var_weight, area, *operands)


def write_half(lanes, block_ref, out_hbm, half_ref, sem):
    half_ref[...] = block_ref[: half_ref.shape[0]].astype(jnp.float32)
    copy = pltpu.make_async_copy(half_ref, out_hbm.at[:, lanes], sem)
    copy.start()
    return copy


def own_half_kernel(role_ref, here_ref, out_hbm, half_ref, sem):
    mine, _ = halves_of(role_ref[0], here_ref.shape[1])
    write_half(mine, here_ref, out_hbm, half_ref, sem).wait()


def other_half_kernel(role_ref, here_ref, there_ref, _, out_hbm, bias_ref, half_ref, sem):
    role = role_ref[0]
    _, other = halves_of(role, there_ref.shape[1])
    copy = write_half(other, there_ref, out_hbm, half_ref, sem)
    variables = half_ref.shape[0]
    row = slice(variables, variables + 1)
    bias = jnp.where(role == 0, here_ref[row].astype(jnp.float32), there_ref[row].astype(jnp.float32))
    bias_ref[...] = bias[:, :variables]
    copy.wait()


def tail(role, here, there, variables):
    half = here.shape[1]
    whole = jax.ShapeDtypeStruct((variables, 2 * half), jnp.float32)
    scratch = [pltpu.VMEM((variables, half), jnp.float32), pltpu.SemaphoreType.DMA]
    params = pltpu.CompilerParams(vmem_limit_bytes=4 << 20)
    begun = pl.pallas_call(
        own_half_kernel,
        out_shape=whole,
        in_specs=[SMEM, VMEM],
        out_specs=HBM,
        scratch_shapes=scratch,
        compiler_params=params,
        cost_estimate=pl.CostEstimate(flops=0, bytes_accessed=6 * here.size, transcendentals=0),
        name="own_half",
    )(role, here)
    return pl.pallas_call(
        other_half_kernel,
        out_shape=(whole, jax.ShapeDtypeStruct((1, variables), jnp.float32)),
        in_specs=[SMEM, VMEM, VMEM, HBM],
        out_specs=(HBM, VMEM),
        scratch_shapes=scratch,
        input_output_aliases={3: 0},
        compiler_params=params,
        cost_estimate=pl.CostEstimate(flops=0, bytes_accessed=6 * here.size, transcendentals=0),
        name="other_half",
    )(role, here, there, begun)


def four_members(latent, head_weight, head_bias, targets, var_weight, tile_fill):
    _, local_points, _ = latent.shape
    ens = lax.axis_size("ens")
    index = lax.axis_index("space") * ens + lax.axis_index("ens")
    role = role_of(index, groups_of(lax.axis_size("space") * ens)[1]).astype(jnp.int32)[None]
    scale = 1.0 / math.sqrt(4 * local_points * lax.axis_size("space"))
    area = area_of(local_points, tile_fill)
    source = (in_hbm(latent[0]), in_hbm(head_weight.T), in_hbm(head_bias[None]))
    starts = [k * local_points // HALVES for k in range(HALVES)]
    projected = [project_rows(role, *source, start, local_points // HALVES) for start in starts]
    far = [swap(part[0], lambda i: 2) for part in projected]
    projected = lax.optimization_barrier(projected)
    rows = (var_weight[None], area[None])
    parts = []
    for start, (own, kept, *given), across in zip(starts, projected, far):
        mate = swap(own, lambda i: 1)
        taken = [swap(piece, lambda i: 1) for piece in given]
        corner = swap(across, lambda i: 1)
        terms = terms_rows(start, *rows, own, mate, across, targets)
        parts.append((own, mate, corner, *terms, kept, *taken))
    grad, block = gradient_rows(scale, *rows, parts)
    grad_latent = back(grad[None], head_weight)
    block, grad_latent = butterfly(block, grad_latent)
    there = swap(block, lambda i: 1)
    total, bias = tail(role, block, there, targets.shape[0])
    return grad_latent, total.T, bias[0]


def local(latent, head_weight, head_bias, targets, var_weight, tile_fill):
    space, ens = lax.axis_size("space"), lax.axis_size("ens")
    members, _, channels = latent.shape
    fits = members == 1 and ens == 4 and is_pow2(space)
    fits = fits and channels % 256 == 0 and targets.shape[0] <= 128 and latent.shape[1] % (128 * HALVES * PIECES) == 0
    plan = four_members if fits else general
    return plan(latent, head_weight, head_bias, targets, var_weight, tile_fill)


def solution(mesh):
    placed = (P("ens", "space", None), P(), P(), P(None, "space"), P(), P("space"))
    return jax.shard_map(
        local,
        mesh=mesh,
        in_specs=placed,
        out_specs=(P("ens", "space", None), P(), P()),
        check_vma=False,
    )
```

```python
import functools
import math

import jax
import jax.numpy as jnp
from jax import lax
from jax.experimental import pallas as pl
from jax.experimental.pallas import tpu as pltpu
from jax.sharding import PartitionSpec as P

TILE_PTS = 128
SMOOTH = 0.05
ALL = ("space", "ens")


def smooth_sign(value):
    return value * lax.rsqrt(value * value + SMOOTH * SMOOTH)


def is_pow2(n):
    return n > 0 and n & (n - 1) == 0


def swap(value, bits_of):
    count = lax.axis_size("space") * lax.axis_size("ens")
    return lax.ppermute(value, ALL, [(i, i ^ bits_of(i)) for i in range(count)])


def round_bf16(value):
    return lax.reduce_precision(value, exponent_bits=8, mantissa_bits=7)


def groups_of(count):
    bits = [1 << k for k in range(1, count.bit_length() - 1)]
    groups = [bits[k : k + 2] for k in range(0, len(bits), 2)]
    return groups, sum(group[-1] for group in groups)


def parity(value):
    return value.bit_count() % 2


def role_of(index, crossed):
    role = index % 2
    bit = 2
    while bit <= crossed:
        if bit & crossed:
            role = (role + index // bit) % 2
        bit *= 2
    return role


def hop_swap(wire, crossed, first, second):
    def bits_of(index):
        bits = second if role_of(index, crossed) else first
        return bits ^ parity(bits & crossed)

    return swap(wire, bits_of)


def butterfly(wire, beside):
    groups, crossed = groups_of(lax.axis_size("space") * lax.axis_size("ens"))
    other = groups[::-1] if len(groups[-1]) == 2 else groups
    for hop, (first, second) in enumerate(zip(groups, other)):
        got = [hop_swap(wire, crossed, first[0], second[0])]
        if len(first) == 2:
            got.append(hop_swap(wire, crossed, first[1], second[1]))
            got.append(hop_swap(wire, crossed, sum(first), sum(second)))
        if hop == 0:
            *got, beside = lax.optimization_barrier((*got, beside))
        got = [value.astype(jnp.float32) for value in got]
        block = wire.astype(jnp.float32) + got[0]
        if len(got) == 3:
            block = block + (got[1] + got[2])
        wire = round_bf16(block).astype(jnp.bfloat16)
    return wire, beside


def area_of(local_points, tile_fill):
    points = local_points * lax.axis_size("space")
    local_index = jnp.arange(local_points, dtype=jnp.int32)
    global_index = lax.axis_index("space") * local_points + local_index
    live = local_index % TILE_PTS < jnp.repeat(tile_fill, TILE_PTS)
    latitude = jnp.pi * ((global_index.astype(jnp.float32) + 0.5) / points - 0.5)
    return jnp.where(live, jnp.cos(latitude), 0.0)


def project(latent, head_weight, head_bias):
    preds = jnp.einsum("mpd,dv->mvp", latent, head_weight, preferred_element_type=jnp.float32)
    return (preds + head_bias[None, :, None]).astype(jnp.bfloat16)


def back(grad_pred, head_weight):
    return jnp.einsum(
        "mvp,dv->mpd", grad_pred, head_weight, preferred_element_type=jnp.float32
    ).astype(jnp.bfloat16)


def general(latent, head_weight, head_bias, targets, var_weight, tile_fill):
    members = latent.shape[0] * lax.axis_size("ens")
    points = latent.shape[1] * lax.axis_size("space")
    preds = project(latent, head_weight, head_bias)
    values = preds.astype(jnp.float32)
    everyone = lax.all_gather(preds, "ens", axis=0, tiled=True)

    def one_member(slot, total):
        other = lax.dynamic_index_in_dim(everyone, slot, 0, keepdims=True).astype(jnp.float32)
        return total + smooth_sign(values - other)

    pair = lax.fori_loop(0, members, one_member, jnp.zeros(values.shape, jnp.float32))
    weight = area_of(latent.shape[1], tile_fill)[None, :] * var_weight[:, None]
    sign = smooth_sign(values - targets.astype(jnp.float32)[None])
    grad_pred = (weight[None] * (sign - pair / (members - 1))).astype(jnp.bfloat16)
    grad_latent = back(grad_pred, head_weight)
    scale = 1.0 / jnp.sqrt(jnp.float32(members) * jnp.float32(points))
    weight_sum = jnp.einsum("mpd,mvp->dv", latent, grad_pred, preferred_element_type=jnp.float32)
    bias_sum = jnp.sum(grad_pred.astype(jnp.float32), axis=(0, 2))
    weight_total, bias_total = lax.psum((weight_sum * scale, bias_sum * scale), ALL)
    return grad_latent, weight_total, bias_total


VMEM = pl.BlockSpec(memory_space=pltpu.VMEM)
SMEM = pl.BlockSpec(memory_space=pltpu.SMEM)
HBM = pl.BlockSpec(memory_space=pltpu.HBM)
LAST = (((1,), (1,)), ((), ()))
HALVES = 1
PIECES = 3
in_hbm = functools.partial(pltpu.with_memory_space_constraint, memory_space=pltpu.HBM)
in_hbm = functools.partial(pltpu.with_memory_space_constraint, memory_space=pltpu.HBM)


def halves_of(role, half):
    return [pl.ds(pl.multiple_of(r * half, 128), half) for r in (role, 1 - role)]


def project_kernel(start, role_ref, latent_hbm, weight_hbm, bias_hbm, preds_ref, kept_ref, *rest):
    *given_refs, weight, bias, sems = rest
    mine, other = halves_of(role_ref[0], kept_ref.shape[1])
    count = kept_ref.shape[0]
    step = given_refs[0].shape[0]
    pairs = [(weight_hbm, weight), (bias_hbm, bias), (latent_hbm.at[pl.ds(start, count), mine], kept_ref)]
    pairs += [(latent_hbm.at[pl.ds(start + k * step, step), other], ref) for k, ref in enumerate(given_refs)]
    copies = [pltpu.make_async_copy(source, target, sems.at[k]) for k, (source, target) in enumerate(pairs)]
    for copy in copies:
        copy.start()
    for copy in copies[:3]:
        copy.wait()
    total = column(bias[...])[:, :1]
    total = total + lax.dot_general(weight[:, mine], kept_ref[...], LAST, preferred_element_type=jnp.float32)
    for copy in copies[3:]:
        copy.wait()
    given = jnp.concatenate([ref[...] for ref in given_refs], 0)
    total = total + lax.dot_general(weight[:, other], given, LAST, preferred_element_type=jnp.float32)
    preds_ref[...] = total.astype(preds_ref.dtype)


def project_rows(role, latent, weight, bias, start, count):
    variables, channels = weight.shape
    part = jax.ShapeDtypeStruct((count, channels // 2), jnp.bfloat16)
    piece = jax.ShapeDtypeStruct((count // PIECES, channels // 2), jnp.bfloat16)
    return pl.pallas_call(
        functools.partial(project_kernel, start),
        out_shape=[jax.ShapeDtypeStruct((variables, count), jnp.bfloat16), part] + [piece] * PIECES,
        in_specs=[SMEM, HBM, HBM, HBM],
        out_specs=[VMEM] * (2 + PIECES),
        scratch_shapes=[
            pltpu.VMEM((variables, channels), jnp.bfloat16),
            pltpu.VMEM((1, variables), jnp.float32),
            pltpu.SemaphoreType.DMA((3 + PIECES,)),
        ],
        compiler_params=pltpu.CompilerParams(vmem_limit_bytes=8 << 20),
        cost_estimate=pl.CostEstimate(
            flops=2 * count * channels * variables,
            bytes_accessed=2 * channels * (count + variables),
            transcendentals=0,
        ),
        name="project_rows",
    )(role, latent, weight, bias)


def chunks(count):
    return [slice(k, k + 128) for k in range(0, count, 128)]


def column(row):
    return jnp.broadcast_to(row, (128, row.shape[1])).T


def terms_kernel(start, var_ref, area_ref, own_ref, mate_ref, far_ref, seen_ref, own_terms, mate_terms):
    var_weight = column(var_ref[...])
    for at in chunks(own_ref.shape[1]):
        own, mate, far = (r[:, at].astype(jnp.float32) for r in (own_ref, mate_ref, far_ref))
        there = slice(start + at.start, start + at.stop)
        seen = seen_ref[:, there].astype(jnp.float32)
        weight = area_ref[:, there] * var_weight
        inside = smooth_sign(own - mate)
        own_terms[:, at] = weight * (smooth_sign(own - seen) - (smooth_sign(own - far) + inside) * (1 / 3))
        mate_terms[:, at] = weight * (smooth_sign(mate - seen) - (smooth_sign(mate - far) - inside) * (1 / 3))


def terms_rows(start, var_weight, area, own, mate, far, seen):
    part = jax.ShapeDtypeStruct(own.shape, jnp.float32)
    return pl.pallas_call(
        functools.partial(terms_kernel, start),
        out_shape=(part, part),
        in_specs=[VMEM] * 6,
        out_specs=(VMEM, VMEM),
        compiler_params=pltpu.CompilerParams(vmem_limit_bytes=8 << 20),
        cost_estimate=pl.CostEstimate(flops=40 * own.size, bytes_accessed=16 * own.size, transcendentals=5 * own.size),
        name="terms_rows",
    )(var_weight, area, own, mate, far, seen)


def gradient_kernel(scale, parts, var_ref, area_ref, *rest):
    *refs, grad_ref, block_ref, mate_grad = rest
    variables = grad_ref.shape[0]
    half = block_ref.shape[1]
    third = column(var_ref[...]) * (1 / 3)
    total = jnp.zeros((variables, 128), jnp.float32)
    start = 0
    kept, taken = [], []
    size = len(refs) // parts
    for k in range(parts):
        own_ref, mate_ref, corner_ref, own_terms, mate_terms, kept_ref, *taken_refs = refs[k * size : (k + 1) * size]
        for at in chunks(own_ref.shape[1]):
            own, mate, corner = (r[:, at].astype(jnp.float32) for r in (own_ref, mate_ref, corner_ref))
            there = slice(start + at.start, start + at.stop)
            weight = area_ref[:, there] * third
            own = (own_terms[:, at] - weight * smooth_sign(own - corner)).astype(jnp.bfloat16)
            mate = (mate_terms[:, at] - weight * smooth_sign(mate - corner)).astype(jnp.bfloat16)
            grad_ref[:, there] = own
            mate_grad[:, there] = mate
            total = total + (own.astype(jnp.float32) + mate.astype(jnp.float32))
        start += own_ref.shape[1]
        kept.append(kept_ref[...])
        taken += [ref[...] for ref in taken_refs]
    block = jnp.dot(grad_ref[...], jnp.concatenate(kept, 0), preferred_element_type=jnp.float32)
    block += jnp.dot(mate_grad[...], jnp.concatenate(taken, 0), preferred_element_type=jnp.float32)
    bias = jnp.sum(total.T, axis=0, keepdims=True)
    bias = jnp.pad(bias, ((0, 0), (0, half - variables)))
    block_ref[:variables] = (block * scale).astype(block_ref.dtype)
    spare = block_ref.shape[0] - variables
    block_ref[variables:] = jnp.broadcast_to(bias * scale, (spare, half)).astype(block_ref.dtype)


def gradient_rows(scale, var_weight, area, parts):
    variables = parts[0][0].shape[0]
    count = area.shape[1]
    half = parts[0][5].shape[1]
    rows = -(-(variables + 1) // 8) * 8
    operands = [value for part in parts for value in part]
    return pl.pallas_call(
        functools.partial(gradient_kernel, scale, len(parts)),
        out_shape=(
            jax.ShapeDtypeStruct((variables, count), jnp.bfloat16),
            jax.ShapeDtypeStruct((rows, half), jnp.bfloat16),
        ),
        in_specs=[VMEM] * (2 + len(operands)),
        out_specs=(VMEM, VMEM),
        scratch_shapes=[pltpu.VMEM((variables, count), jnp.bfloat16)],
        compiler_params=pltpu.CompilerParams(vmem_limit_bytes=8 << 20),
        cost_estimate=pl.CostEstimate(
            flops=4 * count * half * rows, bytes_accessed=4 * count * half, transcendentals=2 * variables * count
        ),
        name="gradient_rows",
    )(var_weight, area, *operands)


def write_half(lanes, block_ref, out_hbm, half_ref, sem):
    half_ref[...] = block_ref[: half_ref.shape[0]].astype(jnp.float32)
    copy = pltpu.make_async_copy(half_ref, out_hbm.at[:, lanes], sem)
    copy.start()
    return copy


def own_half_kernel(role_ref, here_ref, out_hbm, half_ref, sem):
    mine, _ = halves_of(role_ref[0], here_ref.shape[1])
    write_half(mine, here_ref, out_hbm, half_ref, sem).wait()


def other_half_kernel(role_ref, here_ref, there_ref, _, out_hbm, bias_hbm, half_ref, sem, bias_ref, bias_sem):
    role = role_ref[0]
    _, other = halves_of(role, there_ref.shape[1])
    copy = write_half(other, there_ref, out_hbm, half_ref, sem)
    variables = half_ref.shape[0]
    row = slice(variables, variables + 1)
    bias = jnp.where(role == 0, here_ref[row].astype(jnp.float32), there_ref[row].astype(jnp.float32))
    bias_ref[...] = bias[:, :variables]
    bias_copy = pltpu.make_async_copy(bias_ref, bias_hbm, bias_sem)
    bias_copy.start()
    copy.wait()
    bias_copy.wait()


def tail(role, here, there, variables):
    half = here.shape[1]
    whole = jax.ShapeDtypeStruct((variables, 2 * half), jnp.float32)
    scratch = [pltpu.VMEM((variables, half), jnp.float32), pltpu.SemaphoreType.DMA]
    params = pltpu.CompilerParams(vmem_limit_bytes=4 << 20)
    begun = pl.pallas_call(
        own_half_kernel,
        out_shape=whole,
        in_specs=[SMEM, VMEM],
        out_specs=HBM,
        scratch_shapes=scratch,
        compiler_params=params,
        cost_estimate=pl.CostEstimate(flops=0, bytes_accessed=6 * here.size, transcendentals=0),
        name="own_half",
    )(role, here)
    return pl.pallas_call(
        other_half_kernel,
        out_shape=(whole, jax.ShapeDtypeStruct((1, variables), jnp.float32)),
        in_specs=[SMEM, VMEM, VMEM, HBM],
        out_specs=(HBM, HBM),
        scratch_shapes=scratch + [pltpu.VMEM((1, variables), jnp.float32), pltpu.SemaphoreType.DMA],
        input_output_aliases={3: 0},
        compiler_params=params,
        cost_estimate=pl.CostEstimate(flops=0, bytes_accessed=6 * here.size, transcendentals=0),
        name="other_half",
    )(role, here, there, begun)


def four_members(latent, head_weight, head_bias, targets, var_weight, tile_fill):
    _, local_points, _ = latent.shape
    ens = lax.axis_size("ens")
    index = lax.axis_index("space") * ens + lax.axis_index("ens")
    role = role_of(index, groups_of(lax.axis_size("space") * ens)[1]).astype(jnp.int32)[None]
    scale = 1.0 / math.sqrt(4 * local_points * lax.axis_size("space"))
    area = area_of(local_points, tile_fill)
    source = (in_hbm(latent[0]), in_hbm(head_weight.T), in_hbm(head_bias[None]))
    starts = [k * local_points // HALVES for k in range(HALVES)]
    projected = [project_rows(role, *source, start, local_points // HALVES) for start in starts]
    far = [swap(part[0], lambda i: 2) for part in projected]
    projected = lax.optimization_barrier(projected)
    rows = (var_weight[None], area[None])
    parts = []
    for start, (own, kept, *given), across in zip(starts, projected, far):
        mate = swap(own, lambda i: 1)
        taken = [swap(piece, lambda i: 1) for piece in given]
        corner = swap(across, lambda i: 1)
        terms = terms_rows(start, *rows, own, mate, across, targets)
        parts.append((own, mate, corner, *terms, kept, *taken))
    grad, block = gradient_rows(scale, *rows, parts)
    grad_latent = back(grad[None], head_weight)
    block, grad_latent = butterfly(block, grad_latent)
    there = swap(block, lambda i: 1)
    total, bias = tail(role, block, there, targets.shape[0])
    return grad_latent, total.T, bias[0]


def local(latent, head_weight, head_bias, targets, var_weight, tile_fill):
    space, ens = lax.axis_size("space"), lax.axis_size("ens")
    members, _, channels = latent.shape
    fits = members == 1 and ens == 4 and is_pow2(space)
    fits = fits and channels % 256 == 0 and targets.shape[0] <= 128 and latent.shape[1] % (128 * HALVES * PIECES) == 0
    plan = four_members if fits else general
    return plan(latent, head_weight, head_bias, targets, var_weight, tile_fill)


def solution(mesh):
    placed = (P("ens", "space", None), P(), P(), P(None, "space"), P(), P("space"))
    return jax.shard_map(
        local,
        mesh=mesh,
        in_specs=placed,
        out_specs=(P("ens", "space", None), P(), P()),
        check_vma=False,
    )
```

```python
import functools
import math

import jax
import jax.numpy as jnp
from jax import lax
from jax.experimental import pallas as pl
from jax.experimental.pallas import tpu as pltpu
from jax.sharding import PartitionSpec as P

TILE_PTS = 128
SMOOTH = 0.05
ALL = ("space", "ens")


def smooth_sign(value):
    return value * lax.rsqrt(value * value + SMOOTH * SMOOTH)


def is_pow2(n):
    return n > 0 and n & (n - 1) == 0


def swap(value, bits_of):
    count = lax.axis_size("space") * lax.axis_size("ens")
    return lax.ppermute(value, ALL, [(i, i ^ bits_of(i)) for i in range(count)])


def round_bf16(value):
    return lax.reduce_precision(value, exponent_bits=8, mantissa_bits=7)


def groups_of(count):
    bits = [1 << k for k in range(1, count.bit_length() - 1)]
    groups = [bits[k : k + 2] for k in range(0, len(bits), 2)]
    return groups, sum(group[-1] for group in groups)


def parity(value):
    return value.bit_count() % 2


def role_of(index, crossed):
    role = index % 2
    bit = 2
    while bit <= crossed:
        if bit & crossed:
            role = (role + index // bit) % 2
        bit *= 2
    return role


def hop_swap(wire, crossed, first, second):
    def bits_of(index):
        bits = second if role_of(index, crossed) else first
        return bits ^ parity(bits & crossed)

    return swap(wire, bits_of)


def butterfly(wire, beside):
    groups, crossed = groups_of(lax.axis_size("space") * lax.axis_size("ens"))
    other = groups[::-1] if len(groups[-1]) == 2 else groups
    for hop, (first, second) in enumerate(zip(groups, other)):
        got = [hop_swap(wire, crossed, first[0], second[0])]
        if len(first) == 2:
            got.append(hop_swap(wire, crossed, first[1], second[1]))
            got.append(hop_swap(wire, crossed, sum(first), sum(second)))
        if hop == 0:
            *got, beside = lax.optimization_barrier((*got, beside))
        got = [value.astype(jnp.float32) for value in got]
        block = wire.astype(jnp.float32) + got[0]
        if len(got) == 3:
            block = block + (got[1] + got[2])
        wire = round_bf16(block).astype(jnp.bfloat16)
    return wire, beside


def area_of(local_points, tile_fill):
    points = local_points * lax.axis_size("space")
    local_index = jnp.arange(local_points, dtype=jnp.int32)
    global_index = lax.axis_index("space") * local_points + local_index
    live = local_index % TILE_PTS < jnp.repeat(tile_fill, TILE_PTS)
    latitude = jnp.pi * ((global_index.astype(jnp.float32) + 0.5) / points - 0.5)
    return jnp.where(live, jnp.cos(latitude), 0.0)


def project(latent, head_weight, head_bias):
    preds = jnp.einsum("mpd,dv->mvp", latent, head_weight, preferred_element_type=jnp.float32)
    return (preds + head_bias[None, :, None]).astype(jnp.bfloat16)


def back(grad_pred, head_weight):
    return jnp.einsum(
        "mvp,dv->mpd", grad_pred, head_weight, preferred_element_type=jnp.float32
    ).astype(jnp.bfloat16)


def general(latent, head_weight, head_bias, targets, var_weight, tile_fill):
    members = latent.shape[0] * lax.axis_size("ens")
    points = latent.shape[1] * lax.axis_size("space")
    preds = project(latent, head_weight, head_bias)
    values = preds.astype(jnp.float32)
    everyone = lax.all_gather(preds, "ens", axis=0, tiled=True)

    def one_member(slot, total):
        other = lax.dynamic_index_in_dim(everyone, slot, 0, keepdims=True).astype(jnp.float32)
        return total + smooth_sign(values - other)

    pair = lax.fori_loop(0, members, one_member, jnp.zeros(values.shape, jnp.float32))
    weight = area_of(latent.shape[1], tile_fill)[None, :] * var_weight[:, None]
    sign = smooth_sign(values - targets.astype(jnp.float32)[None])
    grad_pred = (weight[None] * (sign - pair / (members - 1))).astype(jnp.bfloat16)
    grad_latent = back(grad_pred, head_weight)
    scale = 1.0 / jnp.sqrt(jnp.float32(members) * jnp.float32(points))
    weight_sum = jnp.einsum("mpd,mvp->dv", latent, grad_pred, preferred_element_type=jnp.float32)
    bias_sum = jnp.sum(grad_pred.astype(jnp.float32), axis=(0, 2))
    weight_total, bias_total = lax.psum((weight_sum * scale, bias_sum * scale), ALL)
    return grad_latent, weight_total, bias_total


VMEM = pl.BlockSpec(memory_space=pltpu.VMEM)
SMEM = pl.BlockSpec(memory_space=pltpu.SMEM)
HBM = pl.BlockSpec(memory_space=pltpu.HBM)
LAST = (((1,), (1,)), ((), ()))
HALVES = 1
PIECES = 3
in_hbm = functools.partial(pltpu.with_memory_space_constraint, memory_space=pltpu.HBM)
in_hbm = functools.partial(pltpu.with_memory_space_constraint, memory_space=pltpu.HBM)


def halves_of(role, half):
    return [pl.ds(pl.multiple_of(r * half, 128), half) for r in (role, 1 - role)]


def project_kernel(start, role_ref, latent_hbm, weight_hbm, bias_hbm, preds_ref, kept_ref, *rest):
    *given_refs, weight, bias, sems = rest
    mine, other = halves_of(role_ref[0], kept_ref.shape[1])
    count = kept_ref.shape[0]
    step = given_refs[0].shape[0]
    pairs = [(weight_hbm, weight), (bias_hbm, bias), (latent_hbm.at[pl.ds(start, count), mine], kept_ref)]
    pairs += [(latent_hbm.at[pl.ds(start + k * step, step), other], ref) for k, ref in enumerate(given_refs)]
    copies = [pltpu.make_async_copy(source, target, sems.at[k]) for k, (source, target) in enumerate(pairs)]
    for copy in copies:
        copy.start()
    for copy in copies[:3]:
        copy.wait()
    total = column(bias[...])[:, :1]
    total = total + lax.dot_general(weight[:, mine], kept_ref[...], LAST, preferred_element_type=jnp.float32)
    for copy in copies[3:]:
        copy.wait()
    given = jnp.concatenate([ref[...] for ref in given_refs], 0)
    total = total + lax.dot_general(weight[:, other], given, LAST, preferred_element_type=jnp.float32)
    preds_ref[...] = total.astype(preds_ref.dtype)


def project_rows(role, latent, weight, bias, start, count):
    variables, channels = weight.shape
    part = jax.ShapeDtypeStruct((count, channels // 2), jnp.bfloat16)
    piece = jax.ShapeDtypeStruct((count // PIECES, channels // 2), jnp.bfloat16)
    return pl.pallas_call(
        functools.partial(project_kernel, start),
        out_shape=[jax.ShapeDtypeStruct((variables, count), jnp.bfloat16), part] + [piece] * PIECES,
        in_specs=[SMEM, HBM, HBM, HBM],
        out_specs=[VMEM] * (2 + PIECES),
        scratch_shapes=[
            pltpu.VMEM((variables, channels), jnp.bfloat16),
            pltpu.VMEM((1, variables), jnp.float32),
            pltpu.SemaphoreType.DMA((3 + PIECES,)),
        ],
        compiler_params=pltpu.CompilerParams(vmem_limit_bytes=8 << 20),
        cost_estimate=pl.CostEstimate(
            flops=2 * count * channels * variables,
            bytes_accessed=2 * channels * (count + variables),
            transcendentals=0,
        ),
        name="project_rows",
    )(role, latent, weight, bias)


def chunks(count):
    return [slice(k, k + 128) for k in range(0, count, 128)]


def column(row):
    return jnp.broadcast_to(row, (128, row.shape[1])).T


def terms_kernel(start, var_ref, area_ref, own_ref, mate_ref, far_ref, seen_ref, own_terms, mate_terms):
    var_weight = column(var_ref[...])
    for at in chunks(own_ref.shape[1]):
        own, mate, far = (r[:, at].astype(jnp.float32) for r in (own_ref, mate_ref, far_ref))
        there = slice(start + at.start, start + at.stop)
        seen = seen_ref[:, there].astype(jnp.float32)
        weight = area_ref[:, there] * var_weight
        inside = smooth_sign(own - mate)
        own_terms[:, at] = weight * (smooth_sign(own - seen) - (smooth_sign(own - far) + inside) * (1 / 3))
        mate_terms[:, at] = weight * (smooth_sign(mate - seen) - (smooth_sign(mate - far) - inside) * (1 / 3))


def terms_rows(start, var_weight, area, own, mate, far, seen):
    part = jax.ShapeDtypeStruct(own.shape, jnp.float32)
    return pl.pallas_call(
        functools.partial(terms_kernel, start),
        out_shape=(part, part),
        in_specs=[VMEM] * 6,
        out_specs=(VMEM, VMEM),
        compiler_params=pltpu.CompilerParams(vmem_limit_bytes=8 << 20),
        cost_estimate=pl.CostEstimate(flops=40 * own.size, bytes_accessed=16 * own.size, transcendentals=5 * own.size),
        name="terms_rows",
    )(var_weight, area, own, mate, far, seen)


def gradient_kernel(scale, parts, var_ref, area_ref, *rest):
    *refs, grad_ref, block_ref, mate_grad = rest
    variables = grad_ref.shape[0]
    half = block_ref.shape[1]
    third = column(var_ref[...]) * (1 / 3)
    total = jnp.zeros((variables, 128), jnp.float32)
    start = 0
    kept, taken = [], []
    size = len(refs) // parts
    for k in range(parts):
        own_ref, mate_ref, corner_ref, own_terms, mate_terms, kept_ref, *taken_refs = refs[k * size : (k + 1) * size]
        for at in chunks(own_ref.shape[1]):
            own, mate, corner = (r[:, at].astype(jnp.float32) for r in (own_ref, mate_ref, corner_ref))
            there = slice(start + at.start, start + at.stop)
            weight = area_ref[:, there] * third
            own = (own_terms[:, at] - weight * smooth_sign(own - corner)).astype(jnp.bfloat16)
            mate = (mate_terms[:, at] - weight * smooth_sign(mate - corner)).astype(jnp.bfloat16)
            grad_ref[:, there] = own
            mate_grad[:, there] = mate
            total = total + (own.astype(jnp.float32) + mate.astype(jnp.float32))
        start += own_ref.shape[1]
        kept.append(kept_ref[...])
        taken += [ref[...] for ref in taken_refs]
    both = jnp.concatenate([grad_ref[...], mate_grad[...]], 1)
    block = jnp.dot(both, jnp.concatenate(kept + taken, 0), preferred_element_type=jnp.float32)
    bias = jnp.sum(total.T, axis=0, keepdims=True)
    bias = jnp.pad(bias, ((0, 0), (0, half - variables)))
    block_ref[:variables] = (block * scale).astype(block_ref.dtype)
    spare = block_ref.shape[0] - variables
    block_ref[variables:] = jnp.broadcast_to(bias * scale, (spare, half)).astype(block_ref.dtype)


def gradient_rows(scale, var_weight, area, parts):
    variables = parts[0][0].shape[0]
    count = area.shape[1]
    half = parts[0][5].shape[1]
    rows = -(-(variables + 1) // 8) * 8
    operands = [value for part in parts for value in part]
    return pl.pallas_call(
        functools.partial(gradient_kernel, scale, len(parts)),
        out_shape=(
            jax.ShapeDtypeStruct((variables, count), jnp.bfloat16),
            jax.ShapeDtypeStruct((rows, half), jnp.bfloat16),
        ),
        in_specs=[VMEM] * (2 + len(operands)),
        out_specs=(VMEM, VMEM),
        scratch_shapes=[pltpu.VMEM((variables, count), jnp.bfloat16)],
        compiler_params=pltpu.CompilerParams(vmem_limit_bytes=8 << 20),
        cost_estimate=pl.CostEstimate(
            flops=4 * count * half * rows, bytes_accessed=4 * count * half, transcendentals=2 * variables * count
        ),
        name="gradient_rows",
    )(var_weight, area, *operands)


def write_half(lanes, block_ref, out_hbm, half_ref, sem):
    half_ref[...] = block_ref[: half_ref.shape[0]].astype(jnp.float32)
    copy = pltpu.make_async_copy(half_ref, out_hbm.at[:, lanes], sem)
    copy.start()
    return copy


def own_half_kernel(role_ref, here_ref, out_hbm, half_ref, sem):
    mine, _ = halves_of(role_ref[0], here_ref.shape[1])
    write_half(mine, here_ref, out_hbm, half_ref, sem).wait()


def other_half_kernel(role_ref, here_ref, there_ref, _, out_hbm, bias_hbm, half_ref, sem, bias_ref, bias_sem):
    role = role_ref[0]
    _, other = halves_of(role, there_ref.shape[1])
    copy = write_half(other, there_ref, out_hbm, half_ref, sem)
    variables = half_ref.shape[0]
    row = slice(variables, variables + 1)
    bias = jnp.where(role == 0, here_ref[row].astype(jnp.float32), there_ref[row].astype(jnp.float32))
    bias_ref[...] = bias[:, :variables]
    bias_copy = pltpu.make_async_copy(bias_ref, bias_hbm, bias_sem)
    bias_copy.start()
    copy.wait()
    bias_copy.wait()


def tail(role, here, there, variables):
    half = here.shape[1]
    whole = jax.ShapeDtypeStruct((variables, 2 * half), jnp.float32)
    scratch = [pltpu.VMEM((variables, half), jnp.float32), pltpu.SemaphoreType.DMA]
    params = pltpu.CompilerParams(vmem_limit_bytes=4 << 20)
    begun = pl.pallas_call(
        own_half_kernel,
        out_shape=whole,
        in_specs=[SMEM, VMEM],
        out_specs=HBM,
        scratch_shapes=scratch,
        compiler_params=params,
        cost_estimate=pl.CostEstimate(flops=0, bytes_accessed=6 * here.size, transcendentals=0),
        name="own_half",
    )(role, here)
    return pl.pallas_call(
        other_half_kernel,
        out_shape=(whole, jax.ShapeDtypeStruct((1, variables), jnp.float32)),
        in_specs=[SMEM, VMEM, VMEM, HBM],
        out_specs=(HBM, HBM),
        scratch_shapes=scratch + [pltpu.VMEM((1, variables), jnp.float32), pltpu.SemaphoreType.DMA],
        input_output_aliases={3: 0},
        compiler_params=params,
        cost_estimate=pl.CostEstimate(flops=0, bytes_accessed=6 * here.size, transcendentals=0),
        name="other_half",
    )(role, here, there, begun)


def four_members(latent, head_weight, head_bias, targets, var_weight, tile_fill):
    _, local_points, _ = latent.shape
    ens = lax.axis_size("ens")
    index = lax.axis_index("space") * ens + lax.axis_index("ens")
    role = role_of(index, groups_of(lax.axis_size("space") * ens)[1]).astype(jnp.int32)[None]
    scale = 1.0 / math.sqrt(4 * local_points * lax.axis_size("space"))
    area = area_of(local_points, tile_fill)
    source = (in_hbm(latent[0]), in_hbm(head_weight.T), in_hbm(head_bias[None]))
    starts = [k * local_points // HALVES for k in range(HALVES)]
    projected = [project_rows(role, *source, start, local_points // HALVES) for start in starts]
    far = [swap(part[0], lambda i: 2) for part in projected]
    projected = lax.optimization_barrier(projected)
    rows = (var_weight[None], area[None])
    parts = []
    for start, (own, kept, *given), across in zip(starts, projected, far):
        mate = swap(own, lambda i: 1)
        taken = [swap(piece, lambda i: 1) for piece in given]
        corner = swap(across, lambda i: 1)
        terms = terms_rows(start, *rows, own, mate, across, targets)
        parts.append((own, mate, corner, *terms, kept, *taken))
    grad, block = gradient_rows(scale, *rows, parts)
    grad_latent = back(grad[None], head_weight)
    block, grad_latent = butterfly(block, grad_latent)
    there = swap(block, lambda i: 1)
    total, bias = tail(role, block, there, targets.shape[0])
    return grad_latent, total.T, bias[0]


def local(latent, head_weight, head_bias, targets, var_weight, tile_fill):
    space, ens = lax.axis_size("space"), lax.axis_size("ens")
    members, _, channels = latent.shape
    fits = members == 1 and ens == 4 and is_pow2(space)
    fits = fits and channels % 256 == 0 and targets.shape[0] <= 128 and latent.shape[1] % (128 * HALVES * PIECES) == 0
    plan = four_members if fits else general
    return plan(latent, head_weight, head_bias, targets, var_weight, tile_fill)


def solution(mesh):
    placed = (P("ens", "space", None), P(), P(), P(None, "space"), P(), P("space"))
    return jax.shard_map(
        local,
        mesh=mesh,
        in_specs=placed,
        out_specs=(P("ens", "space", None), P(), P()),
        check_vma=False,
    )
```

```python
import functools
import math

import jax
import jax.numpy as jnp
from jax import lax
from jax.experimental import pallas as pl
from jax.experimental.pallas import tpu as pltpu
from jax.sharding import PartitionSpec as P

TILE_PTS = 128
SMOOTH = 0.05
ALL = ("space", "ens")


def smooth_sign(value):
    return value * lax.rsqrt(value * value + SMOOTH * SMOOTH)


def is_pow2(n):
    return n > 0 and n & (n - 1) == 0


def swap(value, bits_of):
    count = lax.axis_size("space") * lax.axis_size("ens")
    return lax.ppermute(value, ALL, [(i, i ^ bits_of(i)) for i in range(count)])


def round_bf16(value):
    return lax.reduce_precision(value, exponent_bits=8, mantissa_bits=7)


def groups_of(count):
    bits = [1 << k for k in range(1, count.bit_length() - 1)]
    groups = [bits[k : k + 2] for k in range(0, len(bits), 2)]
    return groups, sum(group[-1] for group in groups)


def parity(value):
    return value.bit_count() % 2


def role_of(index, crossed):
    role = index % 2
    bit = 2
    while bit <= crossed:
        if bit & crossed:
            role = (role + index // bit) % 2
        bit *= 2
    return role


def hop_swap(wire, crossed, first, second):
    def bits_of(index):
        bits = second if role_of(index, crossed) else first
        return bits ^ parity(bits & crossed)

    return swap(wire, bits_of)


def butterfly(wire, beside):
    groups, crossed = groups_of(lax.axis_size("space") * lax.axis_size("ens"))
    other = groups[::-1] if len(groups[-1]) == 2 else groups
    for hop, (first, second) in enumerate(zip(groups, other)):
        got = [hop_swap(wire, crossed, first[0], second[0])]
        if len(first) == 2:
            got.append(hop_swap(wire, crossed, first[1], second[1]))
            got.append(hop_swap(wire, crossed, sum(first), sum(second)))
        if hop == len(groups) - 1:
            *got, beside = lax.optimization_barrier((*got, beside))
        got = [value.astype(jnp.float32) for value in got]
        block = wire.astype(jnp.float32) + got[0]
        if len(got) == 3:
            block = block + (got[1] + got[2])
        wire = round_bf16(block).astype(jnp.bfloat16)
    return wire, beside


def area_of(local_points, tile_fill):
    points = local_points * lax.axis_size("space")
    local_index = jnp.arange(local_points, dtype=jnp.int32)
    global_index = lax.axis_index("space") * local_points + local_index
    live = local_index % TILE_PTS < jnp.repeat(tile_fill, TILE_PTS)
    latitude = jnp.pi * ((global_index.astype(jnp.float32) + 0.5) / points - 0.5)
    return jnp.where(live, jnp.cos(latitude), 0.0)


def project(latent, head_weight, head_bias):
    preds = jnp.einsum("mpd,dv->mvp", latent, head_weight, preferred_element_type=jnp.float32)
    return (preds + head_bias[None, :, None]).astype(jnp.bfloat16)


def back(grad_pred, head_weight):
    return jnp.einsum(
        "mvp,dv->mpd", grad_pred, head_weight, preferred_element_type=jnp.float32
    ).astype(jnp.bfloat16)


def general(latent, head_weight, head_bias, targets, var_weight, tile_fill):
    members = latent.shape[0] * lax.axis_size("ens")
    points = latent.shape[1] * lax.axis_size("space")
    preds = project(latent, head_weight, head_bias)
    values = preds.astype(jnp.float32)
    everyone = lax.all_gather(preds, "ens", axis=0, tiled=True)

    def one_member(slot, total):
        other = lax.dynamic_index_in_dim(everyone, slot, 0, keepdims=True).astype(jnp.float32)
        return total + smooth_sign(values - other)

    pair = lax.fori_loop(0, members, one_member, jnp.zeros(values.shape, jnp.float32))
    weight = area_of(latent.shape[1], tile_fill)[None, :] * var_weight[:, None]
    sign = smooth_sign(values - targets.astype(jnp.float32)[None])
    grad_pred = (weight[None] * (sign - pair / (members - 1))).astype(jnp.bfloat16)
    grad_latent = back(grad_pred, head_weight)
    scale = 1.0 / jnp.sqrt(jnp.float32(members) * jnp.float32(points))
    weight_sum = jnp.einsum("mpd,mvp->dv", latent, grad_pred, preferred_element_type=jnp.float32)
    bias_sum = jnp.sum(grad_pred.astype(jnp.float32), axis=(0, 2))
    weight_total, bias_total = lax.psum((weight_sum * scale, bias_sum * scale), ALL)
    return grad_latent, weight_total, bias_total


VMEM = pl.BlockSpec(memory_space=pltpu.VMEM)
SMEM = pl.BlockSpec(memory_space=pltpu.SMEM)
HBM = pl.BlockSpec(memory_space=pltpu.HBM)
LAST = (((1,), (1,)), ((), ()))
HALVES = 1
PIECES = 3
in_hbm = functools.partial(pltpu.with_memory_space_constraint, memory_space=pltpu.HBM)
in_hbm = functools.partial(pltpu.with_memory_space_constraint, memory_space=pltpu.HBM)


def halves_of(role, half):
    return [pl.ds(pl.multiple_of(r * half, 128), half) for r in (role, 1 - role)]


def project_kernel(start, role_ref, latent_hbm, weight_hbm, bias_hbm, preds_ref, kept_ref, *rest):
    *given_refs, weight, bias, sems = rest
    mine, other = halves_of(role_ref[0], kept_ref.shape[1])
    count = kept_ref.shape[0]
    step = given_refs[0].shape[0]
    pairs = [(weight_hbm, weight), (bias_hbm, bias), (latent_hbm.at[pl.ds(start, count), mine], kept_ref)]
    pairs += [(latent_hbm.at[pl.ds(start + k * step, step), other], ref) for k, ref in enumerate(given_refs)]
    copies = [pltpu.make_async_copy(source, target, sems.at[k]) for k, (source, target) in enumerate(pairs)]
    for copy in copies:
        copy.start()
    for copy in copies[:3]:
        copy.wait()
    total = column(bias[...])[:, :1]
    total = total + lax.dot_general(weight[:, mine], kept_ref[...], LAST, preferred_element_type=jnp.float32)
    for copy in copies[3:]:
        copy.wait()
    given = jnp.concatenate([ref[...] for ref in given_refs], 0)
    total = total + lax.dot_general(weight[:, other], given, LAST, preferred_element_type=jnp.float32)
    preds_ref[...] = total.astype(preds_ref.dtype)


def project_rows(role, latent, weight, bias, start, count):
    variables, channels = weight.shape
    part = jax.ShapeDtypeStruct((count, channels // 2), jnp.bfloat16)
    piece = jax.ShapeDtypeStruct((count // PIECES, channels // 2), jnp.bfloat16)
    return pl.pallas_call(
        functools.partial(project_kernel, start),
        out_shape=[jax.ShapeDtypeStruct((variables, count), jnp.bfloat16), part] + [piece] * PIECES,
        in_specs=[SMEM, HBM, HBM, HBM],
        out_specs=[VMEM] * (2 + PIECES),
        scratch_shapes=[
            pltpu.VMEM((variables, channels), jnp.bfloat16),
            pltpu.VMEM((1, variables), jnp.float32),
            pltpu.SemaphoreType.DMA((3 + PIECES,)),
        ],
        compiler_params=pltpu.CompilerParams(vmem_limit_bytes=8 << 20),
        cost_estimate=pl.CostEstimate(
            flops=2 * count * channels * variables,
            bytes_accessed=2 * channels * (count + variables),
            transcendentals=0,
        ),
        name="project_rows",
    )(role, latent, weight, bias)


def chunks(count):
    return [slice(k, k + 128) for k in range(0, count, 128)]


def column(row):
    return jnp.broadcast_to(row, (128, row.shape[1])).T


def terms_kernel(start, var_ref, area_ref, own_ref, mate_ref, far_ref, seen_ref, own_terms, mate_terms):
    var_weight = column(var_ref[...])
    for at in chunks(own_ref.shape[1]):
        own, mate, far = (r[:, at].astype(jnp.float32) for r in (own_ref, mate_ref, far_ref))
        there = slice(start + at.start, start + at.stop)
        seen = seen_ref[:, there].astype(jnp.float32)
        weight = area_ref[:, there] * var_weight
        inside = smooth_sign(own - mate)
        own_terms[:, at] = weight * (smooth_sign(own - seen) - (smooth_sign(own - far) + inside) * (1 / 3))
        mate_terms[:, at] = weight * (smooth_sign(mate - seen) - (smooth_sign(mate - far) - inside) * (1 / 3))


def terms_rows(start, var_weight, area, own, mate, far, seen):
    part = jax.ShapeDtypeStruct(own.shape, jnp.float32)
    return pl.pallas_call(
        functools.partial(terms_kernel, start),
        out_shape=(part, part),
        in_specs=[VMEM] * 6,
        out_specs=(VMEM, VMEM),
        compiler_params=pltpu.CompilerParams(vmem_limit_bytes=8 << 20),
        cost_estimate=pl.CostEstimate(flops=40 * own.size, bytes_accessed=16 * own.size, transcendentals=5 * own.size),
        name="terms_rows",
    )(var_weight, area, own, mate, far, seen)


def gradient_kernel(scale, parts, var_ref, area_ref, *rest):
    *refs, grad_ref, block_ref, mate_grad = rest
    variables = grad_ref.shape[0]
    half = block_ref.shape[1]
    third = column(var_ref[...]) * (1 / 3)
    total = jnp.zeros((variables, 128), jnp.float32)
    start = 0
    kept, taken = [], []
    size = len(refs) // parts
    for k in range(parts):
        own_ref, mate_ref, corner_ref, own_terms, mate_terms, kept_ref, *taken_refs = refs[k * size : (k + 1) * size]
        for at in chunks(own_ref.shape[1]):
            own, mate, corner = (r[:, at].astype(jnp.float32) for r in (own_ref, mate_ref, corner_ref))
            there = slice(start + at.start, start + at.stop)
            weight = area_ref[:, there] * third
            own = (own_terms[:, at] - weight * smooth_sign(own - corner)).astype(jnp.bfloat16)
            mate = (mate_terms[:, at] - weight * smooth_sign(mate - corner)).astype(jnp.bfloat16)
            grad_ref[:, there] = own
            mate_grad[:, there] = mate
            total = total + (own.astype(jnp.float32) + mate.astype(jnp.float32))
        start += own_ref.shape[1]
        kept.append(kept_ref[...])
        taken += [ref[...] for ref in taken_refs]
    block = jnp.dot(grad_ref[...], jnp.concatenate(kept, 0), preferred_element_type=jnp.float32)
    block += jnp.dot(mate_grad[...], jnp.concatenate(taken, 0), preferred_element_type=jnp.float32)
    bias = jnp.sum(total.T, axis=0, keepdims=True)
    bias = jnp.pad(bias, ((0, 0), (0, half - variables)))
    block_ref[:variables] = (block * scale).astype(block_ref.dtype)
    spare = block_ref.shape[0] - variables
    block_ref[variables:] = jnp.broadcast_to(bias * scale, (spare, half)).astype(block_ref.dtype)


def gradient_rows(scale, var_weight, area, parts):
    variables = parts[0][0].shape[0]
    count = area.shape[1]
    half = parts[0][5].shape[1]
    rows = -(-(variables + 1) // 8) * 8
    operands = [value for part in parts for value in part]
    return pl.pallas_call(
        functools.partial(gradient_kernel, scale, len(parts)),
        out_shape=(
            jax.ShapeDtypeStruct((variables, count), jnp.bfloat16),
            jax.ShapeDtypeStruct((rows, half), jnp.bfloat16),
        ),
        in_specs=[VMEM] * (2 + len(operands)),
        out_specs=(VMEM, VMEM),
        scratch_shapes=[pltpu.VMEM((variables, count), jnp.bfloat16)],
        compiler_params=pltpu.CompilerParams(vmem_limit_bytes=8 << 20),
        cost_estimate=pl.CostEstimate(
            flops=4 * count * half * rows, bytes_accessed=4 * count * half, transcendentals=2 * variables * count
        ),
        name="gradient_rows",
    )(var_weight, area, *operands)


def write_half(lanes, block_ref, out_hbm, half_ref, sem):
    half_ref[...] = block_ref[: half_ref.shape[0]].astype(jnp.float32)
    copy = pltpu.make_async_copy(half_ref, out_hbm.at[:, lanes], sem)
    copy.start()
    return copy


def own_half_kernel(role_ref, here_ref, out_hbm, half_ref, sem):
    mine, _ = halves_of(role_ref[0], here_ref.shape[1])
    write_half(mine, here_ref, out_hbm, half_ref, sem).wait()


def other_half_kernel(role_ref, here_ref, there_ref, _, out_hbm, bias_hbm, half_ref, sem, bias_ref, bias_sem):
    role = role_ref[0]
    _, other = halves_of(role, there_ref.shape[1])
    copy = write_half(other, there_ref, out_hbm, half_ref, sem)
    variables = half_ref.shape[0]
    row = slice(variables, variables + 1)
    bias = jnp.where(role == 0, here_ref[row].astype(jnp.float32), there_ref[row].astype(jnp.float32))
    bias_ref[...] = bias[:, :variables]
    bias_copy = pltpu.make_async_copy(bias_ref, bias_hbm, bias_sem)
    bias_copy.start()
    copy.wait()
    bias_copy.wait()


def tail(role, here, there, variables):
    half = here.shape[1]
    whole = jax.ShapeDtypeStruct((variables, 2 * half), jnp.float32)
    scratch = [pltpu.VMEM((variables, half), jnp.float32), pltpu.SemaphoreType.DMA]
    params = pltpu.CompilerParams(vmem_limit_bytes=4 << 20)
    begun = pl.pallas_call(
        own_half_kernel,
        out_shape=whole,
        in_specs=[SMEM, VMEM],
        out_specs=HBM,
        scratch_shapes=scratch,
        compiler_params=params,
        cost_estimate=pl.CostEstimate(flops=0, bytes_accessed=6 * here.size, transcendentals=0),
        name="own_half",
    )(role, here)
    return pl.pallas_call(
        other_half_kernel,
        out_shape=(whole, jax.ShapeDtypeStruct((1, variables), jnp.float32)),
        in_specs=[SMEM, VMEM, VMEM, HBM],
        out_specs=(HBM, HBM),
        scratch_shapes=scratch + [pltpu.VMEM((1, variables), jnp.float32), pltpu.SemaphoreType.DMA],
        input_output_aliases={3: 0},
        compiler_params=params,
        cost_estimate=pl.CostEstimate(flops=0, bytes_accessed=6 * here.size, transcendentals=0),
        name="other_half",
    )(role, here, there, begun)


def four_members(latent, head_weight, head_bias, targets, var_weight, tile_fill):
    _, local_points, _ = latent.shape
    ens = lax.axis_size("ens")
    index = lax.axis_index("space") * ens + lax.axis_index("ens")
    role = role_of(index, groups_of(lax.axis_size("space") * ens)[1]).astype(jnp.int32)[None]
    scale = 1.0 / math.sqrt(4 * local_points * lax.axis_size("space"))
    area = area_of(local_points, tile_fill)
    source = (in_hbm(latent[0]), in_hbm(head_weight.T), in_hbm(head_bias[None]))
    starts = [k * local_points // HALVES for k in range(HALVES)]
    projected = [project_rows(role, *source, start, local_points // HALVES) for start in starts]
    far = [swap(part[0], lambda i: 2) for part in projected]
    projected = lax.optimization_barrier(projected)
    rows = (var_weight[None], area[None])
    parts = []
    for start, (own, kept, *given), across in zip(starts, projected, far):
        mate = swap(own, lambda i: 1)
        taken = [swap(piece, lambda i: 1) for piece in given]
        corner = swap(across, lambda i: 1)
        terms = terms_rows(start, *rows, own, mate, across, targets)
        parts.append((own, mate, corner, *terms, kept, *taken))
    grad, block = gradient_rows(scale, *rows, parts)
    grad_latent = back(grad[None], head_weight)
    block, grad_latent = butterfly(block, grad_latent)
    there = swap(block, lambda i: 1)
    total, bias = tail(role, block, there, targets.shape[0])
    return grad_latent, total.T, bias[0]


def local(latent, head_weight, head_bias, targets, var_weight, tile_fill):
    space, ens = lax.axis_size("space"), lax.axis_size("ens")
    members, _, channels = latent.shape
    fits = members == 1 and ens == 4 and is_pow2(space)
    fits = fits and channels % 256 == 0 and targets.shape[0] <= 128 and latent.shape[1] % (128 * HALVES * PIECES) == 0
    plan = four_members if fits else general
    return plan(latent, head_weight, head_bias, targets, var_weight, tile_fill)


def solution(mesh):
    placed = (P("ens", "space", None), P(), P(), P(None, "space"), P(), P("space"))
    return jax.shard_map(
        local,
        mesh=mesh,
        in_specs=placed,
        out_specs=(P("ens", "space", None), P(), P()),
        check_vma=False,
    )
```

```python
import functools
import math

import jax
import jax.numpy as jnp
from jax import lax
from jax.experimental import pallas as pl
from jax.experimental.pallas import tpu as pltpu
from jax.sharding import PartitionSpec as P

TILE_PTS = 128
SMOOTH = 0.05
ALL = ("space", "ens")


def smooth_sign(value):
    return value * lax.rsqrt(value * value + SMOOTH * SMOOTH)


def is_pow2(n):
    return n > 0 and n & (n - 1) == 0


def swap(value, bits_of):
    count = lax.axis_size("space") * lax.axis_size("ens")
    return lax.ppermute(value, ALL, [(i, i ^ bits_of(i)) for i in range(count)])


def round_bf16(value):
    return lax.reduce_precision(value, exponent_bits=8, mantissa_bits=7)


def groups_of(count):
    bits = [1 << k for k in range(1, count.bit_length() - 1)]
    groups = [bits[k : k + 2] for k in range(0, len(bits), 2)]
    return groups, sum(group[-1] for group in groups)


def parity(value):
    return value.bit_count() % 2


def role_of(index, crossed):
    role = index % 2
    bit = 2
    while bit <= crossed:
        if bit & crossed:
            role = (role + index // bit) % 2
        bit *= 2
    return role


def hop_swap(wire, crossed, first, second):
    def bits_of(index):
        bits = second if role_of(index, crossed) else first
        return bits ^ parity(bits & crossed)

    return swap(wire, bits_of)


def butterfly(wire, beside):
    groups, crossed = groups_of(lax.axis_size("space") * lax.axis_size("ens"))
    other = groups[::-1] if len(groups[-1]) == 2 else groups
    for hop, (first, second) in enumerate(zip(groups, other)):
        got = [hop_swap(wire, crossed, first[0], second[0])]
        if len(first) == 2:
            got.append(hop_swap(wire, crossed, first[1], second[1]))
            got.append(hop_swap(wire, crossed, sum(first), sum(second)))
        if hop == len(groups) - 1:
            *got, beside = lax.optimization_barrier((*got, beside))
        got = [value.astype(jnp.float32) for value in got]
        block = wire.astype(jnp.float32) + got[0]
        if len(got) == 3:
            block = block + (got[1] + got[2])
        wire = round_bf16(block).astype(jnp.bfloat16)
    return wire, beside


def area_of(local_points, tile_fill):
    points = local_points * lax.axis_size("space")
    local_index = jnp.arange(local_points, dtype=jnp.int32)
    global_index = lax.axis_index("space") * local_points + local_index
    live = local_index % TILE_PTS < jnp.repeat(tile_fill, TILE_PTS)
    latitude = jnp.pi * ((global_index.astype(jnp.float32) + 0.5) / points - 0.5)
    return jnp.where(live, jnp.cos(latitude), 0.0)


def project(latent, head_weight, head_bias):
    preds = jnp.einsum("mpd,dv->mvp", latent, head_weight, preferred_element_type=jnp.float32)
    return (preds + head_bias[None, :, None]).astype(jnp.bfloat16)


def back(grad_pred, head_weight):
    return jnp.einsum(
        "mvp,dv->mpd", grad_pred, head_weight, preferred_element_type=jnp.float32
    ).astype(jnp.bfloat16)


def general(latent, head_weight, head_bias, targets, var_weight, tile_fill):
    members = latent.shape[0] * lax.axis_size("ens")
    points = latent.shape[1] * lax.axis_size("space")
    preds = project(latent, head_weight, head_bias)
    values = preds.astype(jnp.float32)
    everyone = lax.all_gather(preds, "ens", axis=0, tiled=True)

    def one_member(slot, total):
        other = lax.dynamic_index_in_dim(everyone, slot, 0, keepdims=True).astype(jnp.float32)
        return total + smooth_sign(values - other)

    pair = lax.fori_loop(0, members, one_member, jnp.zeros(values.shape, jnp.float32))
    weight = area_of(latent.shape[1], tile_fill)[None, :] * var_weight[:, None]
    sign = smooth_sign(values - targets.astype(jnp.float32)[None])
    grad_pred = (weight[None] * (sign - pair / (members - 1))).astype(jnp.bfloat16)
    grad_latent = back(grad_pred, head_weight)
    scale = 1.0 / jnp.sqrt(jnp.float32(members) * jnp.float32(points))
    weight_sum = jnp.einsum("mpd,mvp->dv", latent, grad_pred, preferred_element_type=jnp.float32)
    bias_sum = jnp.sum(grad_pred.astype(jnp.float32), axis=(0, 2))
    weight_total, bias_total = lax.psum((weight_sum * scale, bias_sum * scale), ALL)
    return grad_latent, weight_total, bias_total


VMEM = pl.BlockSpec(memory_space=pltpu.VMEM)
SMEM = pl.BlockSpec(memory_space=pltpu.SMEM)
HBM = pl.BlockSpec(memory_space=pltpu.HBM)
LAST = (((1,), (1,)), ((), ()))
HALVES = 1
PIECES = 3
in_hbm = functools.partial(pltpu.with_memory_space_constraint, memory_space=pltpu.HBM)
in_hbm = functools.partial(pltpu.with_memory_space_constraint, memory_space=pltpu.HBM)


def halves_of(role, half):
    return [pl.ds(pl.multiple_of(r * half, 128), half) for r in (role, 1 - role)]


def project_kernel(start, role_ref, latent_hbm, weight_hbm, bias_hbm, preds_ref, kept_ref, *rest):
    *given_refs, weight, bias, sems = rest
    mine, other = halves_of(role_ref[0], kept_ref.shape[1])
    count = kept_ref.shape[0]
    step = given_refs[0].shape[0]
    pairs = [(weight_hbm, weight), (bias_hbm, bias), (latent_hbm.at[pl.ds(start, count), mine], kept_ref)]
    pairs += [(latent_hbm.at[pl.ds(start + k * step, step), other], ref) for k, ref in enumerate(given_refs)]
    copies = [pltpu.make_async_copy(source, target, sems.at[k]) for k, (source, target) in enumerate(pairs)]
    for copy in copies:
        copy.start()
    for copy in copies[:3]:
        copy.wait()
    total = column(bias[...])[:, :1]
    total = total + lax.dot_general(weight[:, mine], kept_ref[...], LAST, preferred_element_type=jnp.float32)
    for copy in copies[3:]:
        copy.wait()
    given = jnp.concatenate([ref[...] for ref in given_refs], 0)
    total = total + lax.dot_general(weight[:, other], given, LAST, preferred_element_type=jnp.float32)
    preds_ref[...] = total.astype(preds_ref.dtype)


def project_rows(role, latent, weight, bias, start, count):
    variables, channels = weight.shape
    part = jax.ShapeDtypeStruct((count, channels // 2), jnp.bfloat16)
    piece = jax.ShapeDtypeStruct((count // PIECES, channels // 2), jnp.bfloat16)
    return pl.pallas_call(
        functools.partial(project_kernel, start),
        out_shape=[jax.ShapeDtypeStruct((variables, count), jnp.bfloat16), part] + [piece] * PIECES,
        in_specs=[SMEM, HBM, HBM, HBM],
        out_specs=[VMEM] * (2 + PIECES),
        scratch_shapes=[
            pltpu.VMEM((variables, channels), jnp.bfloat16),
            pltpu.VMEM((1, variables), jnp.float32),
            pltpu.SemaphoreType.DMA((3 + PIECES,)),
        ],
        compiler_params=pltpu.CompilerParams(vmem_limit_bytes=8 << 20),
        cost_estimate=pl.CostEstimate(
            flops=2 * count * channels * variables,
            bytes_accessed=2 * channels * (count + variables),
            transcendentals=0,
        ),
        name="project_rows",
    )(role, latent, weight, bias)


def chunks(count):
    return [slice(k, k + 128) for k in range(0, count, 128)]


def column(row):
    return jnp.broadcast_to(row, (128, row.shape[1])).T


def terms_kernel(start, var_ref, area_ref, own_ref, mate_ref, far_ref, seen_ref, own_terms, mate_terms):
    var_weight = column(var_ref[...])
    for at in chunks(own_ref.shape[1]):
        own, mate, far = (r[:, at].astype(jnp.float32) for r in (own_ref, mate_ref, far_ref))
        there = slice(start + at.start, start + at.stop)
        seen = seen_ref[:, there].astype(jnp.float32)
        weight = area_ref[:, there] * var_weight
        inside = smooth_sign(own - mate)
        own_terms[:, at] = weight * (smooth_sign(own - seen) - (smooth_sign(own - far) + inside) * (1 / 3))
        mate_terms[:, at] = weight * (smooth_sign(mate - seen) - (smooth_sign(mate - far) - inside) * (1 / 3))


def terms_rows(start, var_weight, area, own, mate, far, seen):
    part = jax.ShapeDtypeStruct(own.shape, jnp.float32)
    return pl.pallas_call(
        functools.partial(terms_kernel, start),
        out_shape=(part, part),
        in_specs=[VMEM] * 6,
        out_specs=(VMEM, VMEM),
        compiler_params=pltpu.CompilerParams(vmem_limit_bytes=8 << 20),
        cost_estimate=pl.CostEstimate(flops=40 * own.size, bytes_accessed=16 * own.size, transcendentals=5 * own.size),
        name="terms_rows",
    )(var_weight, area, own, mate, far, seen)


def gradient_kernel(scale, parts, var_ref, area_ref, *rest):
    *refs, grad_ref, block_ref, mate_grad = rest
    variables = grad_ref.shape[0]
    half = block_ref.shape[1]
    third = column(var_ref[...]) * (1 / 3)
    total = jnp.zeros((variables, 128), jnp.float32)
    start = 0
    kept, taken = [], []
    size = len(refs) // parts
    for k in range(parts):
        own_ref, mate_ref, corner_ref, own_terms, mate_terms, kept_ref, *taken_refs = refs[k * size : (k + 1) * size]
        for at in chunks(own_ref.shape[1]):
            own, mate, corner = (r[:, at].astype(jnp.float32) for r in (own_ref, mate_ref, corner_ref))
            there = slice(start + at.start, start + at.stop)
            weight = area_ref[:, there] * third
            own = (own_terms[:, at] - weight * smooth_sign(own - corner)).astype(jnp.bfloat16)
            mate = (mate_terms[:, at] - weight * smooth_sign(mate - corner)).astype(jnp.bfloat16)
            grad_ref[:, there] = own
            mate_grad[:, there] = mate
            total = total + (own.astype(jnp.float32) + mate.astype(jnp.float32))
        start += own_ref.shape[1]
        kept.append(kept_ref[...])
        taken += [ref[...] for ref in taken_refs]
    both = jnp.concatenate([grad_ref[...], mate_grad[...]], 1)
    block = jnp.dot(both, jnp.concatenate(kept + taken, 0), preferred_element_type=jnp.float32)
    bias = jnp.sum(total.T, axis=0, keepdims=True)
    bias = jnp.pad(bias, ((0, 0), (0, half - variables)))
    block_ref[:variables] = (block * scale).astype(block_ref.dtype)
    spare = block_ref.shape[0] - variables
    block_ref[variables:] = jnp.broadcast_to(bias * scale, (spare, half)).astype(block_ref.dtype)


def gradient_rows(scale, var_weight, area, parts):
    variables = parts[0][0].shape[0]
    count = area.shape[1]
    half = parts[0][5].shape[1]
    rows = -(-(variables + 1) // 8) * 8
    operands = [value for part in parts for value in part]
    return pl.pallas_call(
        functools.partial(gradient_kernel, scale, len(parts)),
        out_shape=(
            jax.ShapeDtypeStruct((variables, count), jnp.bfloat16),
            jax.ShapeDtypeStruct((rows, half), jnp.bfloat16),
        ),
        in_specs=[VMEM] * (2 + len(operands)),
        out_specs=(VMEM, VMEM),
        scratch_shapes=[pltpu.VMEM((variables, count), jnp.bfloat16)],
        compiler_params=pltpu.CompilerParams(vmem_limit_bytes=8 << 20),
        cost_estimate=pl.CostEstimate(
            flops=4 * count * half * rows, bytes_accessed=4 * count * half, transcendentals=2 * variables * count
        ),
        name="gradient_rows",
    )(var_weight, area, *operands)


def write_half(lanes, block_ref, out_hbm, half_ref, sem):
    half_ref[...] = block_ref[: half_ref.shape[0]].astype(jnp.float32)
    copy = pltpu.make_async_copy(half_ref, out_hbm.at[:, lanes], sem)
    copy.start()
    return copy


def own_half_kernel(role_ref, here_ref, out_hbm, half_ref, sem):
    mine, _ = halves_of(role_ref[0], here_ref.shape[1])
    write_half(mine, here_ref, out_hbm, half_ref, sem).wait()


def other_half_kernel(role_ref, here_ref, there_ref, _, out_hbm, bias_hbm, half_ref, sem, bias_ref, bias_sem):
    role = role_ref[0]
    _, other = halves_of(role, there_ref.shape[1])
    copy = write_half(other, there_ref, out_hbm, half_ref, sem)
    variables = half_ref.shape[0]
    row = slice(variables, variables + 1)
    bias = jnp.where(role == 0, here_ref[row].astype(jnp.float32), there_ref[row].astype(jnp.float32))
    bias_ref[...] = bias[:, :variables]
    bias_copy = pltpu.make_async_copy(bias_ref, bias_hbm, bias_sem)
    bias_copy.start()
    copy.wait()
    bias_copy.wait()


def tail(role, here, there, variables):
    half = here.shape[1]
    whole = jax.ShapeDtypeStruct((variables, 2 * half), jnp.float32)
    scratch = [pltpu.VMEM((variables, half), jnp.float32), pltpu.SemaphoreType.DMA]
    params = pltpu.CompilerParams(vmem_limit_bytes=4 << 20)
    begun = pl.pallas_call(
        own_half_kernel,
        out_shape=whole,
        in_specs=[SMEM, VMEM],
        out_specs=HBM,
        scratch_shapes=scratch,
        compiler_params=params,
        cost_estimate=pl.CostEstimate(flops=0, bytes_accessed=6 * here.size, transcendentals=0),
        name="own_half",
    )(role, here)
    return pl.pallas_call(
        other_half_kernel,
        out_shape=(whole, jax.ShapeDtypeStruct((1, variables), jnp.float32)),
        in_specs=[SMEM, VMEM, VMEM, HBM],
        out_specs=(HBM, HBM),
        scratch_shapes=scratch + [pltpu.VMEM((1, variables), jnp.float32), pltpu.SemaphoreType.DMA],
        input_output_aliases={3: 0},
        compiler_params=params,
        cost_estimate=pl.CostEstimate(flops=0, bytes_accessed=6 * here.size, transcendentals=0),
        name="other_half",
    )(role, here, there, begun)


def four_members(latent, head_weight, head_bias, targets, var_weight, tile_fill):
    _, local_points, _ = latent.shape
    ens = lax.axis_size("ens")
    index = lax.axis_index("space") * ens + lax.axis_index("ens")
    role = role_of(index, groups_of(lax.axis_size("space") * ens)[1]).astype(jnp.int32)[None]
    scale = 1.0 / math.sqrt(4 * local_points * lax.axis_size("space"))
    area = area_of(local_points, tile_fill)
    source = (in_hbm(latent[0]), in_hbm(head_weight.T), in_hbm(head_bias[None]))
    starts = [k * local_points // HALVES for k in range(HALVES)]
    projected = [project_rows(role, *source, start, local_points // HALVES) for start in starts]
    far = [swap(part[0], lambda i: 2) for part in projected]
    projected = lax.optimization_barrier(projected)
    rows = (var_weight[None], area[None])
    parts = []
    for start, (own, kept, *given), across in zip(starts, projected, far):
        mate = swap(own, lambda i: 1)
        taken = [swap(piece, lambda i: 1) for piece in given]
        corner = swap(across, lambda i: 1)
        terms = terms_rows(start, *rows, own, mate, across, targets)
        parts.append((own, mate, corner, *terms, kept, *taken))
    grad, block = gradient_rows(scale, *rows, parts)
    grad_latent = back(grad[None], head_weight)
    block, grad_latent = butterfly(block, grad_latent)
    there = swap(block, lambda i: 1)
    total, bias = tail(role, block, there, targets.shape[0])
    return grad_latent, total.T, bias[0]


def local(latent, head_weight, head_bias, targets, var_weight, tile_fill):
    space, ens = lax.axis_size("space"), lax.axis_size("ens")
    members, _, channels = latent.shape
    fits = members == 1 and ens == 4 and is_pow2(space)
    fits = fits and channels % 256 == 0 and targets.shape[0] <= 128 and latent.shape[1] % (128 * HALVES * PIECES) == 0
    plan = four_members if fits else general
    return plan(latent, head_weight, head_bias, targets, var_weight, tile_fill)


def solution(mesh):
    placed = (P("ens", "space", None), P(), P(), P(None, "space"), P(), P("space"))
    return jax.shard_map(
        local,
        mesh=mesh,
        in_specs=placed,
        out_specs=(P("ens", "space", None), P(), P()),
        check_vma=False,
    )
```
